32 devices in a mesh: dp: 2 (over y), expert: 16 (over z, x, core).
Axes of the slice: x: 2, y: 2, z: 4, core: 2. Of those that a mesh axis runs over, the one named last changes fastest.
Arguments:
- tokens: bfloat16 [32768, 768], P(('dp', 'expert')), may hold values from -6 to 6
- routes: int32 [32768, 1], P(('dp', 'expert')), may hold values from 0 to 15
- cotangent: bfloat16 [32768, 768], P(('dp', 'expert')), may hold values from -6 to 6
- gain_first: bfloat16 [768], replicated, may hold values from 0.5 to 1.5
- w_query: bfloat16 [768, 768], replicated, may hold values from -0.21875 to 0.21875
- w_key: bfloat16 [768, 768], replicated, may hold values from -0.21875 to 0.21875
- w_value: bfloat16 [768, 768], replicated, may hold values from -0.21875 to 0.21875
- w_output: bfloat16 [768, 768], replicated, may hold values from -1.75 to 1.75
- bias_table: bfloat16 [32, 12], replicated, may hold values from -4 to 4
- gain_second: bfloat16 [768], replicated, may hold values from 0.5 to 1.5
- w_router: bfloat16 [768, 16], replicated, may hold values from -0.109375 to 0.109375
- expert_in: bfloat16 [16, 768, 3072], P('expert'), may hold values from -0.21875 to 0.21875
- expert_out: bfloat16 [16, 3072, 768], P('expert'), may hold values from -2.5 to 2.5
Outputs:
- out_tokens: bfloat16 [32768, 768], P(('dp', 'expert'))
- grad_tokens: float32 [32768, 768], P(('dp', 'expert'))
- grad_gain_first: float32 [768], replicated
- grad_query: float32 [768, 768], replicated
- grad_key: float32 [768, 768], replicated
- grad_value: float32 [768, 768], replicated
- grad_output: float32 [768, 768], replicated
- grad_table: float32 [32, 12], replicated
- grad_gain_second: float32 [768], replicated
- grad_router: float32 [768, 16], replicated
- grad_expert_in: float32 [16, 768, 3072], P('expert', None, 'dp')
- grad_expert_out: float32 [16, 3072, 768], P('expert', 'dp')
The draws below stay inside these ranges and needn't reach their ends.
All inputs are finite; a program needn't handle non-finite values.
Results may differ from the reference program's by a relative error of at most 0.015.
Values may be sent and summed in bfloat16 or wider, within the bound.
A program may use at most 320 MiB of HBM per device.

```python
import jax
import jax.numpy as jnp
from jax import lax

D = 768
HEADS = 12
HEAD = 64
FF = 3072
BUCKETS = 32
LEN = 1024
EXPERTS = 16
CAP = 80
TOKENS = 32768


def levels(rng, dims, cuts, low, high):
    gain, own = 1.0, jax.random.fold_in(rng, 6)
    for dim, blocks in cuts:
        heights = jnp.exp(jax.random.uniform(jax.random.fold_in(own, dim), (blocks,), jnp.float32, low / len(cuts), high / len(cuts)))
        gain = gain * jnp.repeat(heights, dims[dim] // blocks).reshape([-1 if axis == dim else 1 for axis in range(len(dims))])
    return gain


def picks_of(own_key, rows, amount, top, lift):
    order = jax.random.permutation(jax.random.fold_in(own_key, 1), amount)
    boost = order
    for power in range(3):
        boost = boost * boost // amount
    boost = boost * lift // amount
    chance = jax.random.randint(jax.random.fold_in(own_key, 2), (rows, amount), 0, 4096) + boost
    holders = jax.random.permutation(jax.random.fold_in(own_key, 3), rows)[jnp.arange(amount) % rows]
    chance = jnp.where(jnp.arange(rows)[:, None] == holders[None, :], 1 << 14, chance)
    score = chance * amount + jnp.arange(amount)
    return lax.top_k(score.astype(jnp.int32), top)[1].astype(jnp.int32)


def centred(rng, dims, spread, limit, shards=(), kind=jnp.bfloat16):
    array = spread * jax.random.normal(rng, dims, jnp.float32)
    if shards:
        array = array * levels(rng, dims, shards, -0.22, 0.18)
    return jnp.clip(array, -limit, limit).astype(kind)


def setup_inputs(seed: int = 0) -> dict:
    seeds = jax.random.split(jax.random.key(seed), 14)
    return {
        "tokens": centred(seeds[0], (TOKENS, D), 1.0, 6.0, ((0, 32),)),
        "routes": picks_of(seeds[1], TOKENS, EXPERTS, 1, 0),
        "cotangent": centred(seeds[2], (TOKENS, D), 1.0, 6.0, ((0, 32),)),
        "gain_first": jnp.clip(1.0 + 0.1 * jax.random.normal(seeds[3], (D,), jnp.float32), 0.5, 1.5).astype(jnp.bfloat16),
        "w_query": centred(seeds[4], (D, D), D ** -0.5, 0.21875),
        "w_key": centred(seeds[5], (D, D), D ** -0.5, 0.21875),
        "w_value": centred(seeds[6], (D, D), D ** -0.5, 0.21875),
        "w_output": centred(seeds[7], (D, D), (D // 64) ** -0.5, 1.75),
        "bias_table": centred(seeds[8], (BUCKETS, HEADS), 1.0, 4.0),
        "gain_second": jnp.clip(1.0 + 0.1 * jax.random.normal(seeds[9], (D,), jnp.float32), 0.5, 1.5).astype(jnp.bfloat16),
        "w_router": centred(seeds[10], (D, EXPERTS), (4 * D) ** -0.5, 0.109375),
        "expert_in": centred(seeds[11], (EXPERTS, D, FF), D ** -0.5, 0.21875, ((0, 16),)),
        "expert_out": centred(seeds[12], (EXPERTS, FF, D), (1.5 * EXPERTS * FF ** -0.5), 2.5, ((0, 16),)),
    }


@jax.custom_vjp
def low(v):
    return lax.optimization_barrier(v.astype(jnp.bfloat16)).astype(jnp.float32)

@jax.custom_vjp
def low_back(v):
    return v

def low_keep(v):
    return (low(v), None)

def low_pass(kept, grad):
    return (grad,)

def back_keep(v):
    return (v, None)

def back_low(kept, grad):
    return (low(grad),)
low.defvjp(low_keep, low_pass)
low_back.defvjp(back_keep, back_low)
eps_norm = 1e-06
thresholds = (12, 16, 23, 32, 46, 64, 91)
highest = lax.Precision.HIGHEST

def relative_buckets(query_pos, key_pos):
    offset = key_pos[None, :] - query_pos[:, None]
    distance = jnp.abs(offset)
    far_bucket = 8 + sum(((distance >= threshold).astype(jnp.int32) for threshold in thresholds))
    near_far = jnp.where(distance < 8, distance, far_bucket)
    return near_far + 16 * (offset > 0).astype(jnp.int32)

def rms_norm(values, gain_vector):
    scale = lax.rsqrt(lax.optimization_barrier(jnp.mean(values * values, axis=-1, keepdims=True)) + eps_norm)
    return values * scale * gain_vector

def attend_sequence(normed_low, w_query, w_key, w_value, bias_table):
    seq_len = normed_low.shape[0]
    queries = low(low_back(jnp.dot(normed_low, w_query, precision=highest))).reshape(seq_len, HEADS, HEAD)
    key_rows = low(low_back(jnp.dot(normed_low, w_key, precision=highest))).reshape(seq_len, HEADS, HEAD)
    value_rows = low(low_back(jnp.dot(normed_low, w_value, precision=highest))).reshape(seq_len, HEADS, HEAD)
    positions = jnp.arange(seq_len, dtype=jnp.int32)
    buckets = relative_buckets(positions, positions)
    onehot = (buckets[:, :, None] == jnp.arange(BUCKETS, dtype=jnp.int32)[None, None, :]).astype(jnp.float32)
    scores = jnp.einsum('qhd,khd->hqk', queries, key_rows, precision=highest) * HEAD ** (-0.5)
    scores = scores + jnp.einsum('qkb,bh->hqk', onehot, bias_table, precision=highest)
    scores = low_back(scores)
    attn_probs = low(jax.nn.softmax(scores, axis=-1))
    attended = jnp.einsum('hqk,khd->qhd', attn_probs, value_rows, precision=highest)
    return low(low_back(attended.reshape(seq_len, HEADS * HEAD)))

def expert_rows(operands):
    slot_rows, w_in, w_out = operands
    hidden_pre = low_back(jnp.dot(slot_rows, w_in, precision=highest))
    activated = low(jax.nn.gelu(hidden_pre, approximate=True))
    return jnp.dot(activated, w_out, precision=highest)

def forward(routes, inputs, gain_first, w_query, w_key, w_value, w_output, bias_table, gain_second, w_router, expert_in, expert_out):
    groups = inputs.shape[0] // LEN
    normed_low = low(rms_norm(inputs, gain_first))

    def one_sequence(seq_rows):
        return attend_sequence(seq_rows, w_query, w_key, w_value, bias_table)
    attended = lax.map(jax.checkpoint(one_sequence), normed_low.reshape(groups, LEN, D))
    branch = low_back(jnp.dot(attended.reshape(groups * LEN, D), w_output, precision=highest))
    after_attn = inputs + branch
    routed_low = low(rms_norm(after_attn, gain_second))
    logits = low_back(jnp.dot(routed_low, w_router, precision=highest))
    router_probs = jax.nn.softmax(logits, axis=-1)
    expert_hot = (routes[:, 0][:, None] == jnp.arange(EXPERTS, dtype=jnp.int32)[None, :]).astype(jnp.int32)
    grouped_hot = expert_hot.reshape(groups, LEN, EXPERTS)
    position = lax.optimization_barrier(jnp.sum(jnp.cumsum(grouped_hot, axis=1) * grouped_hot, axis=2)) - 1
    slot_hot = position[:, :, None] == jnp.arange(CAP, dtype=jnp.int32)[None, None, :]
    dispatch_table = ((grouped_hot[:, :, :, None] > 0) & slot_hot[:, :, None, :]).astype(jnp.float32)
    gate_value = lax.optimization_barrier(jnp.sum(router_probs * expert_hot.astype(jnp.float32), axis=1))
    slot_rows = jnp.einsum('gtec,gtd->egcd', dispatch_table, routed_low.reshape(groups, LEN, D), precision=highest)
    slot_rows = low_back(slot_rows.reshape(EXPERTS, groups * CAP, D))
    produced = lax.map(jax.checkpoint(expert_rows), (slot_rows, expert_in, expert_out))
    returned = low(low_back(produced)).reshape(EXPERTS, groups, CAP, D)
    combined = jnp.einsum('gtec,egcd->gtd', dispatch_table, returned, precision=highest).reshape(groups * LEN, D)
    return after_attn + gate_value[:, None] * combined

def reference(tokens, routes, cotangent, gain_first, w_query, w_key, w_value, w_output, bias_table, gain_second, w_router, expert_in, expert_out):
    floats = tuple((array_value.astype(jnp.float32) for array_value in (tokens, gain_first, w_query, w_key, w_value, w_output, bias_table, gain_second, w_router, expert_in, expert_out)))

    def closed(*params):
        return forward(routes, *params)
    output, pullback = jax.vjp(closed, *floats)
    gradients = pullback(cotangent.astype(jnp.float32))
    return (output.astype(jnp.bfloat16), gradients[0], gradients[1], gradients[2], gradients[3], gradients[4], gradients[5], gradients[6], gradients[7], gradients[8], gradients[9], gradients[10])
```

```python
import functools

import jax
import jax.numpy as jnp
import numpy as np
from jax import lax
from jax.experimental import pallas as pl
from jax.experimental.pallas import tpu as pltpu
from jax.sharding import PartitionSpec as P

NT = (((1,), (1,)), ((), ()))
NN = (((1,), (0,)), ((), ()))
TN = (((0,), (0,)), ((), ()))


def mm(a, b, dims=NN):
    return lax.dot_general(a, b, dims, preferred_element_type=jnp.float32)


MESH = pl.DeviceIdType.MESH
gelu_a, gelu_b = 0.7978845608028654, 0.044715


def enter(axis_size):
    me, dp = lax.axis_index("expert"), lax.axis_index("dp")
    barrier = pltpu.get_barrier_semaphore()
    for step in range(1, axis_size):
        pl.semaphore_signal(barrier, inc=1, device_id=(dp, me ^ step), device_id_type=MESH)
    pl.semaphore_wait(barrier, axis_size - 1)
    return dp, me


def expert_kernel(
    groups, tile,
    xs_ref, gs_ref, cot_ref, win_ref, wout_ref,
    back_ref, gg_ref, ret_ref, gin_own, gin_oth, gout_own, gout_oth,
    x_scr, c_scr, g_scr, w1, w2, a_scr, p_scr, r_scr, b_scr, e_scr, sq_scr, xt_scr, s32, s16,
    x_send, x_recv, g_send, g_recv, b_send, b_recv, e_send, e_recv, loc, wsem, rsem, osem,
):
    f32, bf16 = jnp.float32, jnp.bfloat16
    n, cap, width = xs_ref.shape
    ff = win_ref.shape[1]
    half = ff // 2
    size = n // groups
    rows = size * cap
    dp, me = enter(n)
    weights = [pltpu.make_async_copy(win_ref, w1, wsem.at[0]), pltpu.make_async_copy(wout_ref, w2, wsem.at[1])]
    own = [
        pltpu.make_async_copy(xs_ref.at[me], x_scr.at[0], loc.at[0]),
        pltpu.make_async_copy(gs_ref.at[me], g_scr.at[0], loc.at[1]),
    ]

    def x_copy(o):
        return pltpu.make_async_remote_copy(xs_ref.at[me ^ o], x_scr.at[o], x_send.at[o], x_recv.at[o], device_id=(dp, me ^ o), device_id_type=MESH)

    def g_copy(o):
        return pltpu.make_async_remote_copy(gs_ref.at[me ^ o], g_scr.at[o], g_send.at[o], g_recv.at[o], device_id=(dp, me ^ o), device_id_type=MESH)

    def b_copy(o):
        return pltpu.make_async_remote_copy(b_scr.at[o], back_ref.at[me], b_send.at[o], b_recv.at[o], device_id=(dp, me ^ o), device_id_type=MESH)

    def e_copy(o):
        return pltpu.make_async_remote_copy(e_scr.at[o], gg_ref.at[me], e_send.at[o], e_recv.at[o], device_id=(dp, me ^ o), device_id_type=MESH)

    def c_copy(o):
        return pltpu.make_async_copy(cot_ref.at[me ^ o], c_scr.at[o], rsem.at[o])

    def r_copy(o):
        return pltpu.make_async_copy(r_scr.at[o], ret_ref.at[me ^ o], rsem.at[o])

    def each(lo, hi, fn):
        if hi - lo <= 4:
            for o in range(lo, hi):
                fn(o)
        else:
            lax.fori_loop(lo, hi, lambda o, c: (fn(o), c)[1], 0)

    for c in weights + own:
        c.start()
    each(1, n, lambda o: x_copy(o).start())
    each(0, n, lambda o: c_copy(o).start())
    each(1, n, lambda o: g_copy(o).start())
    sq_scr[...] = jnp.zeros_like(sq_scr)
    for g in range(groups):
        lo, hi = g * size, (g + 1) * size
        if g == 0:
            for c in own + weights:
                c.wait()
        each(lo, hi, lambda o: c_copy(o).wait())
        each(max(lo, 1), hi, lambda o: x_copy(o).wait_recv())
        x = x_scr[lo:hi].reshape(rows, width)
        ct = c_scr[lo:hi].reshape(rows, width)
        for f in range(0, ff, tile):
            u = mm(x, w1[:, f:f + tile])
            back = mm(ct, w2[f:f + tile, :], NT)
            uu = u * u
            t = jnp.tanh(u * (gelu_a + (gelu_a * gelu_b) * uu))
            hp = 0.5 + 0.5 * t
            a_scr[g * rows:(g + 1) * rows, f:f + tile] = (u * hp).astype(bf16)
            slope = hp + (u * hp) * ((1.0 - t) * (gelu_a + (3.0 * gelu_a * gelu_b) * uu))
            p_scr[g * rows:(g + 1) * rows, f:f + tile] = (back * slope).astype(bf16)
        back = mm(p_scr[g * rows:(g + 1) * rows, :], w1[...], NT)
        b_scr[lo:hi] = back.astype(bf16).reshape(size, cap, width)
        each(max(lo, 1), hi, lambda o: b_copy(o).start())
        r = mm(a_scr[g * rows:(g + 1) * rows, :], w2[...])
        r_scr[lo:hi] = r.astype(bf16).reshape(size, cap, width)
        each(lo, hi, lambda o: r_copy(o).start())
        dots = r * ct.astype(f32)
        part = dots[:, :128]
        for j in range(1, width // 128):
            part = part + dots[:, j * 128:(j + 1) * 128]
        part = part.reshape(size, cap, 128)
        for o in range(lo, hi):
            sq_scr[:cap, :] = part[o - lo]
            line = jnp.sum(sq_scr[...].T, axis=0, keepdims=True)
            e_scr[o] = jnp.broadcast_to(line, (8, 128))
        each(max(lo, 1), hi, lambda o: e_copy(o).start())
    own_back = [
        pltpu.make_async_copy(b_scr.at[0], back_ref.at[me], loc.at[0]),
        pltpu.make_async_copy(e_scr.at[0], gg_ref.at[me], loc.at[1]),
    ]
    for c in own_back:
        c.start()
    each(1, n, lambda o: g_copy(o).wait_recv())

    def gated(o):
        col = jnp.broadcast_to(g_scr[o][:1, :], (128, 128)).T[:cap, :1]
        x_scr[o] = (x_scr[o].astype(f32) * col).astype(bf16)
        c_scr[o] = (c_scr[o].astype(f32) * col).astype(bf16)

    each(0, n, gated)
    total = n * cap
    xt_scr[...] = x_scr[...].reshape(total, width).T
    ct = c_scr[...].reshape(total, width)
    count = half // tile
    pend = {}
    step = 0
    for t in range(count):
        for mine in (True, False):
            start = pl.multiple_of((dp if mine else 1 - dp) * half + t * tile, 128)
            stage = s32 if mine else s16
            slot = t % 2
            outs = (gin_own, gout_own) if mine else (gin_oth, gout_oth)
            if (mine, slot) in pend:
                for c in pend[(mine, slot)]:
                    c.wait()
            gin = mm(xt_scr[...], p_scr[:, pl.ds(start, tile)])
            gout = lax.dot_general(a_scr[:, pl.ds(start, tile)], ct, TN, preferred_element_type=f32)
            stage[0][slot] = gin.astype(stage[0].dtype)
            stage[1][slot] = gout.astype(stage[1].dtype)
            k = (0 if mine else 4) + slot * 2
            cs = [
                pltpu.make_async_copy(stage[0].at[slot], outs[0].at[:, t * tile:(t + 1) * tile], osem.at[k]),
                pltpu.make_async_copy(stage[1].at[slot], outs[1].at[t * tile:(t + 1) * tile, :], osem.at[k + 1]),
            ]
            for c in cs:
                c.start()
            pend[(mine, slot)] = cs
    for cs in pend.values():
        for c in cs:
            c.wait()
    for c in own_back:
        c.wait()
    each(0, n, lambda o: r_copy(o).wait())
    each(1, n, lambda o: x_copy(o).wait_send())
    each(1, n, lambda o: g_copy(o).wait_send())
    each(1, n, lambda o: b_copy(o).wait())
    each(1, n, lambda o: e_copy(o).wait())


def expert_pass(xs, gs, cot, w_in, w_out, groups=4):
    f32, bf16 = jnp.float32, jnp.bfloat16
    n, cap, width = xs.shape
    ff = w_in.shape[1]
    half = ff // 2
    tile = 512 if n * cap <= 1280 else 256
    hbm = pl.BlockSpec(memory_space=pl.ANY)
    dma = pltpu.SemaphoreType.DMA
    flat = jax.ShapeDtypeStruct((n, cap, width), bf16)
    return pl.pallas_call(
        functools.partial(expert_kernel, groups, tile),
        in_specs=[hbm] * 5,
        out_specs=[hbm] * 7,
        out_shape=[
            flat, jax.ShapeDtypeStruct((n, 8, 128), f32), flat,
            jax.ShapeDtypeStruct((width, half), f32), jax.ShapeDtypeStruct((width, half), bf16),
            jax.ShapeDtypeStruct((half, width), f32), jax.ShapeDtypeStruct((half, width), bf16),
        ],
        scratch_shapes=[
            pltpu.VMEM((n, cap, width), bf16), pltpu.VMEM((n, cap, width), bf16), pltpu.VMEM((n, 8, 128), f32),
            pltpu.VMEM((width, ff), bf16), pltpu.VMEM((ff, width), bf16),
            pltpu.VMEM((n * cap, ff), bf16), pltpu.VMEM((n * cap, ff), bf16),
            pltpu.VMEM((n, cap, width), bf16), pltpu.VMEM((n, cap, width), bf16), pltpu.VMEM((n, 8, 128), f32),
            pltpu.VMEM((128, 128), f32), pltpu.VMEM((width, n * cap), bf16),
            [pltpu.VMEM((2, width, tile), f32), pltpu.VMEM((2, tile, width), f32)],
            [pltpu.VMEM((2, width, tile), bf16), pltpu.VMEM((2, tile, width), bf16)],
        ] + [dma((n,))] * 8 + [dma((2,)), dma((2,)), dma((n,)), dma((8,))],
        compiler_params=pltpu.CompilerParams(collective_id=1, has_side_effects=True, vmem_limit_bytes=62 << 20),
        name="experts",
    )(xs, gs, cot, w_in, w_out)

def swap_copy(src, dst, send, recv, dp, me, o):
    return pltpu.make_async_remote_copy(src.at[me ^ o], dst.at[me], send.at[o], recv.at[o], device_id=(dp, me ^ o), device_id_type=MESH)


def swap_start(src, dst, send, recv, loc):
    n = src.shape[0]
    dp, me = enter(n)
    pltpu.make_async_copy(src.at[me], dst.at[me], loc.at[0]).start()
    for o in range(1, n):
        swap_copy(src, dst, send, recv, dp, me, o).start()


def swap_wait(src, dst, send, recv, loc):
    n = src.shape[0]
    dp, me = lax.axis_index("dp"), lax.axis_index("expert")
    pltpu.make_async_copy(src.at[me], dst.at[me], loc.at[0]).wait()
    for o in range(1, n):
        swap_copy(src, dst, send, recv, dp, me, o).wait()


def fwd_kernel(rows, g_ref, q_ref, k_ref, v_ref, cs_ref, o_ref, p_ref, cr_ref, b_scr, send, recv, loc):
    seq = q_ref.shape[0]
    blocks = seq // 128
    step = pl.program_id(0)

    @pl.when(step == 0)
    def _():
        swap_start(cs_ref, cr_ref, send, recv, loc)

    lane = lax.broadcasted_iota(jnp.int32, (rows, 128), 1)
    for hh in range(2):
        own = (lane >= 64) if hh else (lane < 64)
        g = g_ref[0, hh:hh + 1, :]
        near = pltpu.roll(jnp.broadcast_to(g, (128, 512)), 384, axis=1, stride=1, stride_axis=0)
        mid = (blocks - 2) * 128
        b_scr[:, :mid] = jnp.broadcast_to(g[:, :1], (128, mid))
        b_scr[:, mid:mid + 384] = near[:, :384]
        b_scr[:, mid + 384:] = jnp.broadcast_to(g[:, 511:], (128, b_scr.shape[1] - mid - 384))
        for i in range(seq // rows):
            r0 = i * rows
            q = q_ref[r0:r0 + rows, :]
            qm = jnp.where(own, q * jnp.bfloat16(0.125), jnp.bfloat16(0))
            s = mm(qm, k_ref[...], NT)
            parts = []
            for a in range(rows // 128):
                c0 = (blocks - 1 - (r0 // 128 + a)) * 128
                parts.append(s[a * 128:(a + 1) * 128] + b_scr[:, c0:c0 + seq])
            s = jnp.concatenate(parts, 0) if len(parts) > 1 else parts[0]
            m = jnp.max(s, axis=-1, keepdims=True)
            e = jnp.exp(s - m)
            inv = 1.0 / jnp.sum(e, axis=-1, keepdims=True)
            p = (e * inv).astype(jnp.bfloat16)
            p_ref[hh, r0:r0 + rows, :] = p
            o = mm(p, v_ref[...]).astype(jnp.bfloat16)
            if hh == 0:
                o_ref[r0:r0 + rows, :] = o
            else:
                o_ref[r0:r0 + rows, :] = jnp.where(own, o, o_ref[r0:r0 + rows, :])

    @pl.when(step == pl.num_programs(0) - 1)
    def _():
        swap_wait(cs_ref, cr_ref, send, recv, loc)


def attn_fwd(gvec, q, k, v, cs, rows=256):
    seq, width = q.shape
    pairs = width // 128
    n = cs.shape[0]
    col = pl.BlockSpec((seq, 128), lambda h: (0, h))
    hbm = pl.BlockSpec(memory_space=pl.ANY)
    dma = pltpu.SemaphoreType.DMA
    return pl.pallas_call(
        functools.partial(fwd_kernel, rows),
        grid=(pairs,),
        in_specs=[pl.BlockSpec((1, 2, 512), lambda h: (h, 0, 0)), col, col, col, hbm],
        out_specs=[col, pl.BlockSpec((2, seq, seq), lambda h: (h, 0, 0)), hbm],
        out_shape=[
            jax.ShapeDtypeStruct((seq, width), jnp.bfloat16),
            jax.ShapeDtypeStruct((2 * pairs, seq, seq), jnp.bfloat16),
            jax.ShapeDtypeStruct(cs.shape, cs.dtype),
        ],
        scratch_shapes=[pltpu.VMEM((128, 2 * seq - 128), jnp.float32), dma((n,)), dma((n,)), dma((1,))],
        compiler_params=pltpu.CompilerParams(
            dimension_semantics=("arbitrary",), collective_id=3, has_side_effects=True, vmem_limit_bytes=48 << 20
        ),
        name="attn_fwd",
    )(gvec, q, k, v, cs)


def bwd_kernel(
    rows, q_ref, k_ref, v_ref, o_ref, d_ref, p_ref, x_ref, a_ref, br_ref, wq_ref, wk_ref, wv_ref, rs_ref,
    near_ref, far_ref, dw_ref, ng_ref, rr_ref,
    ds_scr, qt_scr, dt_scr, near_scr, far_scr, xt_scr, at_scr, dz_scr, send, recv, loc,
):
    seq = q_ref.shape[0]
    blocks = seq // 128
    step = pl.program_id(0)

    @pl.when(step == 0)
    def _():
        swap_start(rs_ref, rr_ref, send, recv, loc)
        xt_scr[...] = x_ref[...].T
        at_scr[...] = a_ref[...].T

    lane = lax.broadcasted_iota(jnp.int32, (rows, 128), 1)
    sub = lax.broadcasted_iota(jnp.int32, (128, seq), 0)
    qt = q_ref[...].T
    dt = d_ref[...].T
    zero = jnp.bfloat16(0)
    for hh in range(2):
        half = (sub >= 64) if hh else (sub < 64)
        qt_scr[:, hh * seq:(hh + 1) * seq] = jnp.where(half, qt, zero)
        dt_scr[:, hh * seq:(hh + 1) * seq] = jnp.where(half, dt, zero)
    for hh in range(2):
        own = (lane >= 64) if hh else (lane < 64)
        near_scr[...] = jnp.zeros_like(near_scr)
        far_scr[...] = jnp.zeros_like(far_scr)
        for i in range(seq // rows):
            r0 = i * rows
            d = jnp.where(own, d_ref[r0:r0 + rows, :], zero)
            dp = mm(d, v_ref[...], NT)
            delta = jnp.sum(d.astype(jnp.float32) * o_ref[r0:r0 + rows, :].astype(jnp.float32), axis=-1, keepdims=True)
            ds = p_ref[hh, r0:r0 + rows, :].astype(jnp.float32) * (dp - delta)
            low = ds.astype(jnp.bfloat16)
            ds_scr[hh * seq + r0:hh * seq + r0 + rows, :] = low
            for a in range(rows // 128):
                bi = r0 // 128 + a
                strip = ds[a * 128:(a + 1) * 128]
                lo, hi = max(bi - 1, 0), min(bi + 2, blocks)
                near_scr[:, (lo - bi + 1) * 128:(hi - bi + 1) * 128] += strip[:, lo * 128:hi * 128]
                if lo > 0:
                    t = strip[:, :128]
                    for j in range(1, lo):
                        t = t + strip[:, j * 128:(j + 1) * 128]
                    far_scr[:, :128] += t
                if hi < blocks:
                    t = strip[:, hi * 128:(hi + 1) * 128]
                    for j in range(hi + 1, blocks):
                        t = t + strip[:, j * 128:(j + 1) * 128]
                    far_scr[:, 128:] += t
            dq = (0.125 * mm(low, k_ref[...])).astype(jnp.bfloat16)
            if hh == 0:
                dz_scr[r0:r0 + rows, :128] = dq
            else:
                dz_scr[r0:r0 + rows, :128] = jnp.where(own, dq, dz_scr[r0:r0 + rows, :128])
        a = near_scr[...]
        n = 128
        while n > 8:
            n //= 2
            a = a[:n] + pltpu.roll(a[n:], 512 - n, axis=1)
        near_ref[0, hh * 8:(hh + 1) * 8, :] = a
        f = far_scr[...]
        n = 128
        while n > 8:
            n //= 2
            f = f[:n] + f[n:]
        far_ref[0, hh * 8:(hh + 1) * 8, :] = f
    dkt = mm(qt_scr[...], ds_scr[...])
    dz_scr[:, 128:256] = (0.125 * dkt).astype(jnp.bfloat16).T
    dvt = mm(dt_scr[...], p_ref[...].reshape(2 * seq, seq))
    dz_scr[:, 256:] = dvt.astype(jnp.bfloat16).T
    dz = dz_scr[...]
    dw = mm(xt_scr[...], dz).astype(jnp.bfloat16)
    for j in range(3):
        dw_ref[0, j] = dw[:, j * 128:(j + 1) * 128]
    dw_ref[0, 3] = mm(at_scr[...], br_ref[...]).astype(jnp.bfloat16)
    w = jnp.concatenate([wq_ref[...], wk_ref[...], wv_ref[...]], axis=1)
    ng = mm(dz, w, NT)

    @pl.when(step == 0)
    def _():
        ng_ref[...] = ng

    @pl.when(step > 0)
    def _():
        ng_ref[...] += ng

    @pl.when(step == pl.num_programs(0) - 1)
    def _():
        swap_wait(rs_ref, rr_ref, send, recv, loc)


def attn_bwd(q, k, v, o, d, p, x, branch, wq, wk, wv, rs, rows=256):
    f32, bf16 = jnp.float32, jnp.bfloat16
    seq, width = q.shape
    pairs = width // 128
    n = rs.shape[0]
    col = pl.BlockSpec((seq, 128), lambda h: (0, h))
    wcol = pl.BlockSpec((width, 128), lambda h: (0, h))
    full = pl.BlockSpec((seq, width), lambda h: (0, 0))
    hbm = pl.BlockSpec(memory_space=pl.ANY)
    dma = pltpu.SemaphoreType.DMA
    return pl.pallas_call(
        functools.partial(bwd_kernel, rows),
        grid=(pairs,),
        in_specs=[col] * 5 + [pl.BlockSpec((2, seq, seq), lambda h: (h, 0, 0)), full, full, col] + [wcol] * 3 + [hbm],
        out_specs=[
            pl.BlockSpec((1, 16, 512), lambda h: (h, 0, 0)),
            pl.BlockSpec((1, 16, 256), lambda h: (h, 0, 0)),
            pl.BlockSpec((1, 4, width, 128), lambda h: (h, 0, 0, 0)),
            full,
            hbm,
        ],
        out_shape=[
            jax.ShapeDtypeStruct((pairs, 16, 512), f32),
            jax.ShapeDtypeStruct((pairs, 16, 256), f32),
            jax.ShapeDtypeStruct((pairs, 4, width, 128), bf16),
            jax.ShapeDtypeStruct((seq, width), f32),
            jax.ShapeDtypeStruct(rs.shape, rs.dtype),
        ],
        scratch_shapes=[
            pltpu.VMEM((2 * seq, seq), bf16), pltpu.VMEM((128, 2 * seq), bf16), pltpu.VMEM((128, 2 * seq), bf16),
            pltpu.VMEM((128, 512), f32), pltpu.VMEM((128, 256), f32),
            pltpu.VMEM((width, seq), bf16), pltpu.VMEM((width, seq), bf16), pltpu.VMEM((seq, 384), bf16),
            dma((n,)), dma((n,)), dma((1,)),
        ],
        compiler_params=pltpu.CompilerParams(
            dimension_semantics=("arbitrary",), collective_id=4, has_side_effects=True, vmem_limit_bytes=56 << 20
        ),
        name="attn_bwd",
    )(q, k, v, o, d, p, x, o, branch, wq, wk, wv, rs)

def reduce_kernel(main_ref, small_ref, out_q, out_k, out_v, out_o, small_out, acc, rbuf, obuf, s_acc, s_rbuf, s_obuf, send, recv, s_send, s_recv):
    f32, bf16 = jnp.float32, jnp.bfloat16
    chunks, total, rows, _ = main_ref.shape
    n = total // 2
    me, dp = lax.axis_index("expert"), lax.axis_index("dp")
    bits = n.bit_length() - 1
    peers = [((dp, me ^ (1 << b)), (me >> b) & 1) for b in range(bits)] + [((1 - dp, me), dp)]
    barrier = pltpu.get_barrier_semaphore()
    for dev, _ in peers:
        pl.semaphore_signal(barrier, inc=1, device_id=dev, device_id_type=MESH)
    pl.semaphore_wait(barrier, len(peers))
    stages = bits + 1
    base = list(range(stages))
    orders = [base, [0] + base[2:bits] + [1, bits], [0, bits] + base[1:bits]]
    lanes = [(c, main_ref.at[c], acc.at[c], rbuf.at[c], obuf.at[c], send.at[c], recv.at[c], orders[c % 3], bf16) for c in range(chunks)]
    lanes.append((chunks, small_ref, s_acc, s_rbuf, s_obuf, s_send, s_recv, orders[2], f32))
    spans = {c: [] for c in range(chunks + 1)}
    start = {c: 0 for c in range(chunks + 1)}

    def halve(lane, s):
        c, source, mine, inbox, _, ss, rs, order, _ = lane
        dev, own = peers[order[s]]
        size = total >> (s + 1)
        keep = start[c] + own * size
        give = start[c] + (1 - own) * size
        spans[c].append(keep)
        start[c] = keep
        now = source if s == 0 else mine
        off = total - 2 * size
        return pltpu.make_async_remote_copy(now.at[pl.ds(give, size)], inbox.at[pl.ds(off, size)], ss.at[s], rs.at[s], device_id=dev, device_id_type=MESH)

    def fold(lane, s):
        c, source, mine, inbox, outbox, _, _, _, kind = lane
        size = total >> (s + 1)
        now = source if s == 0 else mine
        off = total - 2 * size
        keep = spans[c][s]
        goal = outbox if s == stages - 1 else mine

        def one(j, _):
            goal[keep + j] = (now[keep + j].astype(f32) + inbox[off + j].astype(f32)).astype(kind)
            return 0

        lax.fori_loop(0, size, one, 0)

    def double(lane, s):
        c, _, _, _, outbox, ss, rs, order, _ = lane
        dev, _ = peers[order[s]]
        size = total >> (s + 1)
        piece = outbox.at[pl.ds(spans[c][s], size)]
        k = 2 * stages - 1 - s
        return pltpu.make_async_remote_copy(piece, piece, ss.at[k], rs.at[k], device_id=dev, device_id_type=MESH)

    live = {}
    for s in range(stages):
        for lane in lanes:
            if s:
                live[lane[0]].wait()
                fold(lane, s - 1)
            live[lane[0]] = halve(lane, s)
            live[lane[0]].start()
    for s in reversed(range(stages)):
        for lane in lanes:
            live[lane[0]].wait()
            if s == stages - 1:
                fold(lane, s)
            live[lane[0]] = double(lane, s)
            live[lane[0]].start()
    outs = (out_q, out_k, out_v, out_o)
    depth, width = out_q.shape
    per = depth // rows
    tiles = 4 * (width // 128)
    for c in range(chunks):
        live[c].wait()
        share = tiles // chunks
        for j in range(share):
            t = c * share + j
            out = outs[t % 4]
            out[:, (t // 4) * 128:(t // 4 + 1) * 128] = obuf[c, j * per:(j + 1) * per].reshape(depth, 128).astype(f32)
    live[chunks].wait()
    small_out[...] = s_obuf[...]


def reduce_all(main, small, width):
    f32, bf16 = jnp.float32, jnp.bfloat16
    chunks, total, rows, _ = main.shape
    stages = total.bit_length() - 1
    vm = pl.BlockSpec(memory_space=pltpu.VMEM)
    dma = pltpu.SemaphoreType.DMA
    square = jax.ShapeDtypeStruct((width, width), f32)
    buf, sbuf = pltpu.VMEM(main.shape, bf16), pltpu.VMEM(small.shape, f32)
    return pl.pallas_call(
        reduce_kernel,
        in_specs=[vm, vm],
        out_specs=[vm] * 5,
        out_shape=[square] * 4 + [jax.ShapeDtypeStruct(small.shape, f32)],
        scratch_shapes=[buf, buf, buf, sbuf, sbuf, sbuf, dma((chunks, 2 * stages)), dma((chunks, 2 * stages)), dma((2 * stages,)), dma((2 * stages,))],
        compiler_params=pltpu.CompilerParams(collective_id=2, has_side_effects=True, vmem_limit_bytes=40 << 20),
        name="reduce_all",
    )(main, small)

eps_norm = 1e-06
thresholds = (12, 16, 23, 32, 46, 64, 91)


def bucket_of(offset):
    distance = np.abs(offset)
    far = 8 + sum((distance >= t).astype(np.int32) for t in thresholds)
    return np.where(distance < 8, distance, far) + 16 * (offset > 0)


def hot_of(offset):
    return (bucket_of(offset)[..., None] == np.arange(32)).astype(np.float32)


def local(dp_count, tokens, routes, cotangent, gain_first, w_query, w_key, w_value, w_output, bias_table, gain_second, w_router, expert_in, expert_out):
    f32, bf16 = jnp.float32, jnp.bfloat16
    seq, width = tokens.shape
    heads = bias_table.shape[1]
    experts = w_router.shape[1]
    cap = (5 * seq + 4 * experts - 1) // (4 * experts)
    capp = (cap + 15) // 16 * 16
    slots = experts * capp
    ids = routes[:, 0]
    hot = (ids[:, None] == jnp.arange(experts, dtype=jnp.int32)[None, :]).astype(bf16)
    order = jnp.arange(seq, dtype=jnp.int32)
    before = (order[:, None] > order[None, :]).astype(bf16)
    hot32 = hot.astype(f32)
    position = jnp.sum(mm(before, hot) * hot32, axis=1).astype(jnp.int32)
    slot = jnp.where(position < cap, ids * capp + position, -1)
    table = (slot[:, None] == jnp.arange(slots, dtype=jnp.int32)[None, :]).astype(bf16)

    def pick(values):
        return jnp.sum(table.astype(f32) * values[:, None], axis=0)

    cot_slots = mm(table, cotangent, TN).astype(bf16).reshape(experts, capp, width)

    inputs = tokens.astype(f32)
    g1 = gain_first.astype(f32)
    s1 = lax.rsqrt(jnp.mean(inputs * inputs, axis=-1, keepdims=True) + eps_norm)
    normed_low = (inputs * s1 * g1).astype(bf16)
    q = mm(normed_low, w_query).astype(bf16)
    k = mm(normed_low, w_key).astype(bf16)
    v = mm(normed_low, w_value).astype(bf16)
    near_hot = jnp.asarray(hot_of(np.arange(512) - 256), f32)
    gvec = jnp.einsum("ub,bh->hu", near_hot, bias_table.astype(f32), precision=lax.Precision.HIGHEST)
    attended, probs_low, cot_rows = attn_fwd(gvec.reshape(heads // 2, 2, 512), q, k, v, cot_slots)
    after_attn = inputs + mm(attended, w_output)
    g2 = gain_second.astype(f32)
    s2 = lax.rsqrt(jnp.mean(after_attn * after_attn, axis=-1, keepdims=True) + eps_norm)
    routed_low = (after_attn * s2 * g2).astype(bf16)
    rows = mm(table, routed_low, TN).astype(bf16).reshape(experts, capp, width)
    router_probs = jax.nn.softmax(mm(routed_low, w_router), axis=-1)
    gate = jnp.sum(router_probs * hot32, axis=1)
    gates = jnp.broadcast_to(jnp.pad(pick(gate).reshape(experts, 1, capp), ((0, 0), (0, 0), (0, 128 - capp))), (experts, 8, 128))
    back_tokens, gate_grads, produced, gin_own, gin_oth, gout_own, gout_oth = expert_pass(
        rows, gates, cot_rows, expert_in[0], expert_out[0]
    )
    back_tokens = back_tokens.reshape(slots, width)
    gate_grad_back = gate_grads[:, 0, :capp].reshape(slots)
    around = [(0, 1), (1, 0)]
    gin_oth = lax.ppermute(gin_oth, "dp", around)
    gout_oth = lax.ppermute(gout_oth, "dp", around)

    upstream = cotangent.astype(f32)
    gate_grad = jnp.sum(table.astype(f32) * gate_grad_back[None, :], axis=1)
    logit_grad_low = ((gate_grad * gate)[:, None] * (hot32 - router_probs)).astype(bf16)
    routed_grad = gate[:, None] * mm(table, back_tokens) + mm(logit_grad_low, w_router, NT)
    gdy = g2 * routed_grad
    after_grad = upstream + s2 * gdy - after_attn * (s2 * s2 * s2 * jnp.mean(gdy * after_attn, axis=-1, keepdims=True))
    gain_two = jnp.sum(routed_grad * after_attn * s2, axis=0)
    branch_low = after_grad.astype(bf16)
    attended_grad = mm(branch_low, w_output, NT).astype(bf16)
    grad_router = mm(routed_low, logit_grad_low, TN)
    near, far, dw, normed_grad, returned = attn_bwd(
        q, k, v, attended, attended_grad, probs_low, normed_low, branch_low, w_query, w_key, w_value, produced
    )
    near_index = hot_of((np.arange(512)[None, :] + 128) % 512 - 256 - np.arange(8)[:, None]).reshape(4096, 32)
    far = far.reshape(heads, 8, 2, 128).sum((1, 3))
    table_grad = jnp.einsum("hk,kb->bh", near.reshape(heads, 4096), jnp.asarray(near_index), precision=lax.Precision.HIGHEST)
    table_grad = table_grad.at[15].add(far[:, 0]).at[31].add(far[:, 1])

    gdy = g1 * normed_grad
    input_grad = after_grad + s1 * gdy - inputs * (s1 * s1 * s1 * jnp.mean(gdy * inputs, axis=-1, keepdims=True))
    gain_one = jnp.sum(normed_grad * inputs * s1, axis=0)
    devices = dp_count * experts
    small = [gain_one, gain_two, table_grad.reshape(-1), grad_router.reshape(-1)]
    marks = np.cumsum([0] + [part.size for part in small])
    small = jnp.pad(jnp.concatenate(small), (0, devices * 1024 - int(marks[-1])))
    chunks = 3
    main = dw.reshape(chunks, devices, 4 * width * width // (128 * devices * chunks), 128)
    grad_query, grad_key, grad_value, grad_output, small = reduce_all(main, small.reshape(devices, 8, 128), width)
    small = small.reshape(-1)
    gain_one, gain_two, table_grad, grad_router = (small[marks[i]:marks[i + 1]] for i in range(4))
    combined = mm(table, returned.reshape(slots, width))
    output = (after_attn + gate[:, None] * combined).astype(bf16)
    gin_oth, gout_oth, _ = lax.optimization_barrier((gin_oth, gout_oth, gain_one))
    grad_in = (gin_own + gin_oth.astype(f32))[None]
    grad_out = (gout_own + gout_oth.astype(f32))[None]
    return (
        output,
        input_grad,
        gain_one,
        grad_query,
        grad_key,
        grad_value,
        grad_output,
        table_grad.reshape(bias_table.shape),
        gain_two,
        grad_router.reshape(w_router.shape),
        grad_in,
        grad_out,
    )


def solution(mesh):
    split, whole = P(("dp", "expert"), None), P()
    in_specs = (split, split, split, whole, whole, whole, whole, whole, whole, whole, whole, P("expert", None, None), P("expert", None, None))
    out_specs = (split, split) + (whole,) * 8 + (P("expert", None, "dp"), P("expert", "dp", None))
    return jax.shard_map(
        functools.partial(local, mesh.shape["dp"]), mesh=mesh, in_specs=in_specs, out_specs=out_specs, check_vma=False
    )
```

```python
import functools

import jax
import jax.numpy as jnp
import numpy as np
from jax import lax
from jax.experimental import pallas as pl
from jax.experimental.pallas import tpu as pltpu
from jax.sharding import PartitionSpec as P

NT = (((1,), (1,)), ((), ()))
NN = (((1,), (0,)), ((), ()))
TN = (((0,), (0,)), ((), ()))


def mm(a, b, dims=NN):
    return lax.dot_general(a, b, dims, preferred_element_type=jnp.float32)


MESH = pl.DeviceIdType.MESH
gelu_a, gelu_b = 0.7978845608, 0.044715


def enter(axis_size, across=False):
    me, dp = lax.axis_index("expert"), lax.axis_index("dp")
    barrier = pltpu.get_barrier_semaphore()
    for step in range(1, axis_size):
        pl.semaphore_signal(barrier, inc=1, device_id=(dp, me ^ step), device_id_type=MESH)
    if across:
        pl.semaphore_signal(barrier, inc=1, device_id=(1 - dp, me), device_id_type=MESH)
    pl.semaphore_wait(barrier, axis_size if across else axis_size - 1)
    return dp, me


def expert_kernel(
    groups, tile, early,
    xs_ref, gs_ref, cot_ref, far_ref, win_ref, wout_ref,
    back_ref, gg_ref, ret_ref, gin_ref, gout_ref,
    x_scr, c_scr, g_scr, w1, w2, a_scr, p_scr, ag_scr, pg_scr, r_scr, b_scr, e_scr, sq_scr, gin, gout,
    x_send, x_recv, g_send, g_recv, b_send, b_recv, e_send, e_recv, loc, wsem, csem, rsem, osem, f_send, f_recv,
):
    f32, bf16 = jnp.float32, jnp.bfloat16
    n, cap, width = xs_ref.shape
    ff = win_ref.shape[1]
    half = ff // 2
    size = n // groups
    rows = size * cap
    dp, me = enter(n, True)
    mine = pl.multiple_of(dp * half, 128)
    rest = pl.multiple_of((1 - dp) * half, 128)
    weights = [
        pltpu.make_async_copy(win_ref.at[:, pl.ds(mine, half)], w1.at[:, :half], wsem.at[0]),
        pltpu.make_async_copy(win_ref.at[:, pl.ds(rest, half)], w1.at[:, half:], wsem.at[1]),
        pltpu.make_async_copy(wout_ref.at[pl.ds(mine, half), :], w2.at[:half, :], wsem.at[2]),
        pltpu.make_async_copy(wout_ref.at[pl.ds(rest, half), :], w2.at[half:, :], wsem.at[3]),
    ]
    own = [
        pltpu.make_async_copy(xs_ref.at[me], x_scr.at[0, 0], loc.at[0]),
        pltpu.make_async_copy(gs_ref.at[me], g_scr.at[0, 0], loc.at[1]),
    ]
    cots = [
        pltpu.make_async_copy(cot_ref, c_scr.at[0], csem.at[0]),
        pltpu.make_async_copy(far_ref.at[:early], c_scr.at[1, :early], csem.at[1]),
    ]

    def remote(src, dst, send, recv, dev):
        return pltpu.make_async_remote_copy(src, dst, send, recv, device_id=dev, device_id_type=MESH)

    def x_copy(o):
        return remote(xs_ref.at[me ^ o], x_scr.at[0, o], x_send.at[o], x_recv.at[o], (dp, me ^ o))

    def g_copy(o):
        return remote(gs_ref.at[me ^ o], g_scr.at[0, o], g_send.at[o], g_recv.at[o], (dp, me ^ o))

    def b_copy(o):
        return remote(b_scr.at[o], back_ref.at[me], b_send.at[o], b_recv.at[o], (dp, me ^ o))

    def e_copy(o):
        return remote(e_scr.at[o], gg_ref.at[me], e_send.at[o], e_recv.at[o], (dp, me ^ o))

    def r_copy(o):
        return pltpu.make_async_copy(r_scr.at[o], ret_ref.at[o], rsem.at[o])

    over = (1 - dp, me)
    c_over = remote(cot_ref.at[early:], c_scr.at[1, early:], f_send.at[groups], f_recv.at[groups], over)
    g_over = remote(g_scr.at[0], g_scr.at[1], f_send.at[groups + 1], f_recv.at[groups + 1], over)

    def x_over(g):
        span = slice(g * size, (g + 1) * size)
        return remote(x_scr.at[0, span], x_scr.at[1, span], f_send.at[g], f_recv.at[g], over)

    def each(lo, hi, fn):
        if hi - lo <= 4:
            for o in range(lo, hi):
                fn(o)
        else:
            lax.fori_loop(lo, hi, lambda o, c: (fn(o), c)[1], 0)

    for c in own:
        c.start()
    each(1, n, lambda o: g_copy(o).start())
    each(1, n, lambda o: x_copy(o).start())
    c_over.start()
    for c in cots + weights:
        c.start()
    sq_scr[...] = jnp.zeros_like(sq_scr)

    def gated(side, lo, hi):
        def one(o):
            col = jnp.broadcast_to(g_scr[side, o][:1, :], (128, 128)).T[:cap, :1]
            c_scr[side, o] = (c_scr[side, o].astype(f32) * col).astype(bf16)

        each(lo, hi, one)

    def hidden(x, ct, f):
        u = mm(x, w1[:, f:f + tile])
        back = mm(ct, w2[f:f + tile, :], NT)
        uu = u * u
        t = jnp.tanh(u * (gelu_a + (gelu_a * gelu_b) * uu))
        hp = 0.5 + 0.5 * t
        act = u * hp
        slope = hp + act * ((1.0 - t) * (gelu_a + (3.0 * gelu_a * gelu_b) * uu))
        return act.astype(bf16), (back * slope).astype(bf16)

    for g in range(groups):
        lo, hi = g * size, (g + 1) * size
        if g == 0:
            for c in own + cots[:1]:
                c.wait()
        each(max(lo, 1), hi, lambda o: g_copy(o).wait_recv())
        raw = c_scr[0, lo:hi].reshape(rows, width)
        gated(0, lo, hi)
        each(max(lo, 1), hi, lambda o: x_copy(o).wait_recv())
        x_over(g).start()
        if g == 0:
            for c in weights:
                c.wait()
        x = x_scr[0, lo:hi].reshape(rows, width)
        ct = c_scr[0, lo:hi].reshape(rows, width)
        span = slice(g * rows, (g + 1) * rows)
        for f in range(0, ff, tile):
            act, pre = hidden(x, ct, f)
            if f < half:
                a_scr[span, f:f + tile] = act
                p_scr[span, f:f + tile] = pre
            else:
                ag_scr[:, f - half:f - half + tile] = act
                pg_scr[:, f - half:f - half + tile] = pre
        back = mm(p_scr[span, :], w1[:, :half], NT) + mm(pg_scr[...], w1[:, half:], NT)
        b_scr[lo:hi] = back.astype(bf16).reshape(size, cap, width)
        each(max(lo, 1), hi, lambda o: b_copy(o).start())
        r = mm(a_scr[span, :], w2[:half, :]) + mm(ag_scr[...], w2[half:, :])
        r_scr[lo:hi] = r.astype(bf16).reshape(size, cap, width)
        dots = r * raw.astype(f32)
        part = dots[:, :128]
        for j in range(1, width // 128):
            part = part + dots[:, j * 128:(j + 1) * 128]
        part = part.reshape(size, cap, 128)
        for o in range(lo, hi):
            sq_scr[:cap, :] = part[o - lo]
            line = jnp.sum(sq_scr[...].T, axis=0, keepdims=True)
            e_scr[o] = jnp.broadcast_to(line, (8, 128))
        each(max(lo, 1), hi, lambda o: e_copy(o).start())
    g_over.start()
    each(0, n, lambda o: r_copy(o).start())
    own_back = [
        pltpu.make_async_copy(b_scr.at[0], back_ref.at[me], loc.at[0]),
        pltpu.make_async_copy(e_scr.at[0], gg_ref.at[me], loc.at[1]),
    ]
    for c in own_back:
        c.start()
    total = n * cap

    def gradients(side, first):
        x = x_scr[side].reshape(total, width)
        ct = c_scr[side].reshape(total, width)
        for f in range(0, half, tile):
            part = lax.dot_general(x, p_scr[:, f:f + tile], TN, preferred_element_type=f32)
            if first:
                gin[:, f:f + tile] = part
            else:
                w1[:, f:f + tile] = (gin[:, f:f + tile] + part).astype(bf16)
            part = lax.dot_general(a_scr[:, f:f + tile], ct, TN, preferred_element_type=f32)
            if first:
                gout[f:f + tile, :] = part
            else:
                w2[f:f + tile, :] = (gout[f:f + tile, :] + part).astype(bf16)
                for c in outs(f):
                    c.start()

    def outs(f):
        i = f // tile
        return [
            pltpu.make_async_copy(w1.at[:, f:f + tile], gin_ref.at[:, f:f + tile], osem.at[2 * i]),
            pltpu.make_async_copy(w2.at[f:f + tile, :], gout_ref.at[f:f + tile, :], osem.at[2 * i + 1]),
        ]

    gradients(0, True)
    cots[1].wait()
    c_over.wait()
    g_over.wait()
    gated(1, 0, n)
    for g in range(groups):
        lo, hi = g * size, (g + 1) * size
        x_over(g).wait()
        x = x_scr[1, lo:hi].reshape(rows, width)
        ct = c_scr[1, lo:hi].reshape(rows, width)
        for f in range(0, half, tile):
            act, pre = hidden(x, ct, f)
            a_scr[g * rows:(g + 1) * rows, f:f + tile] = act
            p_scr[g * rows:(g + 1) * rows, f:f + tile] = pre
    gradients(1, False)
    for f in range(0, half, tile):
        for c in outs(f):
            c.wait()
    for c in own_back:
        c.wait()
    each(0, n, lambda o: r_copy(o).wait())
    each(1, n, lambda o: x_copy(o).wait_send())
    each(1, n, lambda o: g_copy(o).wait_send())
    each(1, n, lambda o: b_copy(o).wait())
    each(1, n, lambda o: e_copy(o).wait())


def expert_pass(xs, gs, cot, far, w_in, w_out):
    f32, bf16 = jnp.float32, jnp.bfloat16
    n, cap, width = xs.shape
    ff = w_in.shape[1]
    half = ff // 2
    groups, tile = (4, 512) if n * cap <= 1280 else (8, 256)
    rows = n // groups * cap
    hbm = pl.BlockSpec(memory_space=pl.ANY)
    dma = pltpu.SemaphoreType.DMA
    flat = jax.ShapeDtypeStruct((n, cap, width), bf16)
    return pl.pallas_call(
        functools.partial(expert_kernel, groups, tile, n // 2),
        in_specs=[hbm] * 6,
        out_specs=[hbm] * 5,
        out_shape=[
            flat, jax.ShapeDtypeStruct((n, 8, 128), f32), flat,
            jax.ShapeDtypeStruct((width, half), bf16), jax.ShapeDtypeStruct((half, width), bf16),
        ],
        scratch_shapes=[
            pltpu.VMEM((2, n, cap, width), bf16), pltpu.VMEM((2, n, cap, width), bf16), pltpu.VMEM((2, n, 8, 128), f32),
            pltpu.VMEM((width, ff), bf16), pltpu.VMEM((ff, width), bf16),
            pltpu.VMEM((n * cap, half), bf16), pltpu.VMEM((n * cap, half), bf16),
            pltpu.VMEM((rows, half), bf16), pltpu.VMEM((rows, half), bf16),
            pltpu.VMEM((n, cap, width), bf16), pltpu.VMEM((n, cap, width), bf16), pltpu.VMEM((n, 8, 128), f32),
            pltpu.VMEM((128, 128), f32), pltpu.VMEM((width, half), f32), pltpu.VMEM((half, width), f32),
        ] + [dma((n,))] * 8 + [dma((2,)), dma((4,)), dma((2,)), dma((n,)), dma((2 * half // tile,)), dma((groups + 2,)), dma((groups + 2,))],
        compiler_params=pltpu.CompilerParams(collective_id=1, has_side_effects=True, vmem_limit_bytes=62 << 20),
        name="experts",
    )(xs, gs, cot, far, w_in, w_out)

def fwd_kernel(rows, g_ref, q_ref, k_ref, v_ref, cs_ref, o_ref, p_ref, cr_ref, cp_ref, b_scr, send, recv, loc, f_send, f_recv):
    seq = q_ref.shape[0]
    blocks = seq // 128
    step = pl.program_id(0)

    n = cs_ref.shape[0]
    me, dp = lax.axis_index("expert"), lax.axis_index("dp")
    quarter = n // 4

    def c_copy(o):
        return pltpu.make_async_remote_copy(
            cs_ref.at[me ^ o], cr_ref.at[o], send.at[o], recv.at[o], device_id=(dp, me ^ o), device_id_type=MESH
        )

    def over(i):
        span = pl.ds(i * quarter, quarter)
        return pltpu.make_async_remote_copy(
            cr_ref.at[span], cp_ref.at[span], f_send.at[i], f_recv.at[i], device_id=(1 - dp, me), device_id_type=MESH
        )

    home = pltpu.make_async_copy(cs_ref.at[me], cr_ref.at[0], loc.at[0])

    @pl.when(step == 0)
    def _():
        enter(n, True)
        home.start()
        for o in range(1, n):
            c_copy(o).start()

    for i in range(2):

        @pl.when(step == 2 + 2 * i)
        def _():
            if i == 0:
                home.wait()
            for o in range(max(1, i * quarter), (i + 1) * quarter):
                c_copy(o).wait_recv()
            over(i).start()

    lane = lax.broadcasted_iota(jnp.int32, (rows, 128), 1)
    for hh in range(2):
        own = (lane >= 64) if hh else (lane < 64)
        g = g_ref[0, hh:hh + 1, :]
        near = pltpu.roll(jnp.broadcast_to(g, (128, 512)), 384, axis=1, stride=1, stride_axis=0)
        mid = (blocks - 2) * 128
        b_scr[:, :mid] = jnp.broadcast_to(g[:, :1], (128, mid))
        b_scr[:, mid:mid + 384] = near[:, :384]
        b_scr[:, mid + 384:] = jnp.broadcast_to(g[:, 511:], (128, b_scr.shape[1] - mid - 384))
        for i in range(seq // rows):
            r0 = i * rows
            q = q_ref[r0:r0 + rows, :]
            qm = jnp.where(own, q * jnp.bfloat16(0.125), jnp.bfloat16(0))
            s = mm(qm, k_ref[...], NT)
            parts = []
            for a in range(rows // 128):
                c0 = (blocks - 1 - (r0 // 128 + a)) * 128
                parts.append(s[a * 128:(a + 1) * 128] + b_scr[:, c0:c0 + seq])
            s = jnp.concatenate(parts, 0) if len(parts) > 1 else parts[0]
            m = jnp.max(s, axis=-1, keepdims=True)
            e = jnp.exp(s - m)
            inv = 1.0 / jnp.sum(e, axis=-1, keepdims=True)
            p = (e * inv).astype(jnp.bfloat16)
            p_ref[hh, r0:r0 + rows, :] = p
            o = mm(p, v_ref[...]).astype(jnp.bfloat16)
            if hh == 0:
                o_ref[r0:r0 + rows, :] = o
            else:
                o_ref[r0:r0 + rows, :] = jnp.where(own, o, o_ref[r0:r0 + rows, :])

    @pl.when(step == pl.num_programs(0) - 1)
    def _():
        for o in range(1, n):
            c_copy(o).wait_send()
        for o in range(n // 2, n):
            c_copy(o).wait_recv()
        for i in range(2):
            over(i).wait()


def attn_fwd(gvec, q, k, v, cs, rows=256):
    seq, width = q.shape
    pairs = width // 128
    n = cs.shape[0]
    col = pl.BlockSpec((seq, 128), lambda h: (0, h))
    hbm = pl.BlockSpec(memory_space=pl.ANY)
    dma = pltpu.SemaphoreType.DMA
    return pl.pallas_call(
        functools.partial(fwd_kernel, rows),
        grid=(pairs,),
        in_specs=[pl.BlockSpec((1, 2, 512), lambda h: (h, 0, 0)), col, col, col, hbm],
        out_specs=[col, pl.BlockSpec((2, seq, seq), lambda h: (h, 0, 0)), hbm, hbm],
        out_shape=[
            jax.ShapeDtypeStruct((seq, width), jnp.bfloat16),
            jax.ShapeDtypeStruct((2 * pairs, seq, seq), jnp.bfloat16),
            jax.ShapeDtypeStruct(cs.shape, cs.dtype),
            jax.ShapeDtypeStruct((n // 2, *cs.shape[1:]), cs.dtype),
        ],
        scratch_shapes=[pltpu.VMEM((128, 2 * seq - 128), jnp.float32), dma((n,)), dma((n,)), dma((1,)), dma((2,)), dma((2,))],
        compiler_params=pltpu.CompilerParams(
            dimension_semantics=("arbitrary",), collective_id=3, has_side_effects=True, vmem_limit_bytes=48 << 20
        ),
        name="attn_fwd",
    )(gvec, q, k, v, cs)


def bwd_kernel(
    rows, merge, q_ref, k_ref, v_ref, o_ref, p_ref, wq_ref, wk_ref, wv_ref,
    tok_ref, cot_ref, after_ref, stat_ref, probs_ref, g1_ref, g2_ref, wr_ref, wo_ref, back_ref, gg_ref, rs_ref,
    ig_ref, small_out, sum_ref, rr_ref,
    ds_scr, qt_scr, dt_scr, near_scr, far_scr, xt_scr, d_scr, br_scr, dz_scr, nf_scr, ng_scr, rt_scr, gc_scr,
    acc, inbox, done, s_acc, s_inbox, s_done, send, recv, loc, r_send, r_recv, s_send, s_recv, out_sem,
):
    seq = q_ref.shape[0]
    blocks = seq // 128
    step = pl.program_id(0)
    width = tok_ref.shape[1]
    pairs = width // 128
    f32, bf16 = jnp.float32, jnp.bfloat16
    chunks, total, depth, _ = acc.shape
    n = total // 2
    me, dp = lax.axis_index("expert"), lax.axis_index("dp")
    rounds = rounds_of(n)
    count = len(rounds)

    def place(bits):
        rank, devices = 0, []
        for i, bit in enumerate(bits):
            rank = rank + (dp if bit < 0 else (me >> bit) & 1) * (1 << i)
        for mask in range(1, 1 << len(bits)):
            flip = sum(1 << bit for i, bit in enumerate(bits) if bit >= 0 and mask >> i & 1)
            across = any(bit < 0 and mask >> i & 1 for i, bit in enumerate(bits))
            devices.append((1 - dp if across else dp, me ^ flip))
        return rank, devices

    ranks, spans, at, base, size, lead = [place(bits) for bits in rounds], [], 0, 0, total, 0
    for r, bits in enumerate(rounds):
        size //= 1 << len(bits)
        spans.append((at, at + ranks[r][0] * size, size, base, lead))
        at, base, lead = at + ranks[r][0] * size, base + ((1 << len(bits)) - 1) * size, lead + (1 << len(bits)) - 1
    links = lead

    def spread(lane, r):
        mine, box, _, ss, rs, _ = lane
        start, _, size, base, lead = spans[r]
        rank, devices = ranks[r]
        return [
            pltpu.make_async_remote_copy(
                mine.at[pl.ds(start + (rank ^ m) * size, size)], box.at[base + (m - 1) * size:base + m * size],
                ss.at[lead + m - 1], rs.at[lead + m - 1], device_id=devices[m - 1], device_id_type=MESH,
            )
            for m in range(1, len(devices) + 1)
        ]

    def fold(lane, r):
        mine, box, out, _, _, kind = lane
        _, keep, size, base, _ = spans[r]
        here = pl.ds(keep, size)
        part = mine[here].astype(jnp.float32)
        for m in range(len(ranks[r][1])):
            part = part + box[base + m * size:base + (m + 1) * size].astype(jnp.float32)
        (out if r == count - 1 else mine)[here] = part.astype(kind)

    def share(lane, r):
        _, _, out, ss, rs, _ = lane
        _, keep, size, _, lead = spans[r]
        piece = out.at[pl.ds(keep, size)]
        return [
            pltpu.make_async_remote_copy(
                piece, piece, ss.at[links + lead + m - 1], rs.at[links + lead + m - 1], device_id=dev, device_id_type=MESH
            )
            for m, dev in enumerate(ranks[r][1], 1)
        ]

    def event(lane, e):
        if 0 < e <= count:
            for c in spread(lane, e - 1):
                c.wait()
            fold(lane, e - 1)
        elif e > count:
            for c in share(lane, 2 * count - e):
                c.wait()
        if e < count:
            for c in spread(lane, e):
                c.start()
        elif e < 2 * count:
            for c in share(lane, 2 * count - 1 - e):
                c.start()

    last = 2 * count
    gaps = [3] + [6] * (count - 1)
    gaps = gaps + gaps[::-1]
    due = [sum(gaps[:e]) for e in range(last + 1)]

    def lane_of(c):
        return (acc.at[c], inbox.at[c], done.at[c], r_send.at[c], r_recv.at[c], jnp.bfloat16)

    tiny = (s_acc, s_inbox, s_done, s_send, s_recv, jnp.float32)

    def finish(c):
        return pltpu.make_async_copy(done.at[c], sum_ref.at[c], out_sem.at[c])

    def advance(slot):
        for e in range(last, 0, -1):
            if (slot - due[e] - 2) % 3:
                continue
            ready = step + (slot - due[e] - 2) // 3 + 1
            c = ready // merge - 1

            @pl.when((ready >= merge) & (ready % merge == 0))
            def _():
                event(lane_of(c), e)
                if e == last:
                    finish(c).start()

    def r_copy(o):
        return pltpu.make_async_remote_copy(
            rs_ref.at[o], rr_ref.at[me], send.at[o], recv.at[o], device_id=(dp, me ^ o), device_id_type=MESH
        )

    home = pltpu.make_async_copy(rs_ref.at[0], rr_ref.at[me], loc.at[0])
    experts, cap = rs_ref.shape[0], rs_ref.shape[1]

    @pl.when(step == 0)
    def _():
        others = [(dp, me ^ o) for o in range(1, n)]
        for bits, (_, devices) in zip(rounds, ranks):
            if -1 in bits:
                others += [dev for m, dev in enumerate(devices, 1) if m >> bits.index(-1) & 1]
        barrier = pltpu.get_barrier_semaphore()
        for dev in others:
            pl.semaphore_signal(barrier, inc=1, device_id=dev, device_id_type=MESH)
        pl.semaphore_wait(barrier, len(others))
        home.start()
        for o in range(1, n):
            r_copy(o).start()
        s_acc[...] = jnp.zeros_like(s_acc)
        rt_scr[...] = jnp.zeros_like(rt_scr)
        column = lax.broadcasted_iota(jnp.int32, (cap, 128), 1)

        def split(x, _):
            col = jnp.broadcast_to(gg_ref[x][:1, :], (128, 128)).T[:cap, :1]
            high = col.astype(bf16).astype(f32)
            mid = (col - high).astype(bf16).astype(f32)
            low = col - high - mid
            gc_scr[x] = jnp.where(column == 0, high, jnp.where(column == 1, mid, jnp.where(column == 2, low, 0.0))).astype(bf16)
            return 0

        lax.fori_loop(0, experts, split, 0)
        slots = experts * cap
        back = back_ref[...].reshape(slots, width)
        marks = gc_scr[...].reshape(slots, 128)
        where = lax.broadcasted_iota(jnp.int32, (rows, slots), 1)
        choice = lax.broadcasted_iota(jnp.int32, (rows, probs_ref.shape[1]), 1)
        for i in range(0, seq, rows):
            here = slice(i, i + rows)
            s1, s2, gate = stat_ref[here, 0:1], stat_ref[here, 1:2], stat_ref[here, 2:3]
            table = (stat_ref[here, 3:4].astype(jnp.int32) == where).astype(f32).astype(bf16)
            hot = (stat_ref[here, 4:5].astype(jnp.int32) == choice).astype(f32)
            triple = mm(table, marks)
            gate_grad = triple[:, 0:1] + triple[:, 1:2] + triple[:, 2:3]
            lg = ((gate_grad * gate) * (hot - probs_ref[here, :])).astype(bf16)
            rg = mm(table, back) + mm(lg, wr_ref[...], NT)
            gdy = g2_ref[...] * rg
            scaled = after_ref[here, :] * s2
            mean = jnp.sum(gdy * scaled, axis=-1, keepdims=True) * (1.0 / width)
            after = cot_ref[here, :].astype(f32) + s2 * (gdy - scaled * mean)
            routed = (scaled * g2_ref[...]).astype(bf16)
            rt_scr[1:, :] += lax.dot_general(lg, routed, TN, preferred_element_type=f32)
            rt_scr[:1, :] += jnp.sum(rg * scaled, axis=0, keepdims=True)
            ig_ref[here, :] = after
            low = after.astype(bf16)
            br_scr[here, :] = low
            d_scr[here, :] = mm(low, wo_ref[...], NT).astype(bf16)
            xt_scr[:, here] = (tok_ref[here, :].astype(f32) * s1 * g1_ref[...]).astype(bf16).T

    cols = pl.ds(pl.multiple_of(step * 128, 128), 128)
    lane = lax.broadcasted_iota(jnp.int32, (rows, 128), 1)
    sub = lax.broadcasted_iota(jnp.int32, (128, seq), 0)
    qt = q_ref[...].T
    dt = d_scr[:, cols].T
    zero = jnp.bfloat16(0)
    for hh in range(2):
        half = (sub >= 64) if hh else (sub < 64)
        qt_scr[:, hh * seq:(hh + 1) * seq] = jnp.where(half, qt, zero)
        dt_scr[:, hh * seq:(hh + 1) * seq] = jnp.where(half, dt, zero)
    for hh in range(2):
        own = (lane >= 64) if hh else (lane < 64)
        near_scr[...] = jnp.zeros_like(near_scr)
        far_scr[...] = jnp.zeros_like(far_scr)
        for i in range(seq // rows):
            r0 = i * rows
            d = jnp.where(own, d_scr[r0:r0 + rows, cols], zero)
            grown = mm(d, v_ref[...], NT)
            delta = jnp.sum(d.astype(jnp.float32) * o_ref[r0:r0 + rows, :].astype(jnp.float32), axis=-1, keepdims=True)
            ds = p_ref[hh, r0:r0 + rows, :].astype(jnp.float32) * (grown - delta)
            low = ds.astype(jnp.bfloat16)
            ds_scr[r0:r0 + rows, :] = low
            for a in range(rows // 128):
                bi = r0 // 128 + a
                strip = ds[a * 128:(a + 1) * 128]
                lo, hi = max(bi - 1, 0), min(bi + 2, blocks)
                near_scr[:, (lo - bi + 1) * 128:(hi - bi + 1) * 128] += strip[:, lo * 128:hi * 128]
                if lo > 0:
                    t = strip[:, :128]
                    for j in range(1, lo):
                        t = t + strip[:, j * 128:(j + 1) * 128]
                    far_scr[:, :128] += t
                if hi < blocks:
                    t = strip[:, hi * 128:(hi + 1) * 128]
                    for j in range(hi + 1, blocks):
                        t = t + strip[:, j * 128:(j + 1) * 128]
                    far_scr[:, 128:] += t
            dq = (0.125 * mm(low, k_ref[...])).astype(jnp.bfloat16)
            if hh == 0:
                dz_scr[r0:r0 + rows, :128] = dq
            else:
                dz_scr[r0:r0 + rows, :128] = jnp.where(own, dq, dz_scr[r0:r0 + rows, :128])
        part = mm(qt_scr[:, hh * seq:(hh + 1) * seq], ds_scr[...])
        dkt = part if hh == 0 else dkt + part
        a = near_scr[...]
        w = 128
        while w > 1:
            w //= 2
            a = a[:w] + pltpu.roll(a[w:], 512 - w, axis=1)
        nf_scr[pl.ds(2 * step + hh, 1), :512] = a
        nf_scr[pl.ds(2 * step + hh, 1), 512:] = jnp.sum(far_scr[...], axis=0, keepdims=True)
        if hh == 0:
            advance(0)
    advance(1)
    dz_scr[:, 128:256] = (0.125 * dkt).astype(jnp.bfloat16).T
    dvt = mm(dt_scr[...], p_ref[...].reshape(2 * seq, seq))
    dz_scr[:, 256:] = dvt.astype(jnp.bfloat16).T
    dz = dz_scr[...]
    dw = mm(xt_scr[...], dz).astype(jnp.bfloat16)
    go = lax.dot_general(o_ref[...], br_scr[...], TN, preferred_element_type=f32).astype(bf16)
    tiles = [dw[:, j * 128:(j + 1) * 128] for j in range(3)]
    tiles.append(jnp.concatenate([go[:, j * 128:(j + 1) * 128] for j in range(pairs)], axis=0))
    mine = step // merge
    per = width // depth
    for turn in range(merge):

        @pl.when(step % merge == turn)
        def _():
            for j in range(4):
                at = (turn * 4 + j) * per
                acc[mine, at:at + per] = tiles[j].reshape(per, depth, 128)

    w = jnp.concatenate([wq_ref[...], wk_ref[...], wv_ref[...]], axis=1)
    ng = mm(dz, w, NT)

    @pl.when(step == 0)
    def _():
        ng_scr[...] = ng

    @pl.when(step > 0)
    def _():
        ng_scr[...] += ng

    advance(2)

    @pl.when((step + 1) % merge == 0)
    def _():
        event(lane_of(mine), 0)

    @pl.when(step == pairs - 1)
    def _():
        gain = jnp.zeros((1, width), f32)
        for i in range(0, seq, rows):
            here = slice(i, i + rows)
            scaled = tok_ref[here, :].astype(f32) * stat_ref[here, 0:1]
            gain = gain + jnp.sum(ng_scr[here, :] * scaled, axis=0, keepdims=True)
        pieces = [gain] + [nf_scr[h:h + 1, :] for h in range(2 * pairs)] + [rt_scr[h:h + 1, :] for h in range(rt_scr.shape[0])]
        for i, piece in enumerate(pieces):
            for j in range(6):
                r = i * 6 + j
                s_acc[r // 8, r % 8:r % 8 + 1, :] = piece[:, j * 128:(j + 1) * 128]
        event(tiny, 0)
        left = []
        for c in range(chunks):
            ready = 3 * (c * merge + merge - 1) + 2
            left.append([e for e in range(1, last + 1) if ready + due[e] > 3 * pairs - 1])
        for turn in range(1, last + 1):
            event(tiny, turn)
            for c in range(chunks):
                if left[c]:
                    e = left[c].pop(0)
                    event(lane_of(c), e)
                    if e == last:
                        finish(c).start()
            if turn == 1:
                for i in range(0, seq, rows):
                    here = slice(i, i + rows)
                    s1 = stat_ref[here, 0:1]
                    scaled = tok_ref[here, :].astype(f32) * s1
                    gdy = g1_ref[...] * ng_scr[here, :]
                    mean = jnp.sum(gdy * scaled, axis=-1, keepdims=True) * (1.0 / width)
                    ig_ref[here, :] += s1 * (gdy - scaled * mean)
        small_out[...] = s_done[...]
        for c in range(chunks):
            finish(c).wait()
        home.wait()
        for o in range(1, n):
            r_copy(o).wait()


def rounds_of(n):
    bits = n.bit_length() - 1
    if bits == 4:
        return [[0], [1, -1], [2, 3]]
    rest = list(range(1, bits)) + [-1]
    return [[0]] + [rest[i:i + 2] for i in range(0, len(rest), 2)]


def attn_bwd(q, k, v, o, p, wq, wk, wv, tokens, cotangent, after_attn, stats, probs, g1, g2, wr, wo, back, gg, rs, rows=256):
    f32, bf16 = jnp.float32, jnp.bfloat16
    seq, width = q.shape
    pairs = width // 128
    n, cap = rs.shape[:2]
    total = 2 * n
    experts = probs.shape[1]
    links = sum((1 << len(bits)) - 1 for bits in rounds_of(n))
    merge = 1
    while 4 * width * merge % (total * 8):
        merge += 1
    chunks = pairs // merge
    depth = 4 * width * merge // total
    col = pl.BlockSpec((seq, 128), lambda h: (0, h))
    wcol = pl.BlockSpec((width, 128), lambda h: (0, h))

    def whole(shape):
        return pl.BlockSpec(shape, lambda h: (0,) * len(shape), pipeline_mode=pl.Buffered(1))

    hbm = pl.BlockSpec(memory_space=pl.ANY)
    dma = pltpu.SemaphoreType.DMA
    small = (total, 8, 128)
    store = pltpu.VMEM((chunks, total, depth, 128), bf16)
    small_store = pltpu.VMEM(small, f32)
    singles = (tokens, cotangent, after_attn, stats, probs, g1, g2, wr, wo, back, gg)
    return pl.pallas_call(
        functools.partial(bwd_kernel, rows, merge),
        grid=(pairs,),
        in_specs=[col] * 4 + [pl.BlockSpec((2, seq, seq), lambda h: (h, 0, 0))] + [wcol] * 3 + [whole(x.shape) for x in singles] + [hbm],
        out_specs=[whole((seq, width)), whole(small), hbm, hbm],
        out_shape=[
            jax.ShapeDtypeStruct((seq, width), f32),
            jax.ShapeDtypeStruct(small, f32),
            jax.ShapeDtypeStruct((chunks, total, depth, 128), bf16),
            jax.ShapeDtypeStruct(rs.shape, rs.dtype),
        ],
        scratch_shapes=[
            pltpu.VMEM((seq, seq), bf16), pltpu.VMEM((128, 2 * seq), bf16), pltpu.VMEM((128, 2 * seq), bf16),
            pltpu.VMEM((128, 512), f32), pltpu.VMEM((128, 256), f32),
            pltpu.VMEM((width, seq), bf16), pltpu.VMEM((seq, width), bf16), pltpu.VMEM((seq, width), bf16), pltpu.VMEM((seq, 384), bf16),
            pltpu.VMEM((2 * pairs + 4, 768), f32), pltpu.VMEM((seq, width), f32), pltpu.VMEM((1 + experts, width), f32),
            pltpu.VMEM((n, cap, 128), bf16),
            store, store, store, small_store, small_store, small_store,
            dma((n,)), dma((n,)), dma((1,)),
            dma((chunks, 2 * links)), dma((chunks, 2 * links)), dma((2 * links,)), dma((2 * links,)), dma((chunks,)),
        ],
        compiler_params=pltpu.CompilerParams(
            dimension_semantics=("arbitrary",), collective_id=4, has_side_effects=True, vmem_limit_bytes=63 << 20
        ),
        name="attn_bwd",
    )(q, k, v, o, p, wq, wk, wv, *singles, rs)

def finish_kernel(sum_ref, q_ref, k_ref, v_ref, o_ref):
    for j, out in enumerate((q_ref, k_ref, v_ref)):
        out[...] = sum_ref[0, j].astype(jnp.float32)
    for i in range(sum_ref.shape[2] // 128):
        o_ref[:, i * 128:(i + 1) * 128] = sum_ref[0, 3, i * 128:(i + 1) * 128].astype(jnp.float32)


def finish_sums(sums):
    pairs, _, depth, _ = sums.shape
    col = pl.BlockSpec((depth, 128), lambda h: (0, h))
    return pl.pallas_call(
        finish_kernel,
        grid=(pairs,),
        in_specs=[pl.BlockSpec((1, 4, depth, 128), lambda h: (h, 0, 0, 0))],
        out_specs=[col] * 3 + [pl.BlockSpec((128, depth), lambda h: (h, 0))],
        out_shape=[jax.ShapeDtypeStruct((depth, 128 * pairs), jnp.float32)] * 4,
        compiler_params=pltpu.CompilerParams(dimension_semantics=("arbitrary",), vmem_limit_bytes=16 << 20),
        name="finish_sums",
    )(sums)

eps_norm = 1e-06
thresholds = (12, 16, 23, 32, 46, 64, 91)


def bucket_of(offset):
    distance = np.abs(offset)
    far = 8 + sum((distance >= t).astype(np.int32) for t in thresholds)
    return np.where(distance < 8, distance, far) + 16 * (offset > 0)


def hot_of(offset):
    return (bucket_of(offset)[..., None] == np.arange(32)).astype(np.float32)


def local(dp_count, tokens, routes, cotangent, gain_first, w_query, w_key, w_value, w_output, bias_table, gain_second, w_router, expert_in, expert_out):
    f32, bf16 = jnp.float32, jnp.bfloat16
    seq, width = tokens.shape
    heads = bias_table.shape[1]
    experts = w_router.shape[1]
    cap = (5 * seq + 4 * experts - 1) // (4 * experts)
    capp = (cap + 15) // 16 * 16
    slots = experts * capp
    ids = routes[:, 0]
    hot = (ids[:, None] == jnp.arange(experts, dtype=jnp.int32)[None, :]).astype(bf16)
    order = jnp.arange(seq, dtype=jnp.int32)
    before = (order[:, None] > order[None, :]).astype(bf16)
    hot32 = hot.astype(f32)
    position = jnp.sum(mm(before, hot) * hot32, axis=1).astype(jnp.int32)
    slot = jnp.where(position < cap, ids * capp + position, -1)
    table = (slot[:, None] == jnp.arange(slots, dtype=jnp.int32)[None, :]).astype(bf16)

    def pick(values):
        return jnp.sum(table.astype(f32) * values[:, None], axis=0)

    cot_slots = mm(table, cotangent, TN).astype(bf16).reshape(experts, capp, width)

    inputs = tokens.astype(f32)
    g1 = gain_first.astype(f32)
    s1 = lax.rsqrt(jnp.mean(inputs * inputs, axis=-1, keepdims=True) + eps_norm)
    normed_low = (inputs * s1 * g1).astype(bf16)
    q = mm(normed_low, w_query).astype(bf16)
    k = mm(normed_low, w_key).astype(bf16)
    v = mm(normed_low, w_value).astype(bf16)
    near_hot = jnp.asarray(hot_of(np.arange(512) - 256), f32)
    gvec = jnp.einsum("ub,bh->hu", near_hot, bias_table.astype(f32), precision=lax.Precision.HIGHEST)
    attended, probs_low, cot_rows, cot_far = attn_fwd(gvec.reshape(heads // 2, 2, 512), q, k, v, cot_slots)
    after_attn = inputs + mm(attended, w_output)
    g2 = gain_second.astype(f32)
    s2 = lax.rsqrt(jnp.mean(after_attn * after_attn, axis=-1, keepdims=True) + eps_norm)
    routed_low = (after_attn * s2 * g2).astype(bf16)
    rows = mm(table, routed_low, TN).astype(bf16).reshape(experts, capp, width)
    router_probs = jax.nn.softmax(mm(routed_low, w_router), axis=-1)
    gate = jnp.sum(router_probs * hot32, axis=1)
    gates = jnp.broadcast_to(jnp.pad(pick(gate).reshape(experts, 1, capp), ((0, 0), (0, 0), (0, 128 - capp))), (experts, 8, 128))
    back_tokens, gate_grads, produced, grad_in, grad_out = expert_pass(rows, gates, cot_rows, cot_far, expert_in[0], expert_out[0])
    stats = jnp.stack([s1[:, 0], s2[:, 0], gate, slot.astype(f32), ids.astype(f32), gate, gate, gate], axis=1)
    input_grad, small, sums, returned = attn_bwd(
        q, k, v, attended, probs_low, w_query, w_key, w_value, tokens, cotangent, after_attn, stats, router_probs,
        g1[None, :], g2[None, :], w_router, w_output, back_tokens, gate_grads, produced,
    )
    grad_query, grad_key, grad_value, grad_output = finish_sums(sums.reshape(heads // 2, 4, width, 128))
    small = small.reshape(-1)[:(2 + heads + experts) * 768].reshape(-1, 768)
    gain_one, strips, gain_two, router_rows = small[0], small[1:1 + heads], small[1 + heads], small[2 + heads:]
    grad_router = router_rows.T
    near_index = jnp.asarray(hot_of((np.arange(512) + 128) % 512 - 256))
    table_grad = jnp.einsum("hu,ub->bh", strips[:, :512], near_index, precision=lax.Precision.HIGHEST)
    left, right = jnp.sum(strips[:, 512:640], axis=1), jnp.sum(strips[:, 640:], axis=1)
    bucket = jnp.arange(32, dtype=jnp.int32)[:, None]
    table_grad = table_grad + jnp.where(bucket == 15, left[None, :], 0.0) + jnp.where(bucket == 31, right[None, :], 0.0)
    combined = mm(table, returned.reshape(slots, width))
    output = (after_attn + gate[:, None] * combined).astype(bf16)
    return (
        output,
        input_grad,
        gain_one,
        grad_query,
        grad_key,
        grad_value,
        grad_output,
        table_grad,
        gain_two,
        grad_router,
        grad_in[None].astype(f32),
        grad_out[None].astype(f32),
    )


def solution(mesh):
    split, whole = P(("dp", "expert"), None), P()
    in_specs = (split, split, split, whole, whole, whole, whole, whole, whole, whole, whole, P("expert", None, None), P("expert", None, None))
    out_specs = (split, split) + (whole,) * 8 + (P("expert", None, "dp"), P("expert", "dp", None))
    return jax.shard_map(
        functools.partial(local, mesh.shape["dp"]), mesh=mesh, in_specs=in_specs, out_specs=out_specs, check_vma=False
    )
```

```python
import functools

import jax
import jax.numpy as jnp
import numpy as np
from jax import lax
from jax.experimental import pallas as pl
from jax.experimental.pallas import tpu as pltpu
from jax.sharding import PartitionSpec as P

NT = (((1,), (1,)), ((), ()))
NN = (((1,), (0,)), ((), ()))
TN = (((0,), (0,)), ((), ()))


def mm(a, b, dims=NN):
    return lax.dot_general(a, b, dims, preferred_element_type=jnp.float32)


MESH = pl.DeviceIdType.MESH
gelu_a, gelu_b = 0.7978845608, 0.044715


def enter(axis_size, across=False):
    me, dp = lax.axis_index("expert"), lax.axis_index("dp")
    barrier = pltpu.get_barrier_semaphore()
    for step in range(1, axis_size):
        pl.semaphore_signal(barrier, inc=1, device_id=(dp, me ^ step), device_id_type=MESH)
    if across:
        pl.semaphore_signal(barrier, inc=1, device_id=(1 - dp, me), device_id_type=MESH)
    pl.semaphore_wait(barrier, axis_size if across else axis_size - 1)
    return dp, me


def expert_kernel(
    groups, tile, early,
    xs_ref, gs_ref, cot_ref, far_ref, win_ref, wout_ref,
    back_ref, gg_ref, ret_ref, gin_ref, gout_ref,
    x_scr, c_scr, g_scr, w1, w2, a_scr, p_scr, ag_scr, pg_scr, r_scr, b_scr, e_scr, sq_scr, gin, gout,
    x_send, x_recv, g_send, g_recv, b_send, b_recv, e_send, e_recv, loc, wsem, csem, rsem, osem, f_send, f_recv,
):
    f32, bf16 = jnp.float32, jnp.bfloat16
    n, cap, width = xs_ref.shape
    ff = win_ref.shape[1]
    half = ff // 2
    size = n // groups
    rows = size * cap
    dp, me = enter(n, True)
    mine = pl.multiple_of(dp * half, 128)
    rest = pl.multiple_of((1 - dp) * half, 128)
    weights = [
        pltpu.make_async_copy(win_ref.at[:, pl.ds(mine, half)], w1.at[:, :half], wsem.at[0]),
        pltpu.make_async_copy(win_ref.at[:, pl.ds(rest, half)], w1.at[:, half:], wsem.at[1]),
        pltpu.make_async_copy(wout_ref.at[pl.ds(mine, half), :], w2.at[:half, :], wsem.at[2]),
        pltpu.make_async_copy(wout_ref.at[pl.ds(rest, half), :], w2.at[half:, :], wsem.at[3]),
    ]
    own = [
        pltpu.make_async_copy(xs_ref.at[me], x_scr.at[0, 0], loc.at[0]),
        pltpu.make_async_copy(gs_ref.at[me], g_scr.at[0, 0], loc.at[1]),
    ]
    cots = [
        pltpu.make_async_copy(cot_ref, c_scr.at[0], csem.at[0]),
        pltpu.make_async_copy(far_ref.at[:early], c_scr.at[1, :early], csem.at[1]),
    ]

    def remote(src, dst, send, recv, dev):
        return pltpu.make_async_remote_copy(src, dst, send, recv, device_id=dev, device_id_type=MESH)

    def x_copy(o):
        return remote(xs_ref.at[me ^ o], x_scr.at[0, o], x_send.at[o], x_recv.at[o], (dp, me ^ o))

    def g_copy(o):
        return remote(gs_ref.at[me ^ o], g_scr.at[0, o], g_send.at[o], g_recv.at[o], (dp, me ^ o))

    def b_copy(o):
        return remote(b_scr.at[o], back_ref.at[me], b_send.at[o], b_recv.at[o], (dp, me ^ o))

    def e_copy(o):
        return remote(e_scr.at[o], gg_ref.at[me], e_send.at[o], e_recv.at[o], (dp, me ^ o))

    def r_copy(o):
        return pltpu.make_async_copy(r_scr.at[o], ret_ref.at[o], rsem.at[o])

    over = (1 - dp, me)
    c_over = remote(cot_ref.at[early:], c_scr.at[1, early:], f_send.at[groups], f_recv.at[groups], over)
    g_over = remote(g_scr.at[0], g_scr.at[1], f_send.at[groups + 1], f_recv.at[groups + 1], over)

    def x_over(g):
        span = slice(g * size, (g + 1) * size)
        return remote(x_scr.at[0, span], x_scr.at[1, span], f_send.at[g], f_recv.at[g], over)

    def each(lo, hi, fn):
        if hi - lo <= 4:
            for o in range(lo, hi):
                fn(o)
        else:
            lax.fori_loop(lo, hi, lambda o, c: (fn(o), c)[1], 0)

    for c in own:
        c.start()
    each(1, n, lambda o: g_copy(o).start())
    each(1, n, lambda o: x_copy(o).start())
    c_over.start()
    for c in cots + weights:
        c.start()
    sq_scr[...] = jnp.zeros_like(sq_scr)

    def gated(side, lo, hi):
        def one(o):
            col = jnp.broadcast_to(g_scr[side, o][:1, :], (128, 128)).T[:cap, :1]
            c_scr[side, o] = (c_scr[side, o].astype(f32) * col).astype(bf16)

        each(lo, hi, one)

    def hidden(x, ct, f):
        u = mm(x, w1[:, f:f + tile])
        back = mm(ct, w2[f:f + tile, :], NT)
        uu = u * u
        t = jnp.tanh(u * (gelu_a + (gelu_a * gelu_b) * uu))
        hp = 0.5 + 0.5 * t
        act = u * hp
        slope = hp + act * ((1.0 - t) * (gelu_a + (3.0 * gelu_a * gelu_b) * uu))
        return act.astype(bf16), (back * slope).astype(bf16)

    for g in range(groups):
        lo, hi = g * size, (g + 1) * size
        if g == 0:
            for c in own + cots[:1]:
                c.wait()
        each(max(lo, 1), hi, lambda o: g_copy(o).wait_recv())
        raw = c_scr[0, lo:hi].reshape(rows, width)
        gated(0, lo, hi)
        each(max(lo, 1), hi, lambda o: x_copy(o).wait_recv())
        x_over(g).start()
        if g == 0:
            for c in weights:
                c.wait()
        x = x_scr[0, lo:hi].reshape(rows, width)
        ct = c_scr[0, lo:hi].reshape(rows, width)
        span = slice(g * rows, (g + 1) * rows)
        for f in range(0, ff, tile):
            act, pre = hidden(x, ct, f)
            if f < half:
                a_scr[span, f:f + tile] = act
                p_scr[span, f:f + tile] = pre
            else:
                ag_scr[:, f - half:f - half + tile] = act
                pg_scr[:, f - half:f - half + tile] = pre
        back = mm(p_scr[span, :], w1[:, :half], NT) + mm(pg_scr[...], w1[:, half:], NT)
        b_scr[lo:hi] = back.astype(bf16).reshape(size, cap, width)
        each(max(lo, 1), hi, lambda o: b_copy(o).start())
        r = mm(a_scr[span, :], w2[:half, :]) + mm(ag_scr[...], w2[half:, :])
        r_scr[lo:hi] = r.astype(bf16).reshape(size, cap, width)
        dots = r * raw.astype(f32)
        part = dots[:, :128]
        for j in range(1, width // 128):
            part = part + dots[:, j * 128:(j + 1) * 128]
        part = part.reshape(size, cap, 128)
        for o in range(lo, hi):
            sq_scr[:cap, :] = part[o - lo]
            line = jnp.sum(sq_scr[...].T, axis=0, keepdims=True)
            e_scr[o] = jnp.broadcast_to(line, (8, 128))
        each(max(lo, 1), hi, lambda o: e_copy(o).start())
    g_over.start()
    each(0, n, lambda o: r_copy(o).start())
    own_back = [
        pltpu.make_async_copy(b_scr.at[0], back_ref.at[me], loc.at[0]),
        pltpu.make_async_copy(e_scr.at[0], gg_ref.at[me], loc.at[1]),
    ]
    for c in own_back:
        c.start()
    total = n * cap

    def gradients(side, first):
        x = x_scr[side].reshape(total, width)
        ct = c_scr[side].reshape(total, width)
        for f in range(0, half, tile):
            part = lax.dot_general(x, p_scr[:, f:f + tile], TN, preferred_element_type=f32)
            if first:
                gin[:, f:f + tile] = part
            else:
                w1[:, f:f + tile] = (gin[:, f:f + tile] + part).astype(bf16)
            part = lax.dot_general(a_scr[:, f:f + tile], ct, TN, preferred_element_type=f32)
            if first:
                gout[f:f + tile, :] = part
            else:
                w2[f:f + tile, :] = (gout[f:f + tile, :] + part).astype(bf16)
                for c in outs(f):
                    c.start()

    def outs(f):
        i = f // tile
        return [
            pltpu.make_async_copy(w1.at[:, f:f + tile], gin_ref.at[:, f:f + tile], osem.at[2 * i]),
            pltpu.make_async_copy(w2.at[f:f + tile, :], gout_ref.at[f:f + tile, :], osem.at[2 * i + 1]),
        ]

    gradients(0, True)
    cots[1].wait()
    c_over.wait()
    g_over.wait()
    gated(1, 0, n)
    for g in range(groups):
        lo, hi = g * size, (g + 1) * size
        x_over(g).wait()
        x = x_scr[1, lo:hi].reshape(rows, width)
        ct = c_scr[1, lo:hi].reshape(rows, width)
        for f in range(0, half, tile):
            act, pre = hidden(x, ct, f)
            a_scr[g * rows:(g + 1) * rows, f:f + tile] = act
            p_scr[g * rows:(g + 1) * rows, f:f + tile] = pre
    gradients(1, False)
    for f in range(0, half, tile):
        for c in outs(f):
            c.wait()
    for c in own_back:
        c.wait()
    each(0, n, lambda o: r_copy(o).wait())
    each(1, n, lambda o: x_copy(o).wait_send())
    each(1, n, lambda o: g_copy(o).wait_send())
    each(1, n, lambda o: b_copy(o).wait())
    each(1, n, lambda o: e_copy(o).wait())


def expert_pass(xs, gs, cot, far, w_in, w_out):
    f32, bf16 = jnp.float32, jnp.bfloat16
    n, cap, width = xs.shape
    ff = w_in.shape[1]
    half = ff // 2
    groups, tile = (4, 512) if n * cap <= 1280 else (8, 256)
    rows = n // groups * cap
    hbm = pl.BlockSpec(memory_space=pl.ANY)
    dma = pltpu.SemaphoreType.DMA
    flat = jax.ShapeDtypeStruct((n, cap, width), bf16)
    return pl.pallas_call(
        functools.partial(expert_kernel, groups, tile, n // 2),
        in_specs=[hbm] * 6,
        out_specs=[hbm] * 5,
        out_shape=[
            flat, jax.ShapeDtypeStruct((n, 8, 128), f32), flat,
            jax.ShapeDtypeStruct((width, half), bf16), jax.ShapeDtypeStruct((half, width), bf16),
        ],
        scratch_shapes=[
            pltpu.VMEM((2, n, cap, width), bf16), pltpu.VMEM((2, n, cap, width), bf16), pltpu.VMEM((2, n, 8, 128), f32),
            pltpu.VMEM((width, ff), bf16), pltpu.VMEM((ff, width), bf16),
            pltpu.VMEM((n * cap, half), bf16), pltpu.VMEM((n * cap, half), bf16),
            pltpu.VMEM((rows, half), bf16), pltpu.VMEM((rows, half), bf16),
            pltpu.VMEM((n, cap, width), bf16), pltpu.VMEM((n, cap, width), bf16), pltpu.VMEM((n, 8, 128), f32),
            pltpu.VMEM((128, 128), f32), pltpu.VMEM((width, half), f32), pltpu.VMEM((half, width), f32),
        ] + [dma((n,))] * 8 + [dma((2,)), dma((4,)), dma((2,)), dma((n,)), dma((2 * half // tile,)), dma((groups + 2,)), dma((groups + 2,))],
        compiler_params=pltpu.CompilerParams(collective_id=1, has_side_effects=True, vmem_limit_bytes=62 << 20),
        name="experts",
    )(xs, gs, cot, far, w_in, w_out)

eps_norm = 1e-06
thresholds = (12, 16, 23, 32, 46, 64, 91)


def fwd_kernel(
    rows, limit, tok_ref, cot_ref, ids_ref, bias_ref, gains_ref, wq_ref, wk_ref, wv_ref, wo_ref, wr_ref,
    q_ref, k_ref, v_ref, o_ref, p_ref, aa_ref, probs_ref, stat_ref, xs_ref, gs_ref, cr_ref, cp_ref,
    b_scr, xn_scr, cs_scr, t_scr, rt_scr, gm_scr, sq_scr, vx_scr, g_scr, row_scr, hot_scr, send, recv, loc, f_send, f_recv,
):
    f32, bf16 = jnp.float32, jnp.bfloat16
    seq, width = tok_ref.shape
    blocks = seq // 128
    step = pl.program_id(0)
    n, cap = cs_scr.shape[:2]
    me, dp = lax.axis_index("expert"), lax.axis_index("dp")
    quarter = n // 4
    g1, g2 = gains_ref[0:1, :].astype(f32), gains_ref[1:2, :].astype(f32)

    def remote(src, dst, ss, rs, dev):
        return pltpu.make_async_remote_copy(src, dst, ss, rs, device_id=dev, device_id_type=MESH)

    def c_copy(o):
        return remote(cs_scr.at[o], cr_ref.at[o], send.at[o], recv.at[o], (dp, me ^ o))

    def over(i):
        span = pl.ds(i * quarter, quarter)
        return remote(cr_ref.at[span], cp_ref.at[span], f_send.at[i], f_recv.at[i], (1 - dp, me))

    home = pltpu.make_async_copy(cs_scr.at[0], cr_ref.at[0], loc.at[0])

    def choose(first, pick):
        def one(i, _):
            ids = lax.broadcasted_iota(jnp.int32, (cap, seq), 0) + pick(first + i) * cap
            t_scr[pl.ds(pl.multiple_of(i * cap, 16), cap), :] = (ids == row_scr[0:1, :]).astype(f32).astype(bf16)
            return 0

        lax.fori_loop(0, quarter, one, 0)

    @pl.when(step == 0)
    def _():
        spread = jnp.broadcast_to(ids_ref[...].astype(f32), (128, seq)).T
        choice = lax.broadcasted_iota(jnp.int32, (seq, n), 1)
        routes = spread[:, :1].astype(jnp.int32)
        hot_scr[...] = (routes == choice).astype(f32).astype(bf16)
        for i in range(0, seq, rows):
            here = slice(i, i + rows)
            later = lax.broadcasted_iota(jnp.int32, (rows, seq), 0) + i
            before = (later > lax.broadcasted_iota(jnp.int32, (rows, seq), 1)).astype(f32).astype(bf16)
            position = jnp.sum(mm(before, hot_scr[...]) * hot_scr[here, :].astype(f32), axis=-1, keepdims=True)
            ids = spread[here, :1]
            slot = jnp.where(position < limit, ids * cap + position, -1.0)
            row_scr[:, here] = jnp.broadcast_to(slot, (rows, 128)).T[:8, :].astype(jnp.int32)
            x = tok_ref[here, :].astype(f32)
            s1 = lax.rsqrt(jnp.mean(x * x, axis=-1, keepdims=True) + eps_norm)
            slim = lax.broadcasted_iota(jnp.int32, (rows, 8), 1)
            stat_ref[here, :] = jnp.where(slim == 0, s1, jnp.where(slim == 3, slot, ids))
            xn_scr[here, :] = (x * s1 * g1).astype(bf16)
            aa_ref[here, :] = x
        enter(n, True)
        for g in range(4):
            lo = g * quarter
            choose(lo, lambda o: me ^ o)
            cs_scr[lo:lo + quarter] = mm(t_scr[...], cot_ref[...]).astype(bf16).reshape(quarter, cap, width)
            if g == 0:
                home.start()
            for o in range(max(lo, 1), lo + quarter):
                c_copy(o).start()
        offset = lax.broadcasted_iota(jnp.int32, (32, 512), 1) - 256
        distance = jnp.abs(offset)
        far = jnp.full(offset.shape, 8, jnp.int32)
        for t in thresholds:
            far = far + (distance >= t).astype(jnp.int32)
        bucket = jnp.where(distance < 8, distance, far) + 16 * (offset > 0).astype(jnp.int32)
        pick = (bucket == lax.broadcasted_iota(jnp.int32, (32, 512), 0)).astype(f32).astype(bf16)
        g_scr[...] = mm(bias_ref[...], pick)
        vx_scr[:, 128:] = jnp.ones((seq, 128), bf16)

    for i in range(2):

        @pl.when(step == 2 + 2 * i)
        def _():
            if i == 0:
                home.wait()
            for o in range(max(1, i * quarter), (i + 1) * quarter):
                c_copy(o).wait_recv()
            over(i).start()

    for w_ref, out in ((wq_ref, q_ref), (wk_ref, k_ref), (wv_ref, v_ref)):
        out[...] = mm(xn_scr[...], w_ref[...]).astype(bf16)
    vx_scr[:, :128] = v_ref[...]
    lane = lax.broadcasted_iota(jnp.int32, (rows, 128), 1)
    for hh in range(2):
        own = (lane >= 64) if hh else (lane < 64)
        g = g_scr[pl.ds(2 * step + hh, 1), :]
        near = pltpu.roll(jnp.broadcast_to(g, (128, 512)), 384, axis=1, stride=1, stride_axis=0)
        mid = (blocks - 2) * 128
        b_scr[:, :mid] = jnp.broadcast_to(g[:, :1], (128, mid))
        b_scr[:, mid:mid + 384] = near[:, :384]
        b_scr[:, mid + 384:] = jnp.broadcast_to(g[:, 511:], (128, b_scr.shape[1] - mid - 384))
        for i in range(seq // rows):
            r0 = i * rows
            q = q_ref[r0:r0 + rows, :]
            qm = jnp.where(own, q * jnp.bfloat16(0.125), jnp.bfloat16(0))
            s = mm(qm, k_ref[...], NT)
            parts = []
            for a in range(rows // 128):
                c0 = (blocks - 1 - (r0 // 128 + a)) * 128
                parts.append(s[a * 128:(a + 1) * 128] + b_scr[:, c0:c0 + seq])
            s = jnp.concatenate(parts, 0) if len(parts) > 1 else parts[0]
            m = jnp.max(s, axis=-1, keepdims=True)
            e = jnp.exp(s - m)
            raw = mm(e.astype(bf16), vx_scr[...])
            inv = 1.0 / raw[:, 128:129]
            p_ref[hh, r0:r0 + rows, :] = (e * inv).astype(bf16)
            o = (raw[:, :128] * inv).astype(bf16)
            if hh == 0:
                o_ref[r0:r0 + rows, :] = o
            else:
                o = jnp.where(own, o, o_ref[r0:r0 + rows, :])
                o_ref[r0:r0 + rows, :] = o
                aa_ref[r0:r0 + rows, :] += mm(o, wo_ref[...])

    @pl.when(step == pl.num_programs(0) - 1)
    def _():
        slim = lax.broadcasted_iota(jnp.int32, (rows, 8), 1)
        wide = lax.broadcasted_iota(jnp.int32, (rows, 128), 1)
        for i in range(0, seq, rows):
            here = slice(i, i + rows)
            aa = aa_ref[here, :]
            s2 = lax.rsqrt(jnp.mean(aa * aa, axis=-1, keepdims=True) + eps_norm)
            routed = (aa * s2 * g2).astype(bf16)
            rt_scr[here, :] = routed
            logits = mm(routed, wr_ref[...], NT)
            e = jnp.exp(logits - jnp.max(logits, axis=-1, keepdims=True))
            probs = e / jnp.sum(e, axis=-1, keepdims=True)
            probs_ref[here, :] = probs
            gate = jnp.sum(probs * hot_scr[here, :].astype(f32), axis=-1, keepdims=True)
            stat_ref[here, :] = jnp.where(slim == 1, s2, jnp.where(slim == 2, gate, stat_ref[here, :]))
            high = gate.astype(bf16).astype(f32)
            middle = (gate - high).astype(bf16).astype(f32)
            low = gate - high - middle
            gm_scr[here, :] = jnp.where(wide == 0, high, jnp.where(wide == 1, middle, jnp.where(wide == 2, low, 0.0))).astype(bf16)
        sq_scr[...] = jnp.zeros_like(sq_scr)
        for g in range(4):
            lo = g * quarter
            choose(lo, lambda x: x)
            xs_ref[lo:lo + quarter] = mm(t_scr[...], rt_scr[...]).astype(bf16).reshape(quarter, cap, width)
            gates = mm(t_scr[...], gm_scr[...]).reshape(quarter, cap, 128)
            for x in range(quarter):
                sq_scr[:cap, :] = gates[x]
                gs_ref[lo + x] = jnp.broadcast_to(jnp.sum(sq_scr[...].T, axis=0, keepdims=True), (8, 128))
        for o in range(1, n):
            c_copy(o).wait_send()
        for o in range(n // 2, n):
            c_copy(o).wait_recv()
        for i in range(2):
            over(i).wait()


def attn_fwd(tokens, cotangent, ids, bias, gains, wq, wk, wv, wo, wr, limit, cap, rows=256):
    f32, bf16 = jnp.float32, jnp.bfloat16
    seq, width = tokens.shape
    pairs = width // 128
    n = wr.shape[0]
    col = pl.BlockSpec((seq, 128), lambda h: (0, h))
    wcol = pl.BlockSpec((width, 128), lambda h: (0, h))

    def whole(shape):
        return pl.BlockSpec(shape, lambda h: (0,) * len(shape), pipeline_mode=pl.Buffered(1))

    hbm = pl.BlockSpec(memory_space=pl.ANY)
    dma = pltpu.SemaphoreType.DMA
    tall = jax.ShapeDtypeStruct((seq, width), bf16)
    fixed = [
        jax.ShapeDtypeStruct((seq, width), f32), jax.ShapeDtypeStruct((seq, n), f32), jax.ShapeDtypeStruct((seq, 8), f32),
        jax.ShapeDtypeStruct((n, cap, width), bf16), jax.ShapeDtypeStruct((n, 8, 128), f32),
    ]
    return pl.pallas_call(
        functools.partial(fwd_kernel, rows, limit),
        grid=(pairs,),
        in_specs=[whole(x.shape) for x in (tokens, cotangent, ids, bias, gains)]
        + [wcol] * 3 + [pl.BlockSpec((128, width), lambda h: (h, 0)), whole(wr.shape)],
        out_specs=[col] * 4 + [pl.BlockSpec((2, seq, seq), lambda h: (h, 0, 0))] + [whole(x.shape) for x in fixed] + [hbm, hbm],
        out_shape=[tall] * 4 + [jax.ShapeDtypeStruct((2 * pairs, seq, seq), bf16)] + fixed
        + [jax.ShapeDtypeStruct((n, cap, width), bf16), jax.ShapeDtypeStruct((n // 2, cap, width), bf16)],
        scratch_shapes=[
            pltpu.VMEM((128, 2 * seq - 128), f32), pltpu.VMEM((seq, width), bf16), pltpu.VMEM((n, cap, width), bf16),
            pltpu.VMEM((n // 4 * cap, seq), bf16), pltpu.VMEM((seq, width), bf16), pltpu.VMEM((seq, 128), bf16), pltpu.VMEM((128, 128), f32),
            pltpu.VMEM((seq, 256), bf16), pltpu.VMEM((bias.shape[0], 512), f32), pltpu.VMEM((8, seq), jnp.int32), pltpu.VMEM((seq, n), bf16),
            dma((n,)), dma((n,)), dma((1,)), dma((2,)), dma((2,)),
        ],
        compiler_params=pltpu.CompilerParams(
            dimension_semantics=("arbitrary",), collective_id=3, has_side_effects=True, vmem_limit_bytes=56 << 20
        ),
        name="attn_fwd",
    )(tokens, cotangent, ids, bias, gains, wq, wk, wv, wo, wr)


def bwd_kernel(
    rows, merge, q_ref, k_ref, v_ref, o_ref, p_ref, wq_ref, wk_ref, wv_ref,
    tok_ref, cot_ref, after_ref, stat_ref, probs_ref, gains_ref, wr_ref, wo_ref, back_ref, gg_ref, rs_ref,
    ig_ref, small_out, sum_ref, rr_ref,
    ds_scr, qt_scr, dt_scr, near_scr, far_scr, xt_scr, d_scr, br_scr, dz_scr, nf_scr, ng_scr, rt_scr, gc_scr,
    acc, inbox, done, s_acc, s_inbox, s_done, send, recv, loc, r_send, r_recv, s_send, s_recv, out_sem,
):
    seq = q_ref.shape[0]
    blocks = seq // 128
    step = pl.program_id(0)
    width = tok_ref.shape[1]
    pairs = width // 128
    f32, bf16 = jnp.float32, jnp.bfloat16
    g1, g2 = gains_ref[0:1, :].astype(f32), gains_ref[1:2, :].astype(f32)
    chunks, total, depth, _ = acc.shape
    n = total // 2
    me, dp = lax.axis_index("expert"), lax.axis_index("dp")
    rounds = rounds_of(n)
    count = len(rounds)

    def place(bits):
        rank, devices = 0, []
        for i, bit in enumerate(bits):
            rank = rank + (dp if bit < 0 else (me >> bit) & 1) * (1 << i)
        for mask in range(1, 1 << len(bits)):
            flip = sum(1 << bit for i, bit in enumerate(bits) if bit >= 0 and mask >> i & 1)
            across = any(bit < 0 and mask >> i & 1 for i, bit in enumerate(bits))
            devices.append((1 - dp if across else dp, me ^ flip))
        return rank, devices

    ranks, spans, at, base, size, lead = [place(bits) for bits in rounds], [], 0, 0, total, 0
    for r, bits in enumerate(rounds):
        size //= 1 << len(bits)
        spans.append((at, at + ranks[r][0] * size, size, base, lead))
        at, base, lead = at + ranks[r][0] * size, base + ((1 << len(bits)) - 1) * size, lead + (1 << len(bits)) - 1
    links = lead

    def spread(lane, r):
        mine, box, _, ss, rs, _ = lane
        start, _, size, base, lead = spans[r]
        rank, devices = ranks[r]
        return [
            pltpu.make_async_remote_copy(
                mine.at[pl.ds(start + (rank ^ m) * size, size)], box.at[base + (m - 1) * size:base + m * size],
                ss.at[lead + m - 1], rs.at[lead + m - 1], device_id=devices[m - 1], device_id_type=MESH,
            )
            for m in range(1, len(devices) + 1)
        ]

    def fold(lane, r):
        mine, box, out, _, _, kind = lane
        _, keep, size, base, _ = spans[r]
        here = pl.ds(keep, size)
        part = mine[here].astype(jnp.float32)
        for m in range(len(ranks[r][1])):
            part = part + box[base + m * size:base + (m + 1) * size].astype(jnp.float32)
        (out if r == count - 1 else mine)[here] = part.astype(kind)

    def share(lane, r):
        _, _, out, ss, rs, _ = lane
        _, keep, size, _, lead = spans[r]
        piece = out.at[pl.ds(keep, size)]
        return [
            pltpu.make_async_remote_copy(
                piece, piece, ss.at[links + lead + m - 1], rs.at[links + lead + m - 1], device_id=dev, device_id_type=MESH
            )
            for m, dev in enumerate(ranks[r][1], 1)
        ]

    def event(lane, e):
        if 0 < e <= count:
            for c in spread(lane, e - 1):
                c.wait()
            fold(lane, e - 1)
        elif e > count:
            for c in share(lane, 2 * count - e):
                c.wait()
        if e < count:
            for c in spread(lane, e):
                c.start()
        elif e < 2 * count:
            for c in share(lane, 2 * count - 1 - e):
                c.start()

    last = 2 * count
    gaps = [3] + [6] * (count - 1)
    gaps = gaps + gaps[::-1]
    due = [sum(gaps[:e]) for e in range(last + 1)]

    def lane_of(c):
        return (acc.at[c], inbox.at[c], done.at[c], r_send.at[c], r_recv.at[c], jnp.bfloat16)

    tiny = (s_acc, s_inbox, s_done, s_send, s_recv, jnp.float32)

    def finish(c):
        return pltpu.make_async_copy(done.at[c], sum_ref.at[c], out_sem.at[c])

    def advance(slot):
        for e in range(last, 0, -1):
            if (slot - due[e] - 2) % 3:
                continue
            ready = step + (slot - due[e] - 2) // 3 + 1
            c = ready // merge - 1

            @pl.when((ready >= merge) & (ready % merge == 0))
            def _():
                event(lane_of(c), e)
                if e == last:
                    finish(c).start()

    def r_copy(o):
        return pltpu.make_async_remote_copy(
            rs_ref.at[o], rr_ref.at[me], send.at[o], recv.at[o], device_id=(dp, me ^ o), device_id_type=MESH
        )

    home = pltpu.make_async_copy(rs_ref.at[0], rr_ref.at[me], loc.at[0])
    experts, cap = rs_ref.shape[0], rs_ref.shape[1]

    @pl.when(step == 0)
    def _():
        others = [(dp, me ^ o) for o in range(1, n)]
        for bits, (_, devices) in zip(rounds, ranks):
            if -1 in bits:
                others += [dev for m, dev in enumerate(devices, 1) if m >> bits.index(-1) & 1]
        barrier = pltpu.get_barrier_semaphore()
        for dev in others:
            pl.semaphore_signal(barrier, inc=1, device_id=dev, device_id_type=MESH)
        pl.semaphore_wait(barrier, len(others))
        home.start()
        for o in range(1, n):
            r_copy(o).start()
        s_acc[...] = jnp.zeros_like(s_acc)
        rt_scr[...] = jnp.zeros_like(rt_scr)
        column = lax.broadcasted_iota(jnp.int32, (cap, 128), 1)

        def split(x, _):
            col = jnp.broadcast_to(gg_ref[x][:1, :], (128, 128)).T[:cap, :1]
            high = col.astype(bf16).astype(f32)
            mid = (col - high).astype(bf16).astype(f32)
            low = col - high - mid
            gc_scr[x] = jnp.where(column == 0, high, jnp.where(column == 1, mid, jnp.where(column == 2, low, 0.0))).astype(bf16)
            return 0

        lax.fori_loop(0, experts, split, 0)
        slots = experts * cap
        back = back_ref[...].reshape(slots, width)
        marks = gc_scr[...].reshape(slots, 128)
        where = lax.broadcasted_iota(jnp.int32, (rows, slots), 1)
        choice = lax.broadcasted_iota(jnp.int32, (rows, probs_ref.shape[1]), 1)
        for i in range(0, seq, rows):
            here = slice(i, i + rows)
            s1, s2, gate = stat_ref[here, 0:1], stat_ref[here, 1:2], stat_ref[here, 2:3]
            table = (stat_ref[here, 3:4].astype(jnp.int32) == where).astype(f32).astype(bf16)
            hot = (stat_ref[here, 4:5].astype(jnp.int32) == choice).astype(f32)
            triple = mm(table, marks)
            gate_grad = triple[:, 0:1] + triple[:, 1:2] + triple[:, 2:3]
            lg = ((gate_grad * gate) * (hot - probs_ref[here, :])).astype(bf16)
            rg = mm(table, back) + mm(lg, wr_ref[...])
            gdy = g2 * rg
            scaled = after_ref[here, :] * s2
            mean = jnp.sum(gdy * scaled, axis=-1, keepdims=True) * (1.0 / width)
            after = cot_ref[here, :].astype(f32) + s2 * (gdy - scaled * mean)
            routed = (scaled * g2).astype(bf16)
            rt_scr[1:, :] += lax.dot_general(lg, routed, TN, preferred_element_type=f32)
            rt_scr[:1, :] += jnp.sum(rg * scaled, axis=0, keepdims=True)
            ig_ref[here, :] = after
            low = after.astype(bf16)
            br_scr[here, :] = low
            d_scr[here, :] = mm(low, wo_ref[...], NT).astype(bf16)
            xt_scr[:, here] = (tok_ref[here, :].astype(f32) * s1 * g1).astype(bf16).T

    cols = pl.ds(pl.multiple_of(step * 128, 128), 128)
    lane = lax.broadcasted_iota(jnp.int32, (rows, 128), 1)
    sub = lax.broadcasted_iota(jnp.int32, (128, seq), 0)
    qt = q_ref[...].T
    dt = d_scr[:, cols].T
    zero = jnp.bfloat16(0)
    for hh in range(2):
        half = (sub >= 64) if hh else (sub < 64)
        qt_scr[:, hh * seq:(hh + 1) * seq] = jnp.where(half, qt, zero)
        dt_scr[:, hh * seq:(hh + 1) * seq] = jnp.where(half, dt, zero)
    for hh in range(2):
        own = (lane >= 64) if hh else (lane < 64)
        near_scr[...] = jnp.zeros_like(near_scr)
        far_scr[...] = jnp.zeros_like(far_scr)
        for i in range(seq // rows):
            r0 = i * rows
            d = jnp.where(own, d_scr[r0:r0 + rows, cols], zero)
            grown = mm(d, v_ref[...], NT)
            delta = jnp.sum(d.astype(jnp.float32) * o_ref[r0:r0 + rows, :].astype(jnp.float32), axis=-1, keepdims=True)
            ds = p_ref[hh, r0:r0 + rows, :].astype(jnp.float32) * (grown - delta)
            low = ds.astype(jnp.bfloat16)
            ds_scr[r0:r0 + rows, :] = low
            for a in range(rows // 128):
                bi = r0 // 128 + a
                strip = ds[a * 128:(a + 1) * 128]
                lo, hi = max(bi - 1, 0), min(bi + 2, blocks)
                near_scr[:, (lo - bi + 1) * 128:(hi - bi + 1) * 128] += strip[:, lo * 128:hi * 128]
                if lo > 0:
                    t = strip[:, :128]
                    for j in range(1, lo):
                        t = t + strip[:, j * 128:(j + 1) * 128]
                    far_scr[:, :128] += t
                if hi < blocks:
                    t = strip[:, hi * 128:(hi + 1) * 128]
                    for j in range(hi + 1, blocks):
                        t = t + strip[:, j * 128:(j + 1) * 128]
                    far_scr[:, 128:] += t
            dq = (0.125 * mm(low, k_ref[...])).astype(jnp.bfloat16)
            if hh == 0:
                dz_scr[r0:r0 + rows, :128] = dq
            else:
                dz_scr[r0:r0 + rows, :128] = jnp.where(own, dq, dz_scr[r0:r0 + rows, :128])
        part = mm(qt_scr[:, hh * seq:(hh + 1) * seq], ds_scr[...])
        dkt = part if hh == 0 else dkt + part
        a = near_scr[...]
        w = 128
        while w > 1:
            w //= 2
            a = a[:w] + pltpu.roll(a[w:], 512 - w, axis=1)
        nf_scr[pl.ds(2 * step + hh, 1), :512] = a
        nf_scr[pl.ds(2 * step + hh, 1), 512:] = jnp.sum(far_scr[...], axis=0, keepdims=True)
        if hh == 0:
            advance(0)
    advance(1)
    dz_scr[:, 128:256] = (0.125 * dkt).astype(jnp.bfloat16).T
    dvt = mm(dt_scr[...], p_ref[...].reshape(2 * seq, seq))
    dz_scr[:, 256:] = dvt.astype(jnp.bfloat16).T
    dz = dz_scr[...]
    dw = mm(xt_scr[...], dz).astype(jnp.bfloat16)
    go = lax.dot_general(o_ref[...], br_scr[...], TN, preferred_element_type=f32).astype(bf16)
    tiles = [dw[:, j * 128:(j + 1) * 128] for j in range(3)]
    tiles.append(jnp.concatenate([go[:, j * 128:(j + 1) * 128] for j in range(pairs)], axis=0))
    mine = step // merge
    per = width // depth
    for turn in range(merge):

        @pl.when(step % merge == turn)
        def _():
            for j in range(4):
                at = (turn * 4 + j) * per
                acc[mine, at:at + per] = tiles[j].reshape(per, depth, 128)

    w = jnp.concatenate([wq_ref[...], wk_ref[...], wv_ref[...]], axis=1)
    ng = mm(dz, w, NT)

    @pl.when(step == 0)
    def _():
        ng_scr[...] = ng

    @pl.when(step > 0)
    def _():
        ng_scr[...] += ng

    advance(2)

    @pl.when((step + 1) % merge == 0)
    def _():
        event(lane_of(mine), 0)

    @pl.when(step == pairs - 1)
    def _():
        gain = jnp.zeros((1, width), f32)
        for i in range(0, seq, rows):
            here = slice(i, i + rows)
            scaled = tok_ref[here, :].astype(f32) * stat_ref[here, 0:1]
            gain = gain + jnp.sum(ng_scr[here, :] * scaled, axis=0, keepdims=True)
        pieces = [gain] + [nf_scr[h:h + 1, :] for h in range(2 * pairs)] + [rt_scr[h:h + 1, :] for h in range(rt_scr.shape[0])]
        for i, piece in enumerate(pieces):
            for j in range(6):
                r = i * 6 + j
                s_acc[r // 8, r % 8:r % 8 + 1, :] = piece[:, j * 128:(j + 1) * 128]
        event(tiny, 0)
        left = []
        for c in range(chunks):
            ready = 3 * (c * merge + merge - 1) + 2
            left.append([e for e in range(1, last + 1) if ready + due[e] > 3 * pairs - 1])
        for turn in range(1, last + 1):
            event(tiny, turn)
            for c in range(chunks):
                if left[c]:
                    e = left[c].pop(0)
                    event(lane_of(c), e)
                    if e == last:
                        finish(c).start()
            if turn == 1:
                for i in range(0, seq, rows):
                    here = slice(i, i + rows)
                    s1 = stat_ref[here, 0:1]
                    scaled = tok_ref[here, :].astype(f32) * s1
                    gdy = g1 * ng_scr[here, :]
                    mean = jnp.sum(gdy * scaled, axis=-1, keepdims=True) * (1.0 / width)
                    ig_ref[here, :] += s1 * (gdy - scaled * mean)
        small_out[...] = s_done[...]
        for c in range(chunks):
            finish(c).wait()
        home.wait()
        for o in range(1, n):
            r_copy(o).wait()


def rounds_of(n):
    bits = n.bit_length() - 1
    if bits == 4:
        return [[0], [1, -1], [2, 3]]
    rest = list(range(1, bits)) + [-1]
    return [[0]] + [rest[i:i + 2] for i in range(0, len(rest), 2)]


def attn_bwd(q, k, v, o, p, wq, wk, wv, tokens, cotangent, after_attn, stats, probs, gains, wr, wo, back, gg, rs, rows=256):
    f32, bf16 = jnp.float32, jnp.bfloat16
    seq, width = q.shape
    pairs = width // 128
    n, cap = rs.shape[:2]
    total = 2 * n
    experts = probs.shape[1]
    links = sum((1 << len(bits)) - 1 for bits in rounds_of(n))
    merge = 1
    while 4 * width * merge % (total * 8):
        merge += 1
    chunks = pairs // merge
    depth = 4 * width * merge // total
    col = pl.BlockSpec((seq, 128), lambda h: (0, h))
    wcol = pl.BlockSpec((width, 128), lambda h: (0, h))

    def whole(shape):
        return pl.BlockSpec(shape, lambda h: (0,) * len(shape), pipeline_mode=pl.Buffered(1))

    hbm = pl.BlockSpec(memory_space=pl.ANY)
    dma = pltpu.SemaphoreType.DMA
    small = (total, 8, 128)
    store = pltpu.VMEM((chunks, total, depth, 128), bf16)
    small_store = pltpu.VMEM(small, f32)
    singles = (tokens, cotangent, after_attn, stats, probs, gains, wr, wo, back, gg)
    return pl.pallas_call(
        functools.partial(bwd_kernel, rows, merge),
        grid=(pairs,),
        in_specs=[col] * 4 + [pl.BlockSpec((2, seq, seq), lambda h: (h, 0, 0))] + [wcol] * 3 + [whole(x.shape) for x in singles] + [hbm],
        out_specs=[whole((seq, width)), whole(small), hbm, hbm],
        out_shape=[
            jax.ShapeDtypeStruct((seq, width), f32),
            jax.ShapeDtypeStruct(small, f32),
            jax.ShapeDtypeStruct((chunks, total, depth, 128), bf16),
            jax.ShapeDtypeStruct(rs.shape, rs.dtype),
        ],
        scratch_shapes=[
            pltpu.VMEM((seq, seq), bf16), pltpu.VMEM((128, 2 * seq), bf16), pltpu.VMEM((128, 2 * seq), bf16),
            pltpu.VMEM((128, 512), f32), pltpu.VMEM((128, 256), f32),
            pltpu.VMEM((width, seq), bf16), pltpu.VMEM((seq, width), bf16), pltpu.VMEM((seq, width), bf16), pltpu.VMEM((seq, 384), bf16),
            pltpu.VMEM((2 * pairs + 4, 768), f32), pltpu.VMEM((seq, width), f32), pltpu.VMEM((1 + experts, width), f32),
            pltpu.VMEM((n, cap, 128), bf16),
            store, store, store, small_store, small_store, small_store,
            dma((n,)), dma((n,)), dma((1,)),
            dma((chunks, 2 * links)), dma((chunks, 2 * links)), dma((2 * links,)), dma((2 * links,)), dma((chunks,)),
        ],
        compiler_params=pltpu.CompilerParams(
            dimension_semantics=("arbitrary",), collective_id=4, has_side_effects=True, vmem_limit_bytes=63 << 20
        ),
        name="attn_bwd",
    )(q, k, v, o, p, wq, wk, wv, *singles, rs)

def finish_kernel(sum_ref, q_ref, k_ref, v_ref, o_ref):
    for j, out in enumerate((q_ref, k_ref, v_ref)):
        out[...] = sum_ref[0, j].astype(jnp.float32)
    for i in range(sum_ref.shape[2] // 128):
        o_ref[:, i * 128:(i + 1) * 128] = sum_ref[0, 3, i * 128:(i + 1) * 128].astype(jnp.float32)


def finish_sums(sums):
    pairs, _, depth, _ = sums.shape
    col = pl.BlockSpec((depth, 128), lambda h: (0, h))
    return pl.pallas_call(
        finish_kernel,
        grid=(pairs,),
        in_specs=[pl.BlockSpec((1, 4, depth, 128), lambda h: (h, 0, 0, 0))],
        out_specs=[col] * 3 + [pl.BlockSpec((128, depth), lambda h: (h, 0))],
        out_shape=[jax.ShapeDtypeStruct((depth, 128 * pairs), jnp.float32)] * 4,
        compiler_params=pltpu.CompilerParams(dimension_semantics=("arbitrary",), vmem_limit_bytes=16 << 20),
        name="finish_sums",
    )(sums)


def bucket_of(offset):
    distance = np.abs(offset)
    far = 8 + sum((distance >= t).astype(np.int32) for t in thresholds)
    return np.where(distance < 8, distance, far) + 16 * (offset > 0)


def hot_of(offset):
    return (bucket_of(offset)[..., None] == np.arange(32)).astype(np.float32)


def local(dp_count, tokens, routes, cotangent, gain_first, w_query, w_key, w_value, w_output, bias_table, gain_second, w_router, expert_in, expert_out):
    f32, bf16 = jnp.float32, jnp.bfloat16
    seq, width = tokens.shape
    heads = bias_table.shape[1]
    experts = w_router.shape[1]
    cap = (5 * seq + 4 * experts - 1) // (4 * experts)
    capp = (cap + 15) // 16 * 16
    slots = experts * capp
    ids = routes[:, 0]
    gains = jnp.stack([gain_first, gain_second])
    router = w_router.T
    q, k, v, attended, probs_low, after_attn, router_probs, stats, rows, gates, cot_rows, cot_far = attn_fwd(
        tokens, cotangent, ids[None, :], bias_table.T, gains, w_query, w_key, w_value, w_output, router, cap, capp
    )
    back_tokens, gate_grads, produced, grad_in, grad_out = expert_pass(rows, gates, cot_rows, cot_far, expert_in[0], expert_out[0])
    input_grad, small, sums, returned = attn_bwd(
        q, k, v, attended, probs_low, w_query, w_key, w_value, tokens, cotangent, after_attn, stats, router_probs,
        gains, router, w_output, back_tokens, gate_grads, produced,
    )
    grad_query, grad_key, grad_value, grad_output = finish_sums(sums.reshape(heads // 2, 4, width, 128))
    small = small.reshape(-1)[:(2 + heads + experts) * 768].reshape(-1, 768)
    gain_one, strips, gain_two, router_rows = small[0], small[1:1 + heads], small[1 + heads], small[2 + heads:]
    grad_router = router_rows.T
    near_index = jnp.asarray(hot_of((np.arange(512) + 128) % 512 - 256))
    table_grad = jnp.einsum("hu,ub->bh", strips[:, :512], near_index, precision=lax.Precision.HIGHEST)
    left, right = jnp.sum(strips[:, 512:640], axis=1), jnp.sum(strips[:, 640:], axis=1)
    bucket = jnp.arange(32, dtype=jnp.int32)[:, None]
    table_grad = table_grad + jnp.where(bucket == 15, left[None, :], 0.0) + jnp.where(bucket == 31, right[None, :], 0.0)
    slot = stats[:, 3].astype(jnp.int32)
    table = (slot[:, None] == jnp.arange(slots, dtype=jnp.int32)[None, :]).astype(bf16)
    output = (after_attn + stats[:, 2:3] * mm(table, returned.reshape(slots, width))).astype(bf16)
    return (
        output,
        input_grad,
        gain_one,
        grad_query,
        grad_key,
        grad_value,
        grad_output,
        table_grad,
        gain_two,
        grad_router,
        grad_in[None].astype(f32),
        grad_out[None].astype(f32),
    )


def solution(mesh):
    split, whole = P(("dp", "expert"), None), P()
    in_specs = (split, split, split, whole, whole, whole, whole, whole, whole, whole, whole, P("expert", None, None), P("expert", None, None))
    out_specs = (split, split) + (whole,) * 8 + (P("expert", None, "dp"), P("expert", "dp", None))
    return jax.shard_map(
        functools.partial(local, mesh.shape["dp"]), mesh=mesh, in_specs=in_specs, out_specs=out_specs, check_vma=False
    )
```

```python
import functools

import jax
import jax.numpy as jnp
import numpy as np
from jax import lax
from jax.experimental import pallas as pl
from jax.experimental.pallas import tpu as pltpu
from jax.sharding import PartitionSpec as P

NT = (((1,), (1,)), ((), ()))
NN = (((1,), (0,)), ((), ()))
TN = (((0,), (0,)), ((), ()))


def mm(a, b, dims=NN):
    return lax.dot_general(a, b, dims, preferred_element_type=jnp.float32)


MESH = pl.DeviceIdType.MESH
gelu_a, gelu_b = 0.7978845608, 0.044715


def greet(axis_size):
    me, dp = lax.axis_index("expert"), lax.axis_index("dp")
    barrier = pltpu.get_barrier_semaphore()
    for step in range(1, axis_size):
        pl.semaphore_signal(barrier, inc=1, device_id=(dp, me ^ step), device_id_type=MESH)
    pl.semaphore_signal(barrier, inc=1, device_id=(1 - dp, me), device_id_type=MESH)
    return dp, me


def greeted(axis_size):
    pl.semaphore_wait(pltpu.get_barrier_semaphore(), axis_size)


def expert_kernel(
    groups, tile, early,
    xs_ref, gs_ref, cot_ref, far_ref, win_ref, wout_ref,
    back_ref, gg_ref, ret_ref, gin_ref, gout_ref,
    x_scr, c_scr, g_scr, w1, w2, a_scr, p_scr, ag_scr, pg_scr, r_scr, b_scr, e_scr, sq_scr, gin, gout,
    x_send, x_recv, g_send, g_recv, b_send, b_recv, e_send, e_recv, loc, wsem, csem, rsem, osem, f_send, f_recv,
):
    f32, bf16 = jnp.float32, jnp.bfloat16
    n, cap, width = xs_ref.shape
    ff = win_ref.shape[1]
    half = ff // 2
    size = n // groups
    rows = size * cap
    dp, me = greet(n)
    mine = pl.multiple_of(dp * half, 128)
    rest = pl.multiple_of((1 - dp) * half, 128)
    weights = [
        pltpu.make_async_copy(win_ref.at[:, pl.ds(mine, half)], w1.at[:, :half], wsem.at[0]),
        pltpu.make_async_copy(win_ref.at[:, pl.ds(rest, half)], w1.at[:, half:], wsem.at[1]),
        pltpu.make_async_copy(wout_ref.at[pl.ds(mine, half), :], w2.at[:half, :], wsem.at[2]),
        pltpu.make_async_copy(wout_ref.at[pl.ds(rest, half), :], w2.at[half:, :], wsem.at[3]),
    ]
    own = [
        pltpu.make_async_copy(xs_ref.at[me], x_scr.at[0, 0], loc.at[0]),
        pltpu.make_async_copy(gs_ref.at[me], g_scr.at[0, 0], loc.at[1]),
    ]
    cots = [
        pltpu.make_async_copy(cot_ref, c_scr.at[0], csem.at[0]),
        pltpu.make_async_copy(far_ref.at[:early], c_scr.at[1, :early], csem.at[1]),
    ]

    def remote(src, dst, send, recv, dev):
        return pltpu.make_async_remote_copy(src, dst, send, recv, device_id=dev, device_id_type=MESH)

    def x_copy(o):
        return remote(xs_ref.at[me ^ o], x_scr.at[0, o], x_send.at[o], x_recv.at[o], (dp, me ^ o))

    def g_copy(o):
        return remote(gs_ref.at[me ^ o], g_scr.at[0, o], g_send.at[o], g_recv.at[o], (dp, me ^ o))

    def b_copy(o):
        return remote(b_scr.at[o], back_ref.at[me], b_send.at[o], b_recv.at[o], (dp, me ^ o))

    def e_copy(o):
        return remote(e_scr.at[o], gg_ref.at[me], e_send.at[o], e_recv.at[o], (dp, me ^ o))

    def r_copy(o):
        return pltpu.make_async_copy(r_scr.at[o], ret_ref.at[o], rsem.at[o])

    over = (1 - dp, me)
    c_over = remote(cot_ref.at[early:], c_scr.at[1, early:], f_send.at[groups], f_recv.at[groups], over)
    g_over = remote(g_scr.at[0], g_scr.at[1], f_send.at[groups + 1], f_recv.at[groups + 1], over)

    def x_over(g):
        span = slice(g * size, (g + 1) * size)
        return remote(x_scr.at[0, span], x_scr.at[1, span], f_send.at[g], f_recv.at[g], over)

    def each(lo, hi, fn):
        if hi - lo <= 4:
            for o in range(lo, hi):
                fn(o)
        else:
            lax.fori_loop(lo, hi, lambda o, c: (fn(o), c)[1], 0)

    for c in own + cots + weights:
        c.start()
    greeted(n)
    each(1, n, lambda o: g_copy(o).start())
    each(1, n, lambda o: x_copy(o).start())
    c_over.start()
    sq_scr[...] = jnp.zeros_like(sq_scr)

    def gated(side, lo, hi):
        def one(o):
            col = jnp.broadcast_to(g_scr[side, o][:1, :], (128, 128)).T[:cap, :1]
            c_scr[side, o] = (c_scr[side, o].astype(f32) * col).astype(bf16)

        each(lo, hi, one)

    def hidden(x, ct, f):
        u = mm(x, w1[:, f:f + tile])
        back = mm(ct, w2[f:f + tile, :], NT)
        uu = u * u
        t = jnp.tanh(u * (gelu_a + (gelu_a * gelu_b) * uu))
        hp = 0.5 + 0.5 * t
        act = u * hp
        slope = hp + act * ((1.0 - t) * (gelu_a + (3.0 * gelu_a * gelu_b) * uu))
        return act.astype(bf16), (back * slope).astype(bf16)

    for g in range(groups):
        lo, hi = g * size, (g + 1) * size
        if g == 0:
            for c in own + cots[:1]:
                c.wait()
        each(max(lo, 1), hi, lambda o: g_copy(o).wait_recv())
        raw = c_scr[0, lo:hi].reshape(rows, width)
        gated(0, lo, hi)
        each(max(lo, 1), hi, lambda o: x_copy(o).wait_recv())
        x_over(g).start()
        if g == 0:
            for c in weights:
                c.wait()
        x = x_scr[0, lo:hi].reshape(rows, width)
        ct = c_scr[0, lo:hi].reshape(rows, width)
        span = slice(g * rows, (g + 1) * rows)
        for f in range(0, ff, tile):
            act, pre = hidden(x, ct, f)
            if f < half:
                a_scr[span, f:f + tile] = act
                p_scr[span, f:f + tile] = pre
            else:
                ag_scr[:, f - half:f - half + tile] = act
                pg_scr[:, f - half:f - half + tile] = pre
        back = mm(p_scr[span, :], w1[:, :half], NT) + mm(pg_scr[...], w1[:, half:], NT)
        b_scr[lo:hi] = back.astype(bf16).reshape(size, cap, width)
        each(max(lo, 1), hi, lambda o: b_copy(o).start())
        r = mm(a_scr[span, :], w2[:half, :]) + mm(ag_scr[...], w2[half:, :])
        r_scr[lo:hi] = r.astype(bf16).reshape(size, cap, width)
        dots = r * raw.astype(f32)
        part = dots[:, :128]
        for j in range(1, width // 128):
            part = part + dots[:, j * 128:(j + 1) * 128]
        part = part.reshape(size, cap, 128)
        for o in range(lo, hi):
            sq_scr[:cap, :] = part[o - lo]
            line = jnp.sum(sq_scr[...].T, axis=0, keepdims=True)
            e_scr[o] = jnp.broadcast_to(line, (8, 128))
        each(max(lo, 1), hi, lambda o: e_copy(o).start())
    g_over.start()
    each(0, n, lambda o: r_copy(o).start())
    own_back = [
        pltpu.make_async_copy(b_scr.at[0], back_ref.at[me], loc.at[0]),
        pltpu.make_async_copy(e_scr.at[0], gg_ref.at[me], loc.at[1]),
    ]
    for c in own_back:
        c.start()
    total = n * cap

    def gradients(side, first):
        x = x_scr[side].reshape(total, width)
        ct = c_scr[side].reshape(total, width)
        for f in range(0, half, tile):
            part = lax.dot_general(x, p_scr[:, f:f + tile], TN, preferred_element_type=f32)
            if first:
                gin[:, f:f + tile] = part
            else:
                w1[:, f:f + tile] = (gin[:, f:f + tile] + part).astype(bf16)
            part = lax.dot_general(a_scr[:, f:f + tile], ct, TN, preferred_element_type=f32)
            if first:
                gout[f:f + tile, :] = part
            else:
                w2[f:f + tile, :] = (gout[f:f + tile, :] + part).astype(bf16)
                for c in outs(f):
                    c.start()

    def outs(f):
        i = f // tile
        return [
            pltpu.make_async_copy(w1.at[:, f:f + tile], gin_ref.at[:, f:f + tile], osem.at[2 * i]),
            pltpu.make_async_copy(w2.at[f:f + tile, :], gout_ref.at[f:f + tile, :], osem.at[2 * i + 1]),
        ]

    gradients(0, True)
    cots[1].wait()
    c_over.wait()
    g_over.wait()
    gated(1, 0, n)
    for g in range(groups):
        lo, hi = g * size, (g + 1) * size
        x_over(g).wait()
        x = x_scr[1, lo:hi].reshape(rows, width)
        ct = c_scr[1, lo:hi].reshape(rows, width)
        for f in range(0, half, tile):
            act, pre = hidden(x, ct, f)
            a_scr[g * rows:(g + 1) * rows, f:f + tile] = act
            p_scr[g * rows:(g + 1) * rows, f:f + tile] = pre
    gradients(1, False)
    for f in range(0, half, tile):
        for c in outs(f):
            c.wait()
    for c in own_back:
        c.wait()
    each(0, n, lambda o: r_copy(o).wait())
    each(1, n, lambda o: x_copy(o).wait_send())
    each(1, n, lambda o: g_copy(o).wait_send())
    each(1, n, lambda o: b_copy(o).wait())
    each(1, n, lambda o: e_copy(o).wait())


def expert_pass(xs, gs, cot, far, w_in, w_out):
    f32, bf16 = jnp.float32, jnp.bfloat16
    n, cap, width = xs.shape
    ff = w_in.shape[1]
    half = ff // 2
    groups, tile = (4, 512) if n * cap <= 1280 else (8, 256)
    rows = n // groups * cap
    hbm = pl.BlockSpec(memory_space=pl.ANY)
    dma = pltpu.SemaphoreType.DMA
    flat = jax.ShapeDtypeStruct((n, cap, width), bf16)
    return pl.pallas_call(
        functools.partial(expert_kernel, groups, tile, n // 2),
        in_specs=[hbm] * 6,
        out_specs=[hbm] * 5,
        out_shape=[
            flat, jax.ShapeDtypeStruct((n, 8, 128), f32), flat,
            jax.ShapeDtypeStruct((width, half), bf16), jax.ShapeDtypeStruct((half, width), bf16),
        ],
        scratch_shapes=[
            pltpu.VMEM((2, n, cap, width), bf16), pltpu.VMEM((2, n, cap, width), bf16), pltpu.VMEM((2, n, 8, 128), f32),
            pltpu.VMEM((width, ff), bf16), pltpu.VMEM((ff, width), bf16),
            pltpu.VMEM((n * cap, half), bf16), pltpu.VMEM((n * cap, half), bf16),
            pltpu.VMEM((rows, half), bf16), pltpu.VMEM((rows, half), bf16),
            pltpu.VMEM((n, cap, width), bf16), pltpu.VMEM((n, cap, width), bf16), pltpu.VMEM((n, 8, 128), f32),
            pltpu.VMEM((128, 128), f32), pltpu.VMEM((width, half), f32), pltpu.VMEM((half, width), f32),
        ] + [dma((n,))] * 8 + [dma((2,)), dma((4,)), dma((2,)), dma((n,)), dma((2 * half // tile,)), dma((groups + 2,)), dma((groups + 2,))],
        compiler_params=pltpu.CompilerParams(collective_id=1, has_side_effects=True, vmem_limit_bytes=62 << 20),
        name="experts",
    )(xs, gs, cot, far, w_in, w_out)

eps_norm = 1e-06
thresholds = (12, 16, 23, 32, 46, 64, 91)


def fwd_kernel(
    rows, limit, tok_ref, cot_ref, ids_ref, bias_ref, gains_ref, wq_ref, wk_ref, wv_ref, wo_ref, wr_ref,
    q_ref, k_ref, v_ref, o_ref, p_ref, aa_ref, probs_ref, stat_ref, xs_ref, gs_ref, cr_ref, cp_ref,
    b_scr, xn_scr, cs_scr, t_scr, rt_scr, gm_scr, sq_scr, vx_scr, g_scr, row_scr, hot_scr, send, recv, loc, f_send, f_recv,
):
    f32, bf16 = jnp.float32, jnp.bfloat16
    seq, width = tok_ref.shape
    blocks = seq // 128
    step = pl.program_id(0)
    n, cap = cs_scr.shape[:2]
    me, dp = lax.axis_index("expert"), lax.axis_index("dp")
    quarter = n // 4
    g1, g2 = gains_ref[0:1, :].astype(f32), gains_ref[1:2, :].astype(f32)

    def remote(src, dst, ss, rs, dev):
        return pltpu.make_async_remote_copy(src, dst, ss, rs, device_id=dev, device_id_type=MESH)

    def c_copy(o):
        return remote(cs_scr.at[o], cr_ref.at[o], send.at[o], recv.at[o], (dp, me ^ o))

    def over(i):
        span = pl.ds(i * quarter, quarter)
        return remote(cr_ref.at[span], cp_ref.at[span], f_send.at[i], f_recv.at[i], (1 - dp, me))

    home = pltpu.make_async_copy(cs_scr.at[0], cr_ref.at[0], loc.at[0])

    def choose(first, pick):
        def one(i, _):
            ids = lax.broadcasted_iota(jnp.int32, (cap, seq), 0) + pick(first + i) * cap
            t_scr[pl.ds(pl.multiple_of(i * cap, 16), cap), :] = (ids == row_scr[0:1, :]).astype(f32).astype(bf16)
            return 0

        lax.fori_loop(0, quarter, one, 0)

    @pl.when(step == 0)
    def _():
        greet(n)
        spread = jnp.broadcast_to(ids_ref[...].astype(f32), (128, seq)).T
        choice = lax.broadcasted_iota(jnp.int32, (seq, n), 1)
        routes = spread[:, :1].astype(jnp.int32)
        hot_scr[...] = (routes == choice).astype(f32).astype(bf16)
        for i in range(0, seq, rows):
            here = slice(i, i + rows)
            later = lax.broadcasted_iota(jnp.int32, (rows, seq), 0) + i
            before = (later > lax.broadcasted_iota(jnp.int32, (rows, seq), 1)).astype(f32).astype(bf16)
            position = jnp.sum(mm(before, hot_scr[...]) * hot_scr[here, :].astype(f32), axis=-1, keepdims=True)
            ids = spread[here, :1]
            slot = jnp.where(position < limit, ids * cap + position, -1.0)
            row_scr[:, here] = jnp.broadcast_to(slot, (rows, 128)).T[:8, :].astype(jnp.int32)
            slim = lax.broadcasted_iota(jnp.int32, (rows, 8), 1)
            stat_ref[here, :] = jnp.where(slim == 3, slot, ids)
        greeted(n)
        for g in range(4):
            lo = g * quarter
            choose(lo, lambda o: me ^ o)
            cs_scr[lo:lo + quarter] = mm(t_scr[...], cot_ref[...]).astype(bf16).reshape(quarter, cap, width)
            if g == 0:
                home.start()
            for o in range(max(lo, 1), lo + quarter):
                c_copy(o).start()
        for i in range(0, seq, rows):
            here = slice(i, i + rows)
            x = tok_ref[here, :].astype(f32)
            s1 = lax.rsqrt(jnp.mean(x * x, axis=-1, keepdims=True) + eps_norm)
            slim = lax.broadcasted_iota(jnp.int32, (rows, 8), 1)
            stat_ref[here, :] = jnp.where(slim == 0, s1, stat_ref[here, :])
            xn_scr[here, :] = (x * s1 * g1).astype(bf16)
            aa_ref[here, :] = x
        offset = lax.broadcasted_iota(jnp.int32, (32, 512), 1) - 256
        distance = jnp.abs(offset)
        far = jnp.full(offset.shape, 8, jnp.int32)
        for t in thresholds:
            far = far + (distance >= t).astype(jnp.int32)
        bucket = jnp.where(distance < 8, distance, far) + 16 * (offset > 0).astype(jnp.int32)
        pick = (bucket == lax.broadcasted_iota(jnp.int32, (32, 512), 0)).astype(f32).astype(bf16)
        g_scr[...] = mm(bias_ref[...], pick)
        vx_scr[:, 128:] = jnp.ones((seq, 128), bf16)

    for i in range(2):

        @pl.when(step == 2 + 2 * i)
        def _():
            if i == 0:
                home.wait()
            for o in range(max(1, i * quarter), (i + 1) * quarter):
                c_copy(o).wait_recv()
            over(i).start()

    for w_ref, out in ((wq_ref, q_ref), (wk_ref, k_ref), (wv_ref, v_ref)):
        out[...] = mm(xn_scr[...], w_ref[...]).astype(bf16)
    vx_scr[:, :128] = v_ref[...]
    lane = lax.broadcasted_iota(jnp.int32, (rows, 128), 1)
    for hh in range(2):
        own = (lane >= 64) if hh else (lane < 64)
        g = g_scr[pl.ds(2 * step + hh, 1), :]
        near = pltpu.roll(jnp.broadcast_to(g, (128, 512)), 384, axis=1, stride=1, stride_axis=0)
        mid = (blocks - 2) * 128
        b_scr[:, :mid] = jnp.broadcast_to(g[:, :1], (128, mid))
        b_scr[:, mid:mid + 384] = near[:, :384]
        b_scr[:, mid + 384:] = jnp.broadcast_to(g[:, 511:], (128, b_scr.shape[1] - mid - 384))
        for i in range(seq // rows):
            r0 = i * rows
            q = q_ref[r0:r0 + rows, :]
            qm = jnp.where(own, q * jnp.bfloat16(0.125), jnp.bfloat16(0))
            s = mm(qm, k_ref[...], NT)
            parts = []
            for a in range(rows // 128):
                c0 = (blocks - 1 - (r0 // 128 + a)) * 128
                parts.append(s[a * 128:(a + 1) * 128] + b_scr[:, c0:c0 + seq])
            s = jnp.concatenate(parts, 0) if len(parts) > 1 else parts[0]
            m = jnp.max(s, axis=-1, keepdims=True)
            e = jnp.exp(s - m)
            raw = mm(e.astype(bf16), vx_scr[...])
            inv = 1.0 / raw[:, 128:129]
            p_ref[hh, r0:r0 + rows, :] = (e * inv).astype(bf16)
            o = (raw[:, :128] * inv).astype(bf16)
            if hh == 0:
                o_ref[r0:r0 + rows, :] = o
            else:
                o = jnp.where(own, o, o_ref[r0:r0 + rows, :])
                o_ref[r0:r0 + rows, :] = o
                aa_ref[r0:r0 + rows, :] += mm(o, wo_ref[...])

    @pl.when(step == pl.num_programs(0) - 1)
    def _():
        slim = lax.broadcasted_iota(jnp.int32, (rows, 8), 1)
        wide = lax.broadcasted_iota(jnp.int32, (rows, 128), 1)
        for i in range(0, seq, rows):
            here = slice(i, i + rows)
            aa = aa_ref[here, :]
            s2 = lax.rsqrt(jnp.mean(aa * aa, axis=-1, keepdims=True) + eps_norm)
            routed = (aa * s2 * g2).astype(bf16)
            rt_scr[here, :] = routed
            logits = mm(routed, wr_ref[...], NT)
            e = jnp.exp(logits - jnp.max(logits, axis=-1, keepdims=True))
            probs = e / jnp.sum(e, axis=-1, keepdims=True)
            probs_ref[here, :] = probs
            gate = jnp.sum(probs * hot_scr[here, :].astype(f32), axis=-1, keepdims=True)
            stat_ref[here, :] = jnp.where(slim == 1, s2, jnp.where(slim == 2, gate, stat_ref[here, :]))
            high = gate.astype(bf16).astype(f32)
            middle = (gate - high).astype(bf16).astype(f32)
            low = gate - high - middle
            gm_scr[here, :] = jnp.where(wide == 0, high, jnp.where(wide == 1, middle, jnp.where(wide == 2, low, 0.0))).astype(bf16)
        sq_scr[...] = jnp.zeros_like(sq_scr)
        for g in range(4):
            lo = g * quarter
            choose(lo, lambda x: x)
            xs_ref[lo:lo + quarter] = mm(t_scr[...], rt_scr[...]).astype(bf16).reshape(quarter, cap, width)
            gates = mm(t_scr[...], gm_scr[...]).reshape(quarter, cap, 128)
            for x in range(quarter):
                sq_scr[:cap, :] = gates[x]
                gs_ref[lo + x] = jnp.broadcast_to(jnp.sum(sq_scr[...].T, axis=0, keepdims=True), (8, 128))
        for o in range(1, n):
            c_copy(o).wait_send()
        for o in range(n // 2, n):
            c_copy(o).wait_recv()
        for i in range(2):
            over(i).wait()


def attn_fwd(tokens, cotangent, ids, bias, gains, wq, wk, wv, wo, wr, limit, cap, rows=256):
    f32, bf16 = jnp.float32, jnp.bfloat16
    seq, width = tokens.shape
    pairs = width // 128
    n = wr.shape[0]
    col = pl.BlockSpec((seq, 128), lambda h: (0, h))
    wcol = pl.BlockSpec((width, 128), lambda h: (0, h))

    def whole(shape):
        return pl.BlockSpec(shape, lambda h: (0,) * len(shape), pipeline_mode=pl.Buffered(1))

    hbm = pl.BlockSpec(memory_space=pl.ANY)
    dma = pltpu.SemaphoreType.DMA
    tall = jax.ShapeDtypeStruct((seq, width), bf16)
    fixed = [
        jax.ShapeDtypeStruct((seq, width), f32), jax.ShapeDtypeStruct((seq, n), f32), jax.ShapeDtypeStruct((seq, 8), f32),
        jax.ShapeDtypeStruct((n, cap, width), bf16), jax.ShapeDtypeStruct((n, 8, 128), f32),
    ]
    return pl.pallas_call(
        functools.partial(fwd_kernel, rows, limit),
        grid=(pairs,),
        in_specs=[whole(x.shape) for x in (tokens, cotangent, ids, bias, gains)]
        + [wcol] * 3 + [pl.BlockSpec((128, width), lambda h: (h, 0)), whole(wr.shape)],
        out_specs=[col] * 4 + [pl.BlockSpec((2, seq, seq), lambda h: (h, 0, 0))] + [whole(x.shape) for x in fixed] + [hbm, hbm],
        out_shape=[tall] * 4 + [jax.ShapeDtypeStruct((2 * pairs, seq, seq), bf16)] + fixed
        + [jax.ShapeDtypeStruct((n, cap, width), bf16), jax.ShapeDtypeStruct((n // 2, cap, width), bf16)],
        scratch_shapes=[
            pltpu.VMEM((128, 2 * seq - 128), f32), pltpu.VMEM((seq, width), bf16), pltpu.VMEM((n, cap, width), bf16),
            pltpu.VMEM((n // 4 * cap, seq), bf16), pltpu.VMEM((seq, width), bf16), pltpu.VMEM((seq, 128), bf16), pltpu.VMEM((128, 128), f32),
            pltpu.VMEM((seq, 256), bf16), pltpu.VMEM((bias.shape[0], 512), f32), pltpu.VMEM((8, seq), jnp.int32), pltpu.VMEM((seq, n), bf16),
            dma((n,)), dma((n,)), dma((1,)), dma((2,)), dma((2,)),
        ],
        compiler_params=pltpu.CompilerParams(
            dimension_semantics=("arbitrary",), collective_id=3, has_side_effects=True, vmem_limit_bytes=56 << 20
        ),
        name="attn_fwd",
    )(tokens, cotangent, ids, bias, gains, wq, wk, wv, wo, wr)


def bwd_kernel(
    rows, merge, q_ref, k_ref, v_ref, o_ref, p_ref, wq_ref, wk_ref, wv_ref,
    tok_ref, cot_ref, after_ref, stat_ref, probs_ref, gains_ref, wr_ref, wo_ref, back_ref, gg_ref, rs_ref,
    ig_ref, small_out, sum_ref, rr_ref,
    ds_scr, qt_scr, dt_scr, near_scr, far_scr, xt_scr, d_scr, br_scr, dz_scr, nf_scr, ng_scr, rt_scr, gc_scr,
    acc, inbox, done, s_acc, s_inbox, s_done, send, recv, loc, r_send, r_recv, s_send, s_recv, out_sem,
):
    seq = q_ref.shape[0]
    blocks = seq // 128
    step = pl.program_id(0)
    width = tok_ref.shape[1]
    pairs = width // 128
    f32, bf16 = jnp.float32, jnp.bfloat16
    g1, g2 = gains_ref[0:1, :].astype(f32), gains_ref[1:2, :].astype(f32)
    chunks, total, depth, _ = acc.shape
    n = total // 2
    me, dp = lax.axis_index("expert"), lax.axis_index("dp")
    rounds = rounds_of(n)
    count = len(rounds)

    def place(bits):
        rank, devices = 0, []
        for i, bit in enumerate(bits):
            rank = rank + (dp if bit < 0 else (me >> bit) & 1) * (1 << i)
        for mask in range(1, 1 << len(bits)):
            flip = sum(1 << bit for i, bit in enumerate(bits) if bit >= 0 and mask >> i & 1)
            across = any(bit < 0 and mask >> i & 1 for i, bit in enumerate(bits))
            devices.append((1 - dp if across else dp, me ^ flip))
        return rank, devices

    ranks, spans, at, base, size, lead = [place(bits) for bits in rounds], [], 0, 0, total, 0
    for r, bits in enumerate(rounds):
        size //= 1 << len(bits)
        spans.append((at, at + ranks[r][0] * size, size, base, lead))
        at, base, lead = at + ranks[r][0] * size, base + ((1 << len(bits)) - 1) * size, lead + (1 << len(bits)) - 1
    links = lead

    def spread(lane, r):
        mine, box, _, ss, rs, _ = lane
        start, _, size, base, lead = spans[r]
        rank, devices = ranks[r]
        return [
            pltpu.make_async_remote_copy(
                mine.at[pl.ds(start + (rank ^ m) * size, size)], box.at[base + (m - 1) * size:base + m * size],
                ss.at[lead + m - 1], rs.at[lead + m - 1], device_id=devices[m - 1], device_id_type=MESH,
            )
            for m in range(1, len(devices) + 1)
        ]

    def fold(lane, r):
        mine, box, out, _, _, kind = lane
        _, keep, size, base, _ = spans[r]
        here = pl.ds(keep, size)
        part = mine[here].astype(jnp.float32)
        for m in range(len(ranks[r][1])):
            part = part + box[base + m * size:base + (m + 1) * size].astype(jnp.float32)
        (out if r == count - 1 else mine)[here] = part.astype(kind)

    def share(lane, r):
        _, _, out, ss, rs, _ = lane
        _, keep, size, _, lead = spans[r]
        piece = out.at[pl.ds(keep, size)]
        return [
            pltpu.make_async_remote_copy(
                piece, piece, ss.at[links + lead + m - 1], rs.at[links + lead + m - 1], device_id=dev, device_id_type=MESH
            )
            for m, dev in enumerate(ranks[r][1], 1)
        ]

    def event(lane, e):
        if 0 < e <= count:
            for c in spread(lane, e - 1):
                c.wait()
            fold(lane, e - 1)
        elif e > count:
            for c in share(lane, 2 * count - e):
                c.wait()
        if e < count:
            for c in spread(lane, e):
                c.start()
        elif e < 2 * count:
            for c in share(lane, 2 * count - 1 - e):
                c.start()

    last = 2 * count
    gaps = [3] + [6] * (count - 1)
    gaps = gaps + gaps[::-1]
    due = [sum(gaps[:e]) for e in range(last + 1)]

    def lane_of(c):
        return (acc.at[c], inbox.at[c], done.at[c], r_send.at[c], r_recv.at[c], jnp.bfloat16)

    tiny = (s_acc, s_inbox, s_done, s_send, s_recv, jnp.float32)

    def finish(c):
        return pltpu.make_async_copy(done.at[c], sum_ref.at[c], out_sem.at[c])

    def advance(slot):
        for e in range(last, 0, -1):
            if (slot - due[e] - 2) % 3:
                continue
            ready = step + (slot - due[e] - 2) // 3 + 1
            c = ready // merge - 1

            @pl.when((ready >= merge) & (ready % merge == 0))
            def _():
                event(lane_of(c), e)
                if e == last:
                    finish(c).start()

    def r_copy(o):
        return pltpu.make_async_remote_copy(
            rs_ref.at[o], rr_ref.at[me], send.at[o], recv.at[o], device_id=(dp, me ^ o), device_id_type=MESH
        )

    home = pltpu.make_async_copy(rs_ref.at[0], rr_ref.at[me], loc.at[0])
    experts, cap = rs_ref.shape[0], rs_ref.shape[1]

    @pl.when(step == 0)
    def _():
        others = [(dp, me ^ o) for o in range(1, n)]
        for bits, (_, devices) in zip(rounds, ranks):
            if -1 in bits:
                others += [dev for m, dev in enumerate(devices, 1) if m >> bits.index(-1) & 1]
        barrier = pltpu.get_barrier_semaphore()
        for dev in others:
            pl.semaphore_signal(barrier, inc=1, device_id=dev, device_id_type=MESH)
        s_acc[...] = jnp.zeros_like(s_acc)
        rt_scr[...] = jnp.zeros_like(rt_scr)
        column = lax.broadcasted_iota(jnp.int32, (cap, 128), 1)

        def split(x, _):
            col = jnp.broadcast_to(gg_ref[x][:1, :], (128, 128)).T[:cap, :1]
            high = col.astype(bf16).astype(f32)
            mid = (col - high).astype(bf16).astype(f32)
            low = col - high - mid
            gc_scr[x] = jnp.where(column == 0, high, jnp.where(column == 1, mid, jnp.where(column == 2, low, 0.0))).astype(bf16)
            return 0

        lax.fori_loop(0, experts, split, 0)
        slots = experts * cap
        back = back_ref[...].reshape(slots, width)
        marks = gc_scr[...].reshape(slots, 128)
        where = lax.broadcasted_iota(jnp.int32, (rows, slots), 1)
        choice = lax.broadcasted_iota(jnp.int32, (rows, probs_ref.shape[1]), 1)
        for i in range(0, seq, rows):
            if i == seq // 4:
                pl.semaphore_wait(barrier, len(others))
                home.start()
                for o in range(1, n):
                    r_copy(o).start()
            here = slice(i, i + rows)
            s1, s2, gate = stat_ref[here, 0:1], stat_ref[here, 1:2], stat_ref[here, 2:3]
            table = (stat_ref[here, 3:4].astype(jnp.int32) == where).astype(f32).astype(bf16)
            hot = (stat_ref[here, 4:5].astype(jnp.int32) == choice).astype(f32)
            triple = mm(table, marks)
            gate_grad = triple[:, 0:1] + triple[:, 1:2] + triple[:, 2:3]
            lg = ((gate_grad * gate) * (hot - probs_ref[here, :])).astype(bf16)
            rg = mm(table, back) + mm(lg, wr_ref[...])
            gdy = g2 * rg
            scaled = after_ref[here, :] * s2
            mean = jnp.sum(gdy * scaled, axis=-1, keepdims=True) * (1.0 / width)
            after = cot_ref[here, :].astype(f32) + s2 * (gdy - scaled * mean)
            routed = (scaled * g2).astype(bf16)
            rt_scr[1:, :] += lax.dot_general(lg, routed, TN, preferred_element_type=f32)
            rt_scr[:1, :] += jnp.sum(rg * scaled, axis=0, keepdims=True)
            ig_ref[here, :] = after
            low = after.astype(bf16)
            br_scr[here, :] = low
            d_scr[here, :] = mm(low, wo_ref[...], NT).astype(bf16)
            xt_scr[:, here] = (tok_ref[here, :].astype(f32) * s1 * g1).astype(bf16).T

    cols = pl.ds(pl.multiple_of(step * 128, 128), 128)
    lane = lax.broadcasted_iota(jnp.int32, (rows, 128), 1)
    sub = lax.broadcasted_iota(jnp.int32, (128, seq), 0)
    qt = q_ref[...].T
    dt = d_scr[:, cols].T
    zero = jnp.bfloat16(0)
    for hh in range(2):
        half = (sub >= 64) if hh else (sub < 64)
        qt_scr[:, hh * seq:(hh + 1) * seq] = jnp.where(half, qt, zero)
        dt_scr[:, hh * seq:(hh + 1) * seq] = jnp.where(half, dt, zero)
    for hh in range(2):
        own = (lane >= 64) if hh else (lane < 64)
        near_scr[...] = jnp.zeros_like(near_scr)
        far_scr[...] = jnp.zeros_like(far_scr)
        for i in range(seq // rows):
            r0 = i * rows
            d = jnp.where(own, d_scr[r0:r0 + rows, cols], zero)
            grown = mm(d, v_ref[...], NT)
            delta = jnp.sum(d.astype(jnp.float32) * o_ref[r0:r0 + rows, :].astype(jnp.float32), axis=-1, keepdims=True)
            ds = p_ref[hh, r0:r0 + rows, :].astype(jnp.float32) * (grown - delta)
            low = ds.astype(jnp.bfloat16)
            ds_scr[r0:r0 + rows, :] = low
            for a in range(rows // 128):
                bi = r0 // 128 + a
                strip = ds[a * 128:(a + 1) * 128]
                lo, hi = max(bi - 1, 0), min(bi + 2, blocks)
                near_scr[:, (lo - bi + 1) * 128:(hi - bi + 1) * 128] += strip[:, lo * 128:hi * 128]
                if lo > 0:
                    t = strip[:, :128]
                    for j in range(1, lo):
                        t = t + strip[:, j * 128:(j + 1) * 128]
                    far_scr[:, :128] += t
                if hi < blocks:
                    t = strip[:, hi * 128:(hi + 1) * 128]
                    for j in range(hi + 1, blocks):
                        t = t + strip[:, j * 128:(j + 1) * 128]
                    far_scr[:, 128:] += t
            dq = (0.125 * mm(low, k_ref[...])).astype(jnp.bfloat16)
            if hh == 0:
                dz_scr[r0:r0 + rows, :128] = dq
            else:
                dz_scr[r0:r0 + rows, :128] = jnp.where(own, dq, dz_scr[r0:r0 + rows, :128])
        part = mm(qt_scr[:, hh * seq:(hh + 1) * seq], ds_scr[...])
        dkt = part if hh == 0 else dkt + part
        a = near_scr[...]
        w = 128
        while w > 1:
            w //= 2
            a = a[:w] + pltpu.roll(a[w:], 512 - w, axis=1)
        nf_scr[pl.ds(2 * step + hh, 1), :512] = a
        nf_scr[pl.ds(2 * step + hh, 1), 512:] = jnp.sum(far_scr[...], axis=0, keepdims=True)
        if hh == 0:
            advance(0)
    advance(1)
    dz_scr[:, 128:256] = (0.125 * dkt).astype(jnp.bfloat16).T
    dvt = mm(dt_scr[...], p_ref[...].reshape(2 * seq, seq))
    dz_scr[:, 256:] = dvt.astype(jnp.bfloat16).T
    dz = dz_scr[...]
    dw = mm(xt_scr[...], dz).astype(jnp.bfloat16)
    go = lax.dot_general(o_ref[...], br_scr[...], TN, preferred_element_type=f32).astype(bf16)
    tiles = [dw[:, j * 128:(j + 1) * 128] for j in range(3)]
    tiles.append(jnp.concatenate([go[:, j * 128:(j + 1) * 128] for j in range(pairs)], axis=0))
    mine = step // merge
    per = width // depth
    for turn in range(merge):

        @pl.when(step % merge == turn)
        def _():
            for j in range(4):
                at = (turn * 4 + j) * per
                acc[mine, at:at + per] = tiles[j].reshape(per, depth, 128)

    w = jnp.concatenate([wq_ref[...], wk_ref[...], wv_ref[...]], axis=1)
    ng = mm(dz, w, NT)

    @pl.when(step == 0)
    def _():
        ng_scr[...] = ng

    @pl.when(step > 0)
    def _():
        ng_scr[...] += ng

    advance(2)

    @pl.when((step + 1) % merge == 0)
    def _():
        event(lane_of(mine), 0)

    @pl.when(step == pairs - 1)
    def _():
        gain = jnp.zeros((1, width), f32)
        for i in range(0, seq, rows):
            here = slice(i, i + rows)
            scaled = tok_ref[here, :].astype(f32) * stat_ref[here, 0:1]
            gain = gain + jnp.sum(ng_scr[here, :] * scaled, axis=0, keepdims=True)
        pieces = [gain] + [nf_scr[h:h + 1, :] for h in range(2 * pairs)] + [rt_scr[h:h + 1, :] for h in range(rt_scr.shape[0])]
        for i, piece in enumerate(pieces):
            for j in range(6):
                r = i * 6 + j
                s_acc[r // 8, r % 8:r % 8 + 1, :] = piece[:, j * 128:(j + 1) * 128]
        event(tiny, 0)
        left = []
        for c in range(chunks):
            ready = 3 * (c * merge + merge - 1) + 2
            left.append([e for e in range(1, last + 1) if ready + due[e] > 3 * pairs - 1])
        for turn in range(1, last + 1):
            event(tiny, turn)
            for c in range(chunks):
                if left[c]:
                    e = left[c].pop(0)
                    event(lane_of(c), e)
                    if e == last:
                        finish(c).start()
            if turn == 1:
                for i in range(0, seq, rows):
                    here = slice(i, i + rows)
                    s1 = stat_ref[here, 0:1]
                    scaled = tok_ref[here, :].astype(f32) * s1
                    gdy = g1 * ng_scr[here, :]
                    mean = jnp.sum(gdy * scaled, axis=-1, keepdims=True) * (1.0 / width)
                    ig_ref[here, :] += s1 * (gdy - scaled * mean)
        small_out[...] = s_done[...]
        for c in range(chunks):
            finish(c).wait()
        home.wait()
        for o in range(1, n):
            r_copy(o).wait()


def rounds_of(n):
    bits = n.bit_length() - 1
    if bits == 4:
        return [[0], [1, -1], [2, 3]]
    rest = list(range(1, bits)) + [-1]
    return [[0]] + [rest[i:i + 2] for i in range(0, len(rest), 2)]


def attn_bwd(q, k, v, o, p, wq, wk, wv, tokens, cotangent, after_attn, stats, probs, gains, wr, wo, back, gg, rs, rows=256):
    f32, bf16 = jnp.float32, jnp.bfloat16
    seq, width = q.shape
    pairs = width // 128
    n, cap = rs.shape[:2]
    total = 2 * n
    experts = probs.shape[1]
    links = sum((1 << len(bits)) - 1 for bits in rounds_of(n))
    merge = 1
    while 4 * width * merge % (total * 8):
        merge += 1
    chunks = pairs // merge
    depth = 4 * width * merge // total
    col = pl.BlockSpec((seq, 128), lambda h: (0, h))
    wcol = pl.BlockSpec((width, 128), lambda h: (0, h))

    def whole(shape):
        return pl.BlockSpec(shape, lambda h: (0,) * len(shape), pipeline_mode=pl.Buffered(1))

    hbm = pl.BlockSpec(memory_space=pl.ANY)
    dma = pltpu.SemaphoreType.DMA
    small = (total, 8, 128)
    store = pltpu.VMEM((chunks, total, depth, 128), bf16)
    small_store = pltpu.VMEM(small, f32)
    singles = (tokens, cotangent, after_attn, stats, probs, gains, wr, wo, back, gg)
    return pl.pallas_call(
        functools.partial(bwd_kernel, rows, merge),
        grid=(pairs,),
        in_specs=[col] * 4 + [pl.BlockSpec((2, seq, seq), lambda h: (h, 0, 0))] + [wcol] * 3 + [whole(x.shape) for x in singles] + [hbm],
        out_specs=[whole((seq, width)), whole(small), hbm, hbm],
        out_shape=[
            jax.ShapeDtypeStruct((seq, width), f32),
            jax.ShapeDtypeStruct(small, f32),
            jax.ShapeDtypeStruct((chunks, total, depth, 128), bf16),
            jax.ShapeDtypeStruct(rs.shape, rs.dtype),
        ],
        scratch_shapes=[
            pltpu.VMEM((seq, seq), bf16), pltpu.VMEM((128, 2 * seq), bf16), pltpu.VMEM((128, 2 * seq), bf16),
            pltpu.VMEM((128, 512), f32), pltpu.VMEM((128, 256), f32),
            pltpu.VMEM((width, seq), bf16), pltpu.VMEM((seq, width), bf16), pltpu.VMEM((seq, width), bf16), pltpu.VMEM((seq, 384), bf16),
            pltpu.VMEM((2 * pairs + 4, 768), f32), pltpu.VMEM((seq, width), f32), pltpu.VMEM((1 + experts, width), f32),
            pltpu.VMEM((n, cap, 128), bf16),
            store, store, store, small_store, small_store, small_store,
            dma((n,)), dma((n,)), dma((1,)),
            dma((chunks, 2 * links)), dma((chunks, 2 * links)), dma((2 * links,)), dma((2 * links,)), dma((chunks,)),
        ],
        compiler_params=pltpu.CompilerParams(
            dimension_semantics=("arbitrary",), collective_id=4, has_side_effects=True, vmem_limit_bytes=63 << 20
        ),
        name="attn_bwd",
    )(q, k, v, o, p, wq, wk, wv, *singles, rs)

def finish_kernel(sum_ref, q_ref, k_ref, v_ref, o_ref):
    for j, out in enumerate((q_ref, k_ref, v_ref)):
        out[...] = sum_ref[0, j].astype(jnp.float32)
    for i in range(sum_ref.shape[2] // 128):
        o_ref[:, i * 128:(i + 1) * 128] = sum_ref[0, 3, i * 128:(i + 1) * 128].astype(jnp.float32)


def finish_sums(sums):
    pairs, _, depth, _ = sums.shape
    col = pl.BlockSpec((depth, 128), lambda h: (0, h))
    return pl.pallas_call(
        finish_kernel,
        grid=(pairs,),
        in_specs=[pl.BlockSpec((1, 4, depth, 128), lambda h: (h, 0, 0, 0))],
        out_specs=[col] * 3 + [pl.BlockSpec((128, depth), lambda h: (h, 0))],
        out_shape=[jax.ShapeDtypeStruct((depth, 128 * pairs), jnp.float32)] * 4,
        compiler_params=pltpu.CompilerParams(dimension_semantics=("arbitrary",), vmem_limit_bytes=16 << 20),
        name="finish_sums",
    )(sums)


def bucket_of(offset):
    distance = np.abs(offset)
    far = 8 + sum((distance >= t).astype(np.int32) for t in thresholds)
    return np.where(distance < 8, distance, far) + 16 * (offset > 0)


def hot_of(offset):
    return (bucket_of(offset)[..., None] == np.arange(32)).astype(np.float32)


def local(dp_count, tokens, routes, cotangent, gain_first, w_query, w_key, w_value, w_output, bias_table, gain_second, w_router, expert_in, expert_out):
    f32, bf16 = jnp.float32, jnp.bfloat16
    seq, width = tokens.shape
    heads = bias_table.shape[1]
    experts = w_router.shape[1]
    cap = (5 * seq + 4 * experts - 1) // (4 * experts)
    capp = (cap + 15) // 16 * 16
    slots = experts * capp
    ids = routes[:, 0]
    first = lax.broadcasted_iota(jnp.int32, (2, width), 0) == 0
    gains = jnp.where(first, gain_first[None, :], gain_second[None, :])
    router = w_router.T
    q, k, v, attended, probs_low, after_attn, router_probs, stats, rows, gates, cot_rows, cot_far = attn_fwd(
        tokens, cotangent, ids[None, :], bias_table.T, gains, w_query, w_key, w_value, w_output, router, cap, capp
    )
    back_tokens, gate_grads, produced, grad_in, grad_out = expert_pass(rows, gates, cot_rows, cot_far, expert_in[0], expert_out[0])
    input_grad, small, sums, returned = attn_bwd(
        q, k, v, attended, probs_low, w_query, w_key, w_value, tokens, cotangent, after_attn, stats, router_probs,
        gains, router, w_output, back_tokens, gate_grads, produced,
    )
    grad_query, grad_key, grad_value, grad_output = finish_sums(sums.reshape(heads // 2, 4, width, 128))
    small = small.reshape(-1)[:(2 + heads + experts) * 768].reshape(-1, 768)
    gain_one, strips, gain_two, router_rows = small[0], small[1:1 + heads], small[1 + heads], small[2 + heads:]
    grad_router = router_rows.T
    near_index = jnp.asarray(hot_of((np.arange(512) + 128) % 512 - 256))
    table_grad = jnp.einsum("hu,ub->bh", strips[:, :512], near_index, precision=lax.Precision.HIGHEST)
    left, right = jnp.sum(strips[:, 512:640], axis=1), jnp.sum(strips[:, 640:], axis=1)
    bucket = jnp.arange(32, dtype=jnp.int32)[:, None]
    table_grad = table_grad + jnp.where(bucket == 15, left[None, :], 0.0) + jnp.where(bucket == 31, right[None, :], 0.0)
    slot = stats[:, 3].astype(jnp.int32)
    table = (slot[:, None] == jnp.arange(slots, dtype=jnp.int32)[None, :]).astype(bf16)
    output = (after_attn + stats[:, 2:3] * mm(table, returned.reshape(slots, width))).astype(bf16)
    return (
        output,
        input_grad,
        gain_one,
        grad_query,
        grad_key,
        grad_value,
        grad_output,
        table_grad,
        gain_two,
        grad_router,
        grad_in[None].astype(f32),
        grad_out[None].astype(f32),
    )


def solution(mesh):
    split, whole = P(("dp", "expert"), None), P()
    in_specs = (split, split, split, whole, whole, whole, whole, whole, whole, whole, whole, P("expert", None, None), P("expert", None, None))
    out_specs = (split, split) + (whole,) * 8 + (P("expert", None, "dp"), P("expert", "dp", None))
    return jax.shard_map(
        functools.partial(local, mesh.shape["dp"]), mesh=mesh, in_specs=in_specs, out_specs=out_specs, check_vma=False
    )
```

```python
import functools

import jax
import jax.numpy as jnp
import numpy as np
from jax import lax
from jax.experimental import pallas as pl
from jax.experimental.pallas import tpu as pltpu
from jax.sharding import PartitionSpec as P

NT = (((1,), (1,)), ((), ()))
NN = (((1,), (0,)), ((), ()))
TN = (((0,), (0,)), ((), ()))


def mm(a, b, dims=NN):
    return lax.dot_general(a, b, dims, preferred_element_type=jnp.float32)


MESH = pl.DeviceIdType.MESH
gelu_a, gelu_b = 0.7978845608, 0.044715


def greet(axis_size):
    me, dp = lax.axis_index("expert"), lax.axis_index("dp")
    barrier = pltpu.get_barrier_semaphore()
    for step in range(1, axis_size):
        pl.semaphore_signal(barrier, inc=1, device_id=(dp, me ^ step), device_id_type=MESH)
    pl.semaphore_signal(barrier, inc=1, device_id=(1 - dp, me), device_id_type=MESH)
    return dp, me


def greeted(axis_size):
    pl.semaphore_wait(pltpu.get_barrier_semaphore(), axis_size)


def expert_kernel(
    groups, tile, early,
    xs_ref, gs_ref, cot_ref, far_ref, win_ref, wout_ref,
    back_ref, gg_ref, ret_ref, gin_ref, gout_ref,
    x_scr, c_scr, g_scr, w1, w2, a_scr, p_scr, ag_scr, pg_scr, r_scr, b_scr, e_scr, sq_scr, gin, gout,
    x_send, x_recv, g_send, g_recv, b_send, b_recv, e_send, e_recv, loc, wsem, csem, rsem, osem, f_send, f_recv,
):
    f32, bf16 = jnp.float32, jnp.bfloat16
    n, cap, width = xs_ref.shape
    ff = win_ref.shape[1]
    half = ff // 2
    size = n // groups
    rows = size * cap
    dp, me = greet(n)
    mine = pl.multiple_of(dp * half, 128)
    rest = pl.multiple_of((1 - dp) * half, 128)
    weights = [
        pltpu.make_async_copy(win_ref.at[:, pl.ds(mine, half)], w1.at[:, :half], wsem.at[0]),
        pltpu.make_async_copy(win_ref.at[:, pl.ds(rest, half)], w1.at[:, half:], wsem.at[1]),
        pltpu.make_async_copy(wout_ref.at[pl.ds(mine, half), :], w2.at[:half, :], wsem.at[2]),
        pltpu.make_async_copy(wout_ref.at[pl.ds(rest, half), :], w2.at[half:, :], wsem.at[3]),
    ]
    own = [
        pltpu.make_async_copy(xs_ref.at[0], x_scr.at[0, 0], loc.at[0]),
        pltpu.make_async_copy(gs_ref.at[0], g_scr.at[0, 0], loc.at[1]),
    ]
    cots = [
        pltpu.make_async_copy(cot_ref, c_scr.at[0], csem.at[0]),
        pltpu.make_async_copy(far_ref.at[:early], c_scr.at[1, :early], csem.at[1]),
    ]

    def remote(src, dst, send, recv, dev):
        return pltpu.make_async_remote_copy(src, dst, send, recv, device_id=dev, device_id_type=MESH)

    def x_copy(o):
        return remote(xs_ref.at[o], x_scr.at[0, o], x_send.at[o], x_recv.at[o], (dp, me ^ o))

    def g_copy(o):
        return remote(gs_ref.at[o], g_scr.at[0, o], g_send.at[o], g_recv.at[o], (dp, me ^ o))

    def b_copy(o):
        return remote(b_scr.at[o], back_ref.at[me], b_send.at[o], b_recv.at[o], (dp, me ^ o))

    def e_copy(o):
        return remote(e_scr.at[o], gg_ref.at[me], e_send.at[o], e_recv.at[o], (dp, me ^ o))

    def r_copy(o):
        return pltpu.make_async_copy(r_scr.at[o], ret_ref.at[o], rsem.at[o])

    over = (1 - dp, me)
    c_over = remote(cot_ref.at[early:], c_scr.at[1, early:], f_send.at[groups], f_recv.at[groups], over)
    g_over = remote(g_scr.at[0], g_scr.at[1], f_send.at[groups + 1], f_recv.at[groups + 1], over)

    def x_over(g):
        span = slice(g * size, (g + 1) * size)
        return remote(x_scr.at[0, span], x_scr.at[1, span], f_send.at[g], f_recv.at[g], over)

    def each(lo, hi, fn):
        if hi - lo <= 4:
            for o in range(lo, hi):
                fn(o)
        else:
            lax.fori_loop(lo, hi, lambda o, c: (fn(o), c)[1], 0)

    for c in own + cots + weights:
        c.start()
    greeted(n)
    each(1, n, lambda o: g_copy(o).start())
    each(1, n, lambda o: x_copy(o).start())
    c_over.start()
    sq_scr[...] = jnp.zeros_like(sq_scr)

    def gated(side, lo, hi):
        def one(o):
            col = jnp.broadcast_to(g_scr[side, o][:1, :], (128, 128)).T[:cap, :1]
            c_scr[side, o] = (c_scr[side, o].astype(f32) * col).astype(bf16)

        each(lo, hi, one)

    def hidden(x, ct, f):
        u = mm(x, w1[:, f:f + tile])
        back = mm(ct, w2[f:f + tile, :], NT)
        uu = u * u
        t = jnp.tanh(u * (gelu_a + (gelu_a * gelu_b) * uu))
        hp = 0.5 + 0.5 * t
        act = u * hp
        slope = hp + act * ((1.0 - t) * (gelu_a + (3.0 * gelu_a * gelu_b) * uu))
        return act.astype(bf16), (back * slope).astype(bf16)

    for g in range(groups):
        lo, hi = g * size, (g + 1) * size
        if g == 0:
            for c in own + cots[:1]:
                c.wait()
        each(max(lo, 1), hi, lambda o: g_copy(o).wait_recv())
        raw = c_scr[0, lo:hi].reshape(rows, width)
        gated(0, lo, hi)
        each(max(lo, 1), hi, lambda o: x_copy(o).wait_recv())
        x_over(g).start()
        if g == 0:
            for c in weights:
                c.wait()
        x = x_scr[0, lo:hi].reshape(rows, width)
        ct = c_scr[0, lo:hi].reshape(rows, width)
        span = slice(g * rows, (g + 1) * rows)
        for f in range(0, ff, tile):
            act, pre = hidden(x, ct, f)
            if f < half:
                a_scr[span, f:f + tile] = act
                p_scr[span, f:f + tile] = pre
            else:
                ag_scr[:, f - half:f - half + tile] = act
                pg_scr[:, f - half:f - half + tile] = pre
        back = mm(p_scr[span, :], w1[:, :half], NT) + mm(pg_scr[...], w1[:, half:], NT)
        b_scr[lo:hi] = back.astype(bf16).reshape(size, cap, width)
        each(max(lo, 1), hi, lambda o: b_copy(o).start())
        r = mm(a_scr[span, :], w2[:half, :]) + mm(ag_scr[...], w2[half:, :])
        r_scr[lo:hi] = r.astype(bf16).reshape(size, cap, width)
        dots = r * raw.astype(f32)
        part = dots[:, :128]
        for j in range(1, width // 128):
            part = part + dots[:, j * 128:(j + 1) * 128]
        part = part.reshape(size, cap, 128)
        for o in range(lo, hi):
            sq_scr[:cap, :] = part[o - lo]
            line = jnp.sum(sq_scr[...].T, axis=0, keepdims=True)
            e_scr[o] = jnp.broadcast_to(line, (8, 128))
        each(max(lo, 1), hi, lambda o: e_copy(o).start())
    g_over.start()
    each(0, n, lambda o: r_copy(o).start())
    own_back = [
        pltpu.make_async_copy(b_scr.at[0], back_ref.at[me], loc.at[0]),
        pltpu.make_async_copy(e_scr.at[0], gg_ref.at[me], loc.at[1]),
    ]
    for c in own_back:
        c.start()
    total = n * cap

    def gradients(side, first):
        x = x_scr[side].reshape(total, width)
        ct = c_scr[side].reshape(total, width)
        for f in range(0, half, tile):
            part = lax.dot_general(x, p_scr[:, f:f + tile], TN, preferred_element_type=f32)
            if first:
                gin[:, f:f + tile] = part
            else:
                w1[:, f:f + tile] = (gin[:, f:f + tile] + part).astype(bf16)
            part = lax.dot_general(a_scr[:, f:f + tile], ct, TN, preferred_element_type=f32)
            if first:
                gout[f:f + tile, :] = part
            else:
                w2[f:f + tile, :] = (gout[f:f + tile, :] + part).astype(bf16)
                for c in outs(f):
                    c.start()

    def outs(f):
        i = f // tile
        return [
            pltpu.make_async_copy(w1.at[:, f:f + tile], gin_ref.at[:, f:f + tile], osem.at[2 * i]),
            pltpu.make_async_copy(w2.at[f:f + tile, :], gout_ref.at[f:f + tile, :], osem.at[2 * i + 1]),
        ]

    gradients(0, True)
    cots[1].wait()
    c_over.wait()
    g_over.wait()
    gated(1, 0, n)
    for g in range(groups):
        lo, hi = g * size, (g + 1) * size
        x_over(g).wait()
        x = x_scr[1, lo:hi].reshape(rows, width)
        ct = c_scr[1, lo:hi].reshape(rows, width)
        for f in range(0, half, tile):
            act, pre = hidden(x, ct, f)
            a_scr[g * rows:(g + 1) * rows, f:f + tile] = act
            p_scr[g * rows:(g + 1) * rows, f:f + tile] = pre
    gradients(1, False)
    for f in range(0, half, tile):
        for c in outs(f):
            c.wait()
    for c in own_back:
        c.wait()
    each(0, n, lambda o: r_copy(o).wait())
    each(1, n, lambda o: x_copy(o).wait_send())
    each(1, n, lambda o: g_copy(o).wait_send())
    each(1, n, lambda o: b_copy(o).wait())
    each(1, n, lambda o: e_copy(o).wait())


def expert_pass(xs, gs, cot, far, w_in, w_out):
    f32, bf16 = jnp.float32, jnp.bfloat16
    n, cap, width = xs.shape
    ff = w_in.shape[1]
    half = ff // 2
    groups, tile = (4, 512) if n * cap <= 1280 else (8, 256)
    rows = n // groups * cap
    hbm = pl.BlockSpec(memory_space=pl.ANY)
    dma = pltpu.SemaphoreType.DMA
    flat = jax.ShapeDtypeStruct((n, cap, width), bf16)
    return pl.pallas_call(
        functools.partial(expert_kernel, groups, tile, n // 2),
        in_specs=[hbm] * 6,
        out_specs=[hbm] * 5,
        out_shape=[
            flat, jax.ShapeDtypeStruct((n, 8, 128), f32), flat,
            jax.ShapeDtypeStruct((width, half), bf16), jax.ShapeDtypeStruct((half, width), bf16),
        ],
        scratch_shapes=[
            pltpu.VMEM((2, n, cap, width), bf16), pltpu.VMEM((2, n, cap, width), bf16), pltpu.VMEM((2, n, 8, 128), f32),
            pltpu.VMEM((width, ff), bf16), pltpu.VMEM((ff, width), bf16),
            pltpu.VMEM((n * cap, half), bf16), pltpu.VMEM((n * cap, half), bf16),
            pltpu.VMEM((rows, half), bf16), pltpu.VMEM((rows, half), bf16),
            pltpu.VMEM((n, cap, width), bf16), pltpu.VMEM((n, cap, width), bf16), pltpu.VMEM((n, 8, 128), f32),
            pltpu.VMEM((128, 128), f32), pltpu.VMEM((width, half), f32), pltpu.VMEM((half, width), f32),
        ] + [dma((n,))] * 8 + [dma((2,)), dma((4,)), dma((2,)), dma((n,)), dma((2 * half // tile,)), dma((groups + 2,)), dma((groups + 2,))],
        compiler_params=pltpu.CompilerParams(collective_id=1, has_side_effects=True, vmem_limit_bytes=62 << 20),
        name="experts",
    )(xs, gs, cot, far, w_in, w_out)

eps_norm = 1e-06
thresholds = (12, 16, 23, 32, 46, 64, 91)


def fwd_kernel(
    rows, limit, tok_ref, cot_ref, ids_ref, bias_ref, gains_ref, wq_ref, wk_ref, wv_ref, wo_ref, wr_ref,
    q_ref, k_ref, v_ref, o_ref, p_ref, aa_ref, probs_ref, stat_ref, xs_ref, gs_ref, cr_ref, cp_ref,
    b_scr, xn_scr, cs_scr, t_scr, rt_scr, gm_scr, sq_scr, vx_scr, g_scr, row_scr, hot_scr, send, recv, loc, f_send, f_recv,
):
    f32, bf16 = jnp.float32, jnp.bfloat16
    seq, width = tok_ref.shape
    blocks = seq // 128
    step = pl.program_id(0)
    n, cap = cs_scr.shape[:2]
    me, dp = lax.axis_index("expert"), lax.axis_index("dp")
    quarter = n // 4
    g1, g2 = gains_ref[0:1, :].astype(f32), gains_ref[1:2, :].astype(f32)

    def remote(src, dst, ss, rs, dev):
        return pltpu.make_async_remote_copy(src, dst, ss, rs, device_id=dev, device_id_type=MESH)

    def c_copy(o):
        return remote(cs_scr.at[o], cr_ref.at[o], send.at[o], recv.at[o], (dp, me ^ o))

    def over(i):
        part = pl.ds(i * quarter, quarter)
        return remote(cr_ref.at[part], cp_ref.at[part], f_send.at[i], f_recv.at[i], (1 - dp, me))

    home = pltpu.make_async_copy(cs_scr.at[0], cr_ref.at[0], loc.at[0])

    span = quarter * cap

    def choose(o, _):
        ids = lax.broadcasted_iota(jnp.int32, (cap, seq), 0) + (me ^ o) * cap
        t_scr[pl.ds(pl.multiple_of(o * cap, 16), cap), :] = (ids == row_scr[0:1, :]).astype(f32).astype(bf16)
        return 0

    @pl.when(step == 0)
    def _():
        greet(n)
        spread = jnp.broadcast_to(ids_ref[...].astype(f32), (128, seq)).T
        choice = lax.broadcasted_iota(jnp.int32, (seq, n), 1)
        routes = spread[:, :1].astype(jnp.int32)
        hot_scr[...] = (routes == choice).astype(f32).astype(bf16)
        for i in range(0, seq, rows):
            here = slice(i, i + rows)
            later = lax.broadcasted_iota(jnp.int32, (rows, seq), 0) + i
            before = (later > lax.broadcasted_iota(jnp.int32, (rows, seq), 1)).astype(f32).astype(bf16)
            position = jnp.sum(mm(before, hot_scr[...]) * hot_scr[here, :].astype(f32), axis=-1, keepdims=True)
            ids = spread[here, :1]
            slot = jnp.where(position < limit, ids * cap + position, -1.0)
            row_scr[:, here] = jnp.broadcast_to(slot, (rows, 128)).T[:8, :].astype(jnp.int32)
            slim = lax.broadcasted_iota(jnp.int32, (rows, 8), 1)
            stat_ref[here, :] = jnp.where(slim == 3, slot, ids)
        greeted(n)
        for g in range(4):
            lo = g * quarter
            lax.fori_loop(lo, lo + quarter, choose, 0)
            cs_scr[lo:lo + quarter] = mm(t_scr[g * span:(g + 1) * span, :], cot_ref[...]).astype(bf16).reshape(quarter, cap, width)
            if g == 0:
                home.start()
            for o in range(max(lo, 1), lo + quarter):
                c_copy(o).start()
        for i in range(0, seq, rows):
            here = slice(i, i + rows)
            x = tok_ref[here, :].astype(f32)
            s1 = lax.rsqrt(jnp.mean(x * x, axis=-1, keepdims=True) + eps_norm)
            slim = lax.broadcasted_iota(jnp.int32, (rows, 8), 1)
            stat_ref[here, :] = jnp.where(slim == 0, s1, stat_ref[here, :])
            xn_scr[here, :] = (x * s1 * g1).astype(bf16)
            aa_ref[here, :] = x
        offset = lax.broadcasted_iota(jnp.int32, (32, 512), 1) - 256
        distance = jnp.abs(offset)
        far = jnp.full(offset.shape, 8, jnp.int32)
        for t in thresholds:
            far = far + (distance >= t).astype(jnp.int32)
        bucket = jnp.where(distance < 8, distance, far) + 16 * (offset > 0).astype(jnp.int32)
        pick = (bucket == lax.broadcasted_iota(jnp.int32, (32, 512), 0)).astype(f32).astype(bf16)
        g_scr[...] = mm(bias_ref[...], pick)
        vx_scr[:, 128:] = jnp.ones((seq, 128), bf16)

    for i in range(2):

        @pl.when(step == 2 + 2 * i)
        def _():
            if i == 0:
                home.wait()
            for o in range(max(1, i * quarter), (i + 1) * quarter):
                c_copy(o).wait_recv()
            over(i).start()

    joined = jnp.concatenate([wq_ref[...], wk_ref[...], wv_ref[...]], axis=1)
    for i in range(0, seq, rows):
        here = slice(i, i + rows)
        qkv = mm(xn_scr[here, :], joined).astype(bf16)
        q_ref[here, :], k_ref[here, :], v_ref[here, :] = qkv[:, :128], qkv[:, 128:256], qkv[:, 256:]
    vx_scr[:, :128] = v_ref[...]
    lane = lax.broadcasted_iota(jnp.int32, (rows, 128), 1)
    for hh in range(2):
        own = (lane >= 64) if hh else (lane < 64)
        g = g_scr[pl.ds(2 * step + hh, 1), :]
        near = pltpu.roll(jnp.broadcast_to(g, (128, 512)), 384, axis=1, stride=1, stride_axis=0)
        mid = (blocks - 2) * 128
        b_scr[:, :mid] = jnp.broadcast_to(g[:, :1], (128, mid))
        b_scr[:, mid:mid + 384] = near[:, :384]
        b_scr[:, mid + 384:] = jnp.broadcast_to(g[:, 511:], (128, b_scr.shape[1] - mid - 384))
        for i in range(seq // rows):
            r0 = i * rows
            q = q_ref[r0:r0 + rows, :]
            qm = jnp.where(own, q * jnp.bfloat16(0.125), jnp.bfloat16(0))
            s = mm(qm, k_ref[...], NT)
            parts = []
            for a in range(rows // 128):
                c0 = (blocks - 1 - (r0 // 128 + a)) * 128
                parts.append(s[a * 128:(a + 1) * 128] + b_scr[:, c0:c0 + seq])
            s = jnp.concatenate(parts, 0) if len(parts) > 1 else parts[0]
            m = jnp.max(s, axis=-1, keepdims=True)
            e = jnp.exp(s - m)
            raw = mm(e.astype(bf16), vx_scr[...])
            inv = 1.0 / raw[:, 128:129]
            p_ref[hh, r0:r0 + rows, :] = (e * inv).astype(bf16)
            o = (raw[:, :128] * inv).astype(bf16)
            if hh == 0:
                o_ref[r0:r0 + rows, :] = o
            else:
                o = jnp.where(own, o, o_ref[r0:r0 + rows, :])
                o_ref[r0:r0 + rows, :] = o
                aa_ref[r0:r0 + rows, :] += mm(o, wo_ref[...])

    @pl.when(step == pl.num_programs(0) - 1)
    def _():
        slim = lax.broadcasted_iota(jnp.int32, (rows, 8), 1)
        wide = lax.broadcasted_iota(jnp.int32, (rows, 128), 1)
        for i in range(0, seq, rows):
            here = slice(i, i + rows)
            aa = aa_ref[here, :]
            s2 = lax.rsqrt(jnp.mean(aa * aa, axis=-1, keepdims=True) + eps_norm)
            routed = (aa * s2 * g2).astype(bf16)
            rt_scr[here, :] = routed
            logits = mm(routed, wr_ref[...], NT)
            e = jnp.exp(logits - jnp.max(logits, axis=-1, keepdims=True))
            probs = e / jnp.sum(e, axis=-1, keepdims=True)
            probs_ref[here, :] = probs
            gate = jnp.sum(probs * hot_scr[here, :].astype(f32), axis=-1, keepdims=True)
            stat_ref[here, :] = jnp.where(slim == 1, s2, jnp.where(slim == 2, gate, stat_ref[here, :]))
            high = gate.astype(bf16).astype(f32)
            middle = (gate - high).astype(bf16).astype(f32)
            low = gate - high - middle
            gm_scr[here, :] = jnp.where(wide == 0, high, jnp.where(wide == 1, middle, jnp.where(wide == 2, low, 0.0))).astype(bf16)
        sq_scr[...] = jnp.zeros_like(sq_scr)
        for g in range(4):
            lo = g * quarter
            here = slice(g * span, (g + 1) * span)
            xs_ref[lo:lo + quarter] = mm(t_scr[here, :], rt_scr[...]).astype(bf16).reshape(quarter, cap, width)
            gates = mm(t_scr[here, :], gm_scr[...]).reshape(quarter, cap, 128)
            for x in range(quarter):
                sq_scr[:cap, :] = gates[x]
                gs_ref[lo + x] = jnp.broadcast_to(jnp.sum(sq_scr[...].T, axis=0, keepdims=True), (8, 128))
        for o in range(1, n):
            c_copy(o).wait_send()
        for o in range(n // 2, n):
            c_copy(o).wait_recv()
        for i in range(2):
            over(i).wait()


def attn_fwd(tokens, cotangent, ids, bias, gains, wq, wk, wv, wo, wr, limit, cap, rows=256):
    f32, bf16 = jnp.float32, jnp.bfloat16
    seq, width = tokens.shape
    pairs = width // 128
    n = wr.shape[0]
    col = pl.BlockSpec((seq, 128), lambda h: (0, h))
    wcol = pl.BlockSpec((width, 128), lambda h: (0, h))

    def whole(shape):
        return pl.BlockSpec(shape, lambda h: (0,) * len(shape), pipeline_mode=pl.Buffered(1))

    hbm = pl.BlockSpec(memory_space=pl.ANY)
    dma = pltpu.SemaphoreType.DMA
    tall = jax.ShapeDtypeStruct((seq, width), bf16)
    fixed = [
        jax.ShapeDtypeStruct((seq, width), f32), jax.ShapeDtypeStruct((seq, n), f32), jax.ShapeDtypeStruct((seq, 8), f32),
        jax.ShapeDtypeStruct((n, cap, width), bf16), jax.ShapeDtypeStruct((n, 8, 128), f32),
    ]
    return pl.pallas_call(
        functools.partial(fwd_kernel, rows, limit),
        grid=(pairs,),
        in_specs=[whole(x.shape) for x in (tokens, cotangent, ids, bias, gains)]
        + [wcol] * 3 + [pl.BlockSpec((128, width), lambda h: (h, 0)), whole(wr.shape)],
        out_specs=[col] * 4 + [pl.BlockSpec((2, seq, seq), lambda h: (h, 0, 0))] + [whole(x.shape) for x in fixed] + [hbm, hbm],
        out_shape=[tall] * 4 + [jax.ShapeDtypeStruct((2 * pairs, seq, seq), bf16)] + fixed
        + [jax.ShapeDtypeStruct((n, cap, width), bf16), jax.ShapeDtypeStruct((n // 2, cap, width), bf16)],
        scratch_shapes=[
            pltpu.VMEM((128, 2 * seq - 128), f32), pltpu.VMEM((seq, width), bf16), pltpu.VMEM((n, cap, width), bf16),
            pltpu.VMEM((n * cap, seq), bf16), pltpu.VMEM((seq, width), bf16), pltpu.VMEM((seq, 128), bf16), pltpu.VMEM((128, 128), f32),
            pltpu.VMEM((seq, 256), bf16), pltpu.VMEM((bias.shape[0], 512), f32), pltpu.VMEM((8, seq), jnp.int32), pltpu.VMEM((seq, n), bf16),
            dma((n,)), dma((n,)), dma((1,)), dma((2,)), dma((2,)),
        ],
        compiler_params=pltpu.CompilerParams(
            dimension_semantics=("arbitrary",), collective_id=3, has_side_effects=True, vmem_limit_bytes=56 << 20
        ),
        name="attn_fwd",
    )(tokens, cotangent, ids, bias, gains, wq, wk, wv, wo, wr)


def bwd_kernel(
    rows, merge, q_ref, k_ref, v_ref, o_ref, p_ref, wq_ref, wk_ref, wv_ref,
    tok_ref, cot_ref, after_ref, stat_ref, probs_ref, gains_ref, wr_ref, wo_ref, back_ref, gg_ref, rs_ref,
    ig_ref, small_out, sum_ref, rr_ref,
    ds_scr, qt_scr, dt_scr, near_scr, far_scr, xt_scr, d_scr, br_scr, dz_scr, nf_scr, ng_scr, rt_scr, gc_scr,
    acc, inbox, done, s_acc, s_inbox, s_done, send, recv, loc, r_send, r_recv, s_send, s_recv, out_sem,
):
    seq = q_ref.shape[0]
    blocks = seq // 128
    step = pl.program_id(0)
    width = tok_ref.shape[1]
    pairs = width // 128
    f32, bf16 = jnp.float32, jnp.bfloat16
    g1, g2 = gains_ref[0:1, :].astype(f32), gains_ref[1:2, :].astype(f32)
    chunks, total, depth, _ = acc.shape
    n = total // 2
    me, dp = lax.axis_index("expert"), lax.axis_index("dp")
    rounds = rounds_of(n)
    count = len(rounds)

    def place(bits):
        rank, devices = 0, []
        for i, bit in enumerate(bits):
            rank = rank + (dp if bit < 0 else (me >> bit) & 1) * (1 << i)
        for mask in range(1, 1 << len(bits)):
            flip = sum(1 << bit for i, bit in enumerate(bits) if bit >= 0 and mask >> i & 1)
            across = any(bit < 0 and mask >> i & 1 for i, bit in enumerate(bits))
            devices.append((1 - dp if across else dp, me ^ flip))
        return rank, devices

    ranks, spans, at, base, size, lead = [place(bits) for bits in rounds], [], 0, 0, total, 0
    for r, bits in enumerate(rounds):
        size //= 1 << len(bits)
        spans.append((at, at + ranks[r][0] * size, size, base, lead))
        at, base, lead = at + ranks[r][0] * size, base + ((1 << len(bits)) - 1) * size, lead + (1 << len(bits)) - 1
    links = lead

    def spread(lane, r):
        mine, box, _, ss, rs, _ = lane
        start, _, size, base, lead = spans[r]
        rank, devices = ranks[r]
        return [
            pltpu.make_async_remote_copy(
                mine.at[pl.ds(start + (rank ^ m) * size, size)], box.at[base + (m - 1) * size:base + m * size],
                ss.at[lead + m - 1], rs.at[lead + m - 1], device_id=devices[m - 1], device_id_type=MESH,
            )
            for m in range(1, len(devices) + 1)
        ]

    def fold(lane, r):
        mine, box, out, _, _, kind = lane
        _, keep, size, base, _ = spans[r]
        here = pl.ds(keep, size)
        part = mine[here].astype(jnp.float32)
        for m in range(len(ranks[r][1])):
            part = part + box[base + m * size:base + (m + 1) * size].astype(jnp.float32)
        (out if r == count - 1 else mine)[here] = part.astype(kind)

    def share(lane, r):
        _, _, out, ss, rs, _ = lane
        _, keep, size, _, lead = spans[r]
        piece = out.at[pl.ds(keep, size)]
        return [
            pltpu.make_async_remote_copy(
                piece, piece, ss.at[links + lead + m - 1], rs.at[links + lead + m - 1], device_id=dev, device_id_type=MESH
            )
            for m, dev in enumerate(ranks[r][1], 1)
        ]

    def event(lane, e):
        if 0 < e <= count:
            for c in spread(lane, e - 1):
                c.wait()
            fold(lane, e - 1)
        elif e > count:
            for c in share(lane, 2 * count - e):
                c.wait()
        if e < count:
            for c in spread(lane, e):
                c.start()
        elif e < 2 * count:
            for c in share(lane, 2 * count - 1 - e):
                c.start()

    last = 2 * count
    gaps = [3] + [6] * (count - 1)
    gaps = gaps + gaps[::-1]
    due = [sum(gaps[:e]) for e in range(last + 1)]

    def lane_of(c):
        return (acc.at[c], inbox.at[c], done.at[c], r_send.at[c], r_recv.at[c], jnp.bfloat16)

    tiny = (s_acc, s_inbox, s_done, s_send, s_recv, jnp.float32)

    def finish(c):
        return pltpu.make_async_copy(done.at[c], sum_ref.at[c], out_sem.at[c])

    def advance(slot):
        for e in range(last, 0, -1):
            if (slot - due[e] - 2) % 3:
                continue
            ready = step + (slot - due[e] - 2) // 3 + 1
            c = ready // merge - 1

            @pl.when((ready >= merge) & (ready % merge == 0))
            def _():
                event(lane_of(c), e)
                if e == last:
                    finish(c).start()

    def r_copy(o):
        return pltpu.make_async_remote_copy(
            rs_ref.at[o], rr_ref.at[me], send.at[o], recv.at[o], device_id=(dp, me ^ o), device_id_type=MESH
        )

    home = pltpu.make_async_copy(rs_ref.at[0], rr_ref.at[me], loc.at[0])
    experts, cap = rs_ref.shape[0], rs_ref.shape[1]

    @pl.when(step == 0)
    def _():
        others = [(dp, me ^ o) for o in range(1, n)]
        for bits, (_, devices) in zip(rounds, ranks):
            if -1 in bits:
                others += [dev for m, dev in enumerate(devices, 1) if m >> bits.index(-1) & 1]
        barrier = pltpu.get_barrier_semaphore()
        for dev in others:
            pl.semaphore_signal(barrier, inc=1, device_id=dev, device_id_type=MESH)
        s_acc[...] = jnp.zeros_like(s_acc)
        rt_scr[...] = jnp.zeros_like(rt_scr)
        column = lax.broadcasted_iota(jnp.int32, (cap, 128), 1)

        def split(x, _):
            col = jnp.broadcast_to(gg_ref[x][:1, :], (128, 128)).T[:cap, :1]
            high = col.astype(bf16).astype(f32)
            mid = (col - high).astype(bf16).astype(f32)
            low = col - high - mid
            gc_scr[x] = jnp.where(column == 0, high, jnp.where(column == 1, mid, jnp.where(column == 2, low, 0.0))).astype(bf16)
            return 0

        lax.fori_loop(0, experts, split, 0)
        slots = experts * cap
        back = back_ref[...].reshape(slots, width)
        marks = gc_scr[...].reshape(slots, 128)
        where = lax.broadcasted_iota(jnp.int32, (rows, slots), 1)
        choice = lax.broadcasted_iota(jnp.int32, (rows, probs_ref.shape[1]), 1)
        for i in range(0, seq, rows):
            if i == seq // 4:
                pl.semaphore_wait(barrier, len(others))
                home.start()
                for o in range(1, n):
                    r_copy(o).start()
            here = slice(i, i + rows)
            s1, s2, gate = stat_ref[here, 0:1], stat_ref[here, 1:2], stat_ref[here, 2:3]
            table = (stat_ref[here, 3:4].astype(jnp.int32) == where).astype(f32).astype(bf16)
            hot = (stat_ref[here, 4:5].astype(jnp.int32) == choice).astype(f32)
            triple = mm(table, marks)
            gate_grad = triple[:, 0:1] + triple[:, 1:2] + triple[:, 2:3]
            lg = ((gate_grad * gate) * (hot - probs_ref[here, :])).astype(bf16)
            rg = mm(table, back) + mm(lg, wr_ref[...])
            gdy = g2 * rg
            scaled = after_ref[here, :] * s2
            mean = jnp.sum(gdy * scaled, axis=-1, keepdims=True) * (1.0 / width)
            after = cot_ref[here, :].astype(f32) + s2 * (gdy - scaled * mean)
            routed = (scaled * g2).astype(bf16)
            rt_scr[1:, :] += lax.dot_general(lg, routed, TN, preferred_element_type=f32)
            rt_scr[:1, :] += jnp.sum(rg * scaled, axis=0, keepdims=True)
            ig_ref[here, :] = after
            low = after.astype(bf16)
            br_scr[here, :] = low
            d_scr[here, :] = mm(low, wo_ref[...], NT).astype(bf16)
            xt_scr[:, here] = (tok_ref[here, :].astype(f32) * s1 * g1).astype(bf16).T

    cols = pl.ds(pl.multiple_of(step * 128, 128), 128)
    lane = lax.broadcasted_iota(jnp.int32, (rows, 128), 1)
    sub = lax.broadcasted_iota(jnp.int32, (128, seq), 0)
    qt = q_ref[...].T
    dt = d_scr[:, cols].T
    zero = jnp.bfloat16(0)
    for hh in range(2):
        half = (sub >= 64) if hh else (sub < 64)
        qt_scr[:, hh * seq:(hh + 1) * seq] = jnp.where(half, qt, zero)
        dt_scr[:, hh * seq:(hh + 1) * seq] = jnp.where(half, dt, zero)
    for hh in range(2):
        own = (lane >= 64) if hh else (lane < 64)
        near_scr[...] = jnp.zeros_like(near_scr)
        far_scr[...] = jnp.zeros_like(far_scr)
        for i in range(seq // rows):
            r0 = i * rows
            d = jnp.where(own, d_scr[r0:r0 + rows, cols], zero)
            grown = mm(d, v_ref[...], NT)
            delta = jnp.sum(d.astype(jnp.float32) * o_ref[r0:r0 + rows, :].astype(jnp.float32), axis=-1, keepdims=True)
            ds = p_ref[hh, r0:r0 + rows, :].astype(jnp.float32) * (grown - delta)
            low = ds.astype(jnp.bfloat16)
            ds_scr[r0:r0 + rows, :] = low
            for a in range(rows // 128):
                bi = r0 // 128 + a
                strip = ds[a * 128:(a + 1) * 128]
                lo, hi = max(bi - 1, 0), min(bi + 2, blocks)
                near_scr[:, (lo - bi + 1) * 128:(hi - bi + 1) * 128] += strip[:, lo * 128:hi * 128]
                if lo > 0:
                    t = strip[:, :128]
                    for j in range(1, lo):
                        t = t + strip[:, j * 128:(j + 1) * 128]
                    far_scr[:, :128] += t
                if hi < blocks:
                    t = strip[:, hi * 128:(hi + 1) * 128]
                    for j in range(hi + 1, blocks):
                        t = t + strip[:, j * 128:(j + 1) * 128]
                    far_scr[:, 128:] += t
            dq = (0.125 * mm(low, k_ref[...])).astype(jnp.bfloat16)
            if hh == 0:
                dz_scr[r0:r0 + rows, :128] = dq
            else:
                dz_scr[r0:r0 + rows, :128] = jnp.where(own, dq, dz_scr[r0:r0 + rows, :128])
        part = mm(qt_scr[:, hh * seq:(hh + 1) * seq], ds_scr[...])
        dkt = part if hh == 0 else dkt + part
        a = near_scr[...]
        w = 128
        while w > 1:
            w //= 2
            a = a[:w] + pltpu.roll(a[w:], 512 - w, axis=1)
        nf_scr[pl.ds(2 * step + hh, 1), :512] = a
        nf_scr[pl.ds(2 * step + hh, 1), 512:] = jnp.sum(far_scr[...], axis=0, keepdims=True)
        if hh == 0:
            advance(0)
    advance(1)
    dz_scr[:, 128:256] = (0.125 * dkt).astype(jnp.bfloat16).T
    dvt = mm(dt_scr[...], p_ref[...].reshape(2 * seq, seq))
    dz_scr[:, 256:] = dvt.astype(jnp.bfloat16).T
    dz = dz_scr[...]
    dw = mm(xt_scr[...], dz).astype(jnp.bfloat16)
    go = lax.dot_general(o_ref[...], br_scr[...], TN, preferred_element_type=f32).astype(bf16)
    tiles = [dw[:, j * 128:(j + 1) * 128] for j in range(3)]
    tiles.append(jnp.concatenate([go[:, j * 128:(j + 1) * 128] for j in range(pairs)], axis=0))
    mine = step // merge
    per = width // depth
    for turn in range(merge):

        @pl.when(step % merge == turn)
        def _():
            for j in range(4):
                at = (turn * 4 + j) * per
                acc[mine, at:at + per] = tiles[j].reshape(per, depth, 128)

    w = jnp.concatenate([wq_ref[...], wk_ref[...], wv_ref[...]], axis=1)
    ng = mm(dz, w, NT)

    @pl.when(step == 0)
    def _():
        ng_scr[...] = ng

    @pl.when(step > 0)
    def _():
        ng_scr[...] += ng

    advance(2)

    @pl.when((step + 1) % merge == 0)
    def _():
        event(lane_of(mine), 0)

    @pl.when(step == pairs - 1)
    def _():
        gain = jnp.zeros((1, width), f32)
        for i in range(0, seq, rows):
            here = slice(i, i + rows)
            scaled = tok_ref[here, :].astype(f32) * stat_ref[here, 0:1]
            gain = gain + jnp.sum(ng_scr[here, :] * scaled, axis=0, keepdims=True)
        pieces = [gain] + [nf_scr[h:h + 1, :] for h in range(2 * pairs)] + [rt_scr[h:h + 1, :] for h in range(rt_scr.shape[0])]
        for i, piece in enumerate(pieces):
            for j in range(6):
                r = i * 6 + j
                s_acc[r // 8, r % 8:r % 8 + 1, :] = piece[:, j * 128:(j + 1) * 128]
        event(tiny, 0)
        left = []
        for c in range(chunks):
            ready = 3 * (c * merge + merge - 1) + 2
            left.append([e for e in range(1, last + 1) if ready + due[e] > 3 * pairs - 1])
        for turn in range(1, last + 1):
            for c in reversed(range(chunks)):
                if left[c]:
                    e = left[c].pop(0)
                    event(lane_of(c), e)
                    if e == last:
                        finish(c).start()
            event(tiny, turn)
            if turn == 1:
                for i in range(0, seq, rows):
                    here = slice(i, i + rows)
                    s1 = stat_ref[here, 0:1]
                    scaled = tok_ref[here, :].astype(f32) * s1
                    gdy = g1 * ng_scr[here, :]
                    mean = jnp.sum(gdy * scaled, axis=-1, keepdims=True) * (1.0 / width)
                    ig_ref[here, :] += s1 * (gdy - scaled * mean)
        small_out[...] = s_done[...]
        for c in range(chunks):
            finish(c).wait()
        home.wait()
        for o in range(1, n):
            r_copy(o).wait()


def rounds_of(n):
    bits = n.bit_length() - 1
    if bits == 4:
        return [[0], [1, -1], [2, 3]]
    rest = list(range(1, bits)) + [-1]
    return [[0]] + [rest[i:i + 2] for i in range(0, len(rest), 2)]


def attn_bwd(q, k, v, o, p, wq, wk, wv, tokens, cotangent, after_attn, stats, probs, gains, wr, wo, back, gg, rs, rows=256):
    f32, bf16 = jnp.float32, jnp.bfloat16
    seq, width = q.shape
    pairs = width // 128
    n, cap = rs.shape[:2]
    total = 2 * n
    experts = probs.shape[1]
    links = sum((1 << len(bits)) - 1 for bits in rounds_of(n))
    merge = 1
    while 4 * width * merge % (total * 8):
        merge += 1
    chunks = pairs // merge
    depth = 4 * width * merge // total
    col = pl.BlockSpec((seq, 128), lambda h: (0, h))
    wcol = pl.BlockSpec((width, 128), lambda h: (0, h))

    def whole(shape):
        return pl.BlockSpec(shape, lambda h: (0,) * len(shape), pipeline_mode=pl.Buffered(1))

    hbm = pl.BlockSpec(memory_space=pl.ANY)
    dma = pltpu.SemaphoreType.DMA
    small = (total, 8, 128)
    store = pltpu.VMEM((chunks, total, depth, 128), bf16)
    small_store = pltpu.VMEM(small, f32)
    singles = (tokens, cotangent, after_attn, stats, probs, gains, wr, wo, back, gg)
    return pl.pallas_call(
        functools.partial(bwd_kernel, rows, merge),
        grid=(pairs,),
        in_specs=[col] * 4 + [pl.BlockSpec((2, seq, seq), lambda h: (h, 0, 0))] + [wcol] * 3 + [whole(x.shape) for x in singles] + [hbm],
        out_specs=[whole((seq, width)), whole(small), hbm, hbm],
        out_shape=[
            jax.ShapeDtypeStruct((seq, width), f32),
            jax.ShapeDtypeStruct(small, f32),
            jax.ShapeDtypeStruct((chunks, total, depth, 128), bf16),
            jax.ShapeDtypeStruct(rs.shape, rs.dtype),
        ],
        scratch_shapes=[
            pltpu.VMEM((seq, seq), bf16), pltpu.VMEM((128, 2 * seq), bf16), pltpu.VMEM((128, 2 * seq), bf16),
            pltpu.VMEM((128, 512), f32), pltpu.VMEM((128, 256), f32),
            pltpu.VMEM((width, seq), bf16), pltpu.VMEM((seq, width), bf16), pltpu.VMEM((seq, width), bf16), pltpu.VMEM((seq, 384), bf16),
            pltpu.VMEM((2 * pairs + 4, 768), f32), pltpu.VMEM((seq, width), f32), pltpu.VMEM((1 + experts, width), f32),
            pltpu.VMEM((n, cap, 128), bf16),
            store, store, store, small_store, small_store, small_store,
            dma((n,)), dma((n,)), dma((1,)),
            dma((chunks, 2 * links)), dma((chunks, 2 * links)), dma((2 * links,)), dma((2 * links,)), dma((chunks,)),
        ],
        compiler_params=pltpu.CompilerParams(
            dimension_semantics=("arbitrary",), collective_id=4, has_side_effects=True, vmem_limit_bytes=63 << 20
        ),
        name="attn_bwd",
    )(q, k, v, o, p, wq, wk, wv, *singles, rs)

def finish_kernel(sum_ref, q_ref, k_ref, v_ref, o_ref):
    for j, out in enumerate((q_ref, k_ref, v_ref)):
        out[...] = sum_ref[0, j].astype(jnp.float32)
    for i in range(sum_ref.shape[2] // 128):
        o_ref[:, i * 128:(i + 1) * 128] = sum_ref[0, 3, i * 128:(i + 1) * 128].astype(jnp.float32)


def finish_sums(sums):
    pairs, _, depth, _ = sums.shape
    col = pl.BlockSpec((depth, 128), lambda h: (0, h))
    return pl.pallas_call(
        finish_kernel,
        grid=(pairs,),
        in_specs=[pl.BlockSpec((1, 4, depth, 128), lambda h: (h, 0, 0, 0))],
        out_specs=[col] * 3 + [pl.BlockSpec((128, depth), lambda h: (h, 0))],
        out_shape=[jax.ShapeDtypeStruct((depth, 128 * pairs), jnp.float32)] * 4,
        compiler_params=pltpu.CompilerParams(dimension_semantics=("arbitrary",), vmem_limit_bytes=16 << 20),
        name="finish_sums",
    )(sums)


def bucket_of(offset):
    distance = np.abs(offset)
    far = 8 + sum((distance >= t).astype(np.int32) for t in thresholds)
    return np.where(distance < 8, distance, far) + 16 * (offset > 0)


def hot_of(offset):
    return (bucket_of(offset)[..., None] == np.arange(32)).astype(np.float32)


def local(dp_count, tokens, routes, cotangent, gain_first, w_query, w_key, w_value, w_output, bias_table, gain_second, w_router, expert_in, expert_out):
    f32, bf16 = jnp.float32, jnp.bfloat16
    seq, width = tokens.shape
    heads = bias_table.shape[1]
    experts = w_router.shape[1]
    cap = (5 * seq + 4 * experts - 1) // (4 * experts)
    capp = (cap + 15) // 16 * 16
    slots = experts * capp
    ids = routes[:, 0]
    first = lax.broadcasted_iota(jnp.int32, (2, width), 0) == 0
    gains = jnp.where(first, gain_first[None, :], gain_second[None, :])
    router = w_router.T
    q, k, v, attended, probs_low, after_attn, router_probs, stats, rows, gates, cot_rows, cot_far = attn_fwd(
        tokens, cotangent, ids[None, :], bias_table.T, gains, w_query, w_key, w_value, w_output, router, cap, capp
    )
    back_tokens, gate_grads, produced, grad_in, grad_out = expert_pass(rows, gates, cot_rows, cot_far, expert_in[0], expert_out[0])
    input_grad, small, sums, returned = attn_bwd(
        q, k, v, attended, probs_low, w_query, w_key, w_value, tokens, cotangent, after_attn, stats, router_probs,
        gains, router, w_output, back_tokens, gate_grads, produced,
    )
    grad_query, grad_key, grad_value, grad_output = finish_sums(sums.reshape(heads // 2, 4, width, 128))
    small = small.reshape(-1)[:(2 + heads + experts) * 768].reshape(-1, 768)
    gain_one, strips, gain_two, router_rows = small[0], small[1:1 + heads], small[1 + heads], small[2 + heads:]
    grad_router = router_rows.T
    near_index = jnp.asarray(hot_of((np.arange(512) + 128) % 512 - 256))
    table_grad = jnp.einsum("hu,ub->bh", strips[:, :512], near_index, precision=lax.Precision.HIGHEST)
    left, right = jnp.sum(strips[:, 512:640], axis=1), jnp.sum(strips[:, 640:], axis=1)
    bucket = jnp.arange(32, dtype=jnp.int32)[:, None]
    table_grad = table_grad + jnp.where(bucket == 15, left[None, :], 0.0) + jnp.where(bucket == 31, right[None, :], 0.0)
    slot = stats[:, 3].astype(jnp.int32)
    table = (slot[:, None] == jnp.arange(slots, dtype=jnp.int32)[None, :]).astype(bf16)
    output = (after_attn + stats[:, 2:3] * mm(table, returned.reshape(slots, width))).astype(bf16)
    return (
        output,
        input_grad,
        gain_one,
        grad_query,
        grad_key,
        grad_value,
        grad_output,
        table_grad,
        gain_two,
        grad_router,
        grad_in[None].astype(f32),
        grad_out[None].astype(f32),
    )


def solution(mesh):
    split, whole = P(("dp", "expert"), None), P()
    in_specs = (split, split, split, whole, whole, whole, whole, whole, whole, whole, whole, P("expert", None, None), P("expert", None, None))
    out_specs = (split, split) + (whole,) * 8 + (P("expert", None, "dp"), P("expert", "dp", None))
    return jax.shard_map(
        functools.partial(local, mesh.shape["dp"]), mesh=mesh, in_specs=in_specs, out_specs=out_specs, check_vma=False
    )
```
